32 devices in a mesh: row: 4 (over z), col: 8 (over y, x, core).
Axes of the slice: x: 2, y: 2, z: 4, core: 2. Of those that a mesh axis runs over, the one named last changes fastest.
Arguments:
- inverse_top: bfloat16 [1024, 1024], P('col', 'row'), may hold values from -0.1875 to 0.1875
- inverse_one: bfloat16 [1536, 768], P('col', 'row'), may hold values from -0.21875 to 0.21875
- inverse_two: bfloat16 [2048, 512], P('col', 'row'), may hold values from -0.25 to 0.25
- inverse_leaf: bfloat16 [2048, 256], P('col', 'row'), may hold values from -0.375 to 0.375
- coupling_one: bfloat16 [768, 1536], P('row', 'col'), may hold values from -0.21875 to 0.21875
- coupling_two: bfloat16 [512, 2048], P('row', 'col'), may hold values from -0.25 to 0.25
- coupling_leaf: bfloat16 [256, 2048], P('row', 'col'), may hold values from -0.375 to 0.375
- rhs_top: bfloat16 [1024, 256], P('row', 'col'), may hold values from -6 to 6
- rhs_one: bfloat16 [768, 512], P('row', 'col'), may hold values from -6 to 6
- rhs_two: bfloat16 [512, 1024], P('row', 'col'), may hold values from -6 to 6
- rhs_leaf: bfloat16 [256, 2048], P('row', 'col'), may hold values from -6 to 6
- parent_map_one: int32 [2, 768], replicated, may hold values from 0 to 1023, as said below
- parent_map_two: int32 [4, 512], replicated, may hold values from 0 to 1535, as said below
- parent_map_leaf: int32 [8, 256], replicated, may hold values from 0 to 1023, as said below
Outputs:
- solution_top: bfloat16 [1024, 256], P('row', 'col')
- solution_one: bfloat16 [768, 512], P('row', 'col')
- solution_two: bfloat16 [512, 1024], P('row', 'col')
- solution_leaf: bfloat16 [256, 2048], P('row', 'col')
The draws below stay inside these ranges and needn't reach their ends.
Inputs may be any that keep to these rules, and one draw needn't show every extreme that they name: `parent_map_one`: row k lists distinct rows of the top front, one for each of the 768 update rows of front k. Cut the update rows and the top separator each into 4 equal blocks: at most 96 rows of one block land in one block of the top front, a number that is reached in every row, and every block of the top front receives exactly 192 rows from each child. `parent_map_two`: row k lists distinct rows of the front k // 2 of the second level (its 768 separator rows first, then its 768 update rows), one for each of the 512 update rows of front k. Cut the update rows into 4 equal blocks, and the parent's separator rows and its update rows each into 4 equal blocks, block j of the parent being the j-th separator block with the j-th update block: at most 64 rows of one block land in one parent block, reached in every row, and every parent block receives exactly 128 rows from each child. `parent_map_leaf`: as for parent_map_two, one level lower: 256 update rows of front k into front k // 2 of the third level, at most 32 rows of one block into one parent block, reached in every row, and exactly 64 rows from each child into every parent block.
All inputs are finite; a program needn't handle non-finite values.
Results may differ from the reference program's by a relative error of at most 0.03.
Values may be sent and summed in bfloat16 or wider, within the bound.
A program may use at most 64 MiB of HBM per device.

```python
import jax
import jax.numpy as jnp
from jax import lax

COLUMNS = 256
STRIPS = 4
SEP_TOP = 1024
SEP_ONE = 768
SEP_TWO = 512
SEP_LEAF = 256


def level_map(key, fronts, upd_order, sep_parent, upd_parent):
    strips = STRIPS
    block_rows = upd_order // strips
    mean_load = upd_order // (strips * strips)
    block_len = (sep_parent + upd_parent) // strips
    sep_rows = sep_parent // strips
    upd_rows = max(upd_parent // strips, 1)

    def one_child(child_key):
        subkeys = jax.random.split(child_key, 4)
        pairing = jax.random.permutation(subkeys[0], strips)
        swings = jax.random.randint(subkeys[1], (strips // 2,), 0, mean_load + 1).astype(jnp.int32)
        swings = swings.at[0].set(mean_load)
        shifts = jnp.zeros((strips,), jnp.int32).at[pairing[0::2]].set(swings).at[pairing[1::2]].set(-swings)
        source = jnp.arange(strips, dtype=jnp.int32)[:, None]
        target = jnp.arange(strips, dtype=jnp.int32)[None, :]
        load_table = mean_load + shifts[(target - source) % strips]
        load_ends = jnp.cumsum(load_table, axis=1)
        local_at = jnp.arange(block_rows, dtype=jnp.int32)
        target_of = jnp.sum((load_ends[:, None, :] <= local_at[None, :, None]).astype(jnp.int32), axis=2)
        starts = load_ends - load_table
        slot_of = local_at[None, :] - jnp.take_along_axis(starts, target_of, axis=1)
        before = jnp.cumsum(load_table, axis=0) - load_table
        rank_of = jnp.take_along_axis(before, target_of, axis=1) + slot_of
        orders = jax.vmap(lambda subkey: jax.random.permutation(subkey, block_len))(jax.random.split(subkeys[2], strips))
        placed = orders[target_of, rank_of]
        values = jnp.where(placed < sep_rows, target_of * sep_rows + placed, sep_parent + target_of * upd_rows + placed - sep_rows)
        shuffles = jax.vmap(lambda subkey: jax.random.permutation(subkey, block_rows))(jax.random.split(subkeys[3], strips))
        result = jnp.zeros((strips, block_rows), jnp.int32).at[jnp.arange(strips)[:, None], shuffles].set(values.astype(jnp.int32))
        return result.reshape(upd_order).astype(jnp.int32)
    return jax.vmap(one_child)(jax.random.split(key, fronts))


def draw_parent_map_one(key, part):
    return level_map(jax.random.fold_in(key, 11), 2, SEP_ONE, SEP_TOP, 0)


def draw_parent_map_two(key, part):
    return level_map(jax.random.fold_in(key, 12), 4, SEP_TWO, SEP_ONE, SEP_ONE)


def draw_parent_map_leaf(key, part):
    return level_map(jax.random.fold_in(key, 13), 8, SEP_LEAF, SEP_TWO, SEP_TWO)


def block_scale(key, extent, cuts, low, largest):
    loudness, own = 1.0, jax.random.fold_in(key, 6)
    for position, parts in cuts:
        draws = jnp.exp(jax.random.uniform(jax.random.fold_in(own, position), (parts,), jnp.float32, low / len(cuts), largest / len(cuts)))
        loudness = loudness * jnp.repeat(draws, extent[position] // parts).reshape([-1 if axis == position else 1 for axis in range(len(extent))])
    return loudness


def gaussian(key, shape, scale, reach, cuts=(), kind=jnp.bfloat16):
    gain = block_scale(key, shape, cuts, -0.22, 0.18) if cuts else 1.0
    array = jax.random.normal(key, shape, jnp.float32) * scale * gain
    return jnp.minimum(jnp.maximum(array, -reach), reach).astype(kind)


def setup_inputs(seed: int = 0) -> dict:
    keys = jax.random.split(jax.random.key(seed), 15)
    return {
        "inverse_top": gaussian(keys[0], (SEP_TOP, SEP_TOP), SEP_TOP ** -0.5, 0.1875, ((0, 8), (1, 4))),
        "inverse_one": gaussian(keys[1], (2 * SEP_ONE, SEP_ONE), SEP_ONE ** -0.5, 0.21875, ((0, 8), (1, 4))),
        "inverse_two": gaussian(keys[2], (4 * SEP_TWO, SEP_TWO), SEP_TWO ** -0.5, 0.25, ((0, 8), (1, 4))),
        "inverse_leaf": gaussian(keys[3], (8 * SEP_LEAF, SEP_LEAF), SEP_LEAF ** -0.5, 0.375, ((0, 8), (1, 4))),
        "coupling_one": gaussian(keys[4], (SEP_ONE, 2 * SEP_ONE), SEP_ONE ** -0.5, 0.21875, ((0, 4), (1, 8))),
        "coupling_two": gaussian(keys[5], (SEP_TWO, 4 * SEP_TWO), SEP_TWO ** -0.5, 0.25, ((0, 4), (1, 8))),
        "coupling_leaf": gaussian(keys[6], (SEP_LEAF, 8 * SEP_LEAF), SEP_LEAF ** -0.5, 0.375, ((0, 4), (1, 8))),
        "rhs_top": gaussian(keys[7], (SEP_TOP, COLUMNS), 1.0, 6.0, ((0, 4), (1, 8))),
        "rhs_one": gaussian(keys[8], (SEP_ONE, 2 * COLUMNS), 1.0, 6.0, ((0, 4), (1, 8))),
        "rhs_two": gaussian(keys[9], (SEP_TWO, 4 * COLUMNS), 1.0, 6.0, ((0, 4), (1, 8))),
        "rhs_leaf": gaussian(keys[10], (SEP_LEAF, 8 * COLUMNS), 1.0, 6.0, ((0, 4), (1, 8))),
        "parent_map_one": draw_parent_map_one(jax.random.fold_in(keys[14], 71), 0),
        "parent_map_two": draw_parent_map_two(jax.random.fold_in(keys[14], 71), 0),
        "parent_map_leaf": draw_parent_map_leaf(jax.random.fold_in(keys[14], 71), 0),
    }


def pivot_product(inverse, vector):
    strip_width = inverse.shape[1] // STRIPS
    summed = jnp.zeros((inverse.shape[0], vector.shape[1]), jnp.float32)
    for strip_at in range(STRIPS):
        low_edge = strip_at * strip_width
        partial_value = jnp.dot(inverse[:, low_edge:low_edge + strip_width], vector[low_edge:low_edge + strip_width], preferred_element_type=jnp.float32)
        summed = summed + lax.optimization_barrier(partial_value.astype(jnp.bfloat16)).astype(jnp.float32)
    return summed


def coupling_back(coupling, gathered):
    strip_width = coupling.shape[0] // STRIPS
    summed = jnp.zeros((coupling.shape[1], gathered.shape[1]), jnp.float32)
    for strip_at in range(STRIPS):
        low_edge = strip_at * strip_width
        partial_value = jnp.dot(coupling[low_edge:low_edge + strip_width].T, gathered[low_edge:low_edge + strip_width], preferred_element_type=jnp.float32)
        summed = summed + lax.optimization_barrier(partial_value.astype(jnp.bfloat16)).astype(jnp.float32)
    return summed


def reference(inverse_top, inverse_one, inverse_two, inverse_leaf, coupling_one, coupling_two, coupling_leaf, rhs_top, rhs_one, rhs_two, rhs_leaf, parent_map_one, parent_map_two, parent_map_leaf):
    inverses = [inverse_top, inverse_one, inverse_two, inverse_leaf]
    couplings = [None, coupling_one, coupling_two, coupling_leaf]
    right_sides = [rhs_top, rhs_one, rhs_two, rhs_leaf]
    parent_maps = [None, parent_map_one, parent_map_two, parent_map_leaf]
    orders = [SEP_TOP, SEP_ONE, SEP_TWO, SEP_LEAF]
    pivots = [[None] * (2 ** tree_level) for tree_level in range(4)]
    updates = [[None] * (2 ** tree_level) for tree_level in range(4)]
    for tree_level in (3, 2, 1, 0):
        sep_order = orders[tree_level]
        for front_at in range(2 ** tree_level):
            right_side = right_sides[tree_level][:, front_at * COLUMNS:(front_at + 1) * COLUMNS]
            if tree_level == 3:
                separator = right_side
                update = jnp.zeros((sep_order, COLUMNS), jnp.bfloat16)
            else:
                length = sep_order + (sep_order if tree_level > 0 else 0)
                extended = jnp.zeros((length, COLUMNS), jnp.float32)
                for child_at in (2 * front_at, 2 * front_at + 1):
                    extended = extended.at[parent_maps[tree_level + 1][child_at]].add(updates[tree_level + 1][child_at].astype(jnp.float32))
                separator = (right_side.astype(jnp.float32) + extended[:sep_order]).astype(jnp.bfloat16)
                update = lax.optimization_barrier(extended[sep_order:].astype(jnp.bfloat16))
            inverse = inverses[tree_level][front_at * sep_order:(front_at + 1) * sep_order]
            pivot_out = pivot_product(inverse, separator).astype(jnp.bfloat16)
            pivots[tree_level][front_at] = pivot_out
            if tree_level > 0:
                coupling = couplings[tree_level][:, front_at * sep_order:(front_at + 1) * sep_order]
                coupled = jnp.dot(coupling, pivot_out, preferred_element_type=jnp.float32)
                updates[tree_level][front_at] = (update.astype(jnp.float32) - coupled).astype(jnp.bfloat16)
    solutions = [[None] * (2 ** tree_level) for tree_level in range(4)]
    gathered_rows = [[None] * (2 ** tree_level) for tree_level in range(4)]
    for tree_level in range(4):
        sep_order = orders[tree_level]
        for front_at in range(2 ** tree_level):
            pivot_out = pivots[tree_level][front_at]
            if tree_level == 0:
                residual = pivot_out
            else:
                parent_at = front_at // 2
                pieces = [solutions[tree_level - 1][parent_at]]
                if tree_level > 1:
                    pieces.append(gathered_rows[tree_level - 1][parent_at])
                parent_rows = jnp.concatenate(pieces, axis=0)
                gathered = parent_rows[parent_maps[tree_level][front_at]]
                gathered_rows[tree_level][front_at] = gathered
                coupling = couplings[tree_level][:, front_at * sep_order:(front_at + 1) * sep_order]
                residual = (pivot_out.astype(jnp.float32) - coupling_back(coupling, gathered)).astype(jnp.bfloat16)
            inverse = inverses[tree_level][front_at * sep_order:(front_at + 1) * sep_order]
            solutions[tree_level][front_at] = jnp.dot(inverse.T, residual, preferred_element_type=jnp.float32).astype(jnp.bfloat16)
    outputs = [jnp.concatenate(solutions[tree_level], axis=1) for tree_level in range(4)]
    return (outputs[0], outputs[1], outputs[2], outputs[3])
```

```python
import functools

import jax
import jax.numpy as jnp
from jax import lax
from jax.experimental import pallas as pl
from jax.experimental.pallas import tpu as pltpu
from jax.sharding import PartitionSpec as P


def swapped(value, axis, stride):
    mask = 2**stride
    pairs = [(source, source ^ mask) for source in range(lax.axis_size(axis))]
    return lax.ppermute(value, axis, pairs)


def route_tables(mapping, child_index, parent_sep, parent_upd, strips, row_index):
    positions = lax.dynamic_index_in_dim(mapping, child_index, 0, keepdims=False)
    sep_rows = parent_sep // strips
    in_separator = positions < parent_sep
    if parent_upd > 0:
        upd_rows = parent_upd // strips
        target = jnp.where(
            in_separator, positions // sep_rows, (positions - parent_sep) // upd_rows
        )
        offset = jnp.where(
            in_separator, positions % sep_rows, sep_rows + (positions - parent_sep) % upd_rows
        )
    else:
        target = positions // sep_rows
        offset = positions % sep_rows
    block_rows = positions.shape[0] // strips
    blocks = target.reshape(strips, block_rows)
    matches = (blocks[:, :, None] == jnp.arange(strips, dtype=jnp.int32)[None, None, :]).astype(
        jnp.int32
    )
    slot_of = jnp.sum((jnp.cumsum(matches, axis=1) - 1) * matches, axis=2).reshape(-1)
    block_len = sep_rows + parent_upd // strips
    capacity = 2 * positions.shape[0] // (strips * strips)
    source = jnp.arange(positions.shape[0], dtype=jnp.int32) // block_rows
    mine_here = target == row_index
    column_at = jnp.where(mine_here, slot_of, capacity)
    lookup = jnp.full((strips, capacity + 1), block_len, jnp.int32)
    lookup = lookup.at[source, column_at].set(jnp.where(mine_here, offset, block_len))[:, :capacity]
    local_target = lax.dynamic_slice_in_dim(target, row_index * block_rows, block_rows)
    local_slots = lax.dynamic_slice_in_dim(slot_of, row_index * block_rows, block_rows)
    return (local_target, local_slots, lookup, capacity, block_len)


def pack_rows(values, local_target, local_slots, strips, capacity):
    buffer = jnp.zeros((strips, capacity, values.shape[1]), values.dtype)
    return buffer.at[local_target, local_slots].set(values)


def unpack_rows(received, lookup, block_len):
    summed = jnp.zeros((block_len + 1, received.shape[2]), jnp.float32)
    return summed.at[lookup].add(received.astype(jnp.float32))[:block_len]


def spread(portion, depth_bits, pass_on, column):
    for bit_index in range(depth_bits):
        partner = pass_on(portion, bit_index)
        is_upper = column >> bit_index & 1 == 1
        portion = jnp.where(
            is_upper,
            jnp.concatenate([partner, portion], axis=-1),
            jnp.concatenate([portion, partner], axis=-1),
        )
    return portion


def shrink(entire, depth_bits, pass_on, column):
    for bit_index in reversed(range(depth_bits)):
        half_width = entire.shape[-1] // 2
        low_part = entire[..., :half_width]
        high_part = entire[..., half_width:]
        is_upper = column >> bit_index & 1 == 1
        kept_part = jnp.where(is_upper, high_part, low_part)
        sent_part = jnp.where(is_upper, low_part, high_part)
        entire = kept_part + pass_on(sent_part, bit_index)
    return entire


def per_device(
    inverse_top,
    inverse_one,
    inverse_two,
    inverse_leaf,
    coupling_one,
    coupling_two,
    coupling_leaf,
    rhs_top,
    rhs_one,
    rhs_two,
    rhs_leaf,
    parent_map_one,
    parent_map_two,
    parent_map_leaf,
):
    strips = lax.axis_size("row")
    col_count = lax.axis_size("col")
    row_here = lax.axis_index("row")
    column = lax.axis_index("col")
    inverses = [inverse_top, inverse_one, inverse_two, inverse_leaf]
    couplings = [None, coupling_one, coupling_two, coupling_leaf]
    right_sides = [rhs_top, rhs_one, rhs_two, rhs_leaf]
    parent_maps = [None, parent_map_one, parent_map_two, parent_map_leaf]
    orders = [inverse.shape[1] * strips for inverse in inverses]
    groups = [col_count >> tree_level for tree_level in range(4)]
    group_bits = [group_size.bit_length() - 1 for group_size in groups]
    pass_rhs = lambda values, bit_index: swapped(values, "col", bit_index)
    pass_update_sum = lambda values, bit_index: swapped(
        values.astype(jnp.bfloat16), "col", bit_index
    ).astype(values.dtype)
    pass_update_spread = lambda values, bit_index: swapped(values, "col", bit_index)
    pass_solution_sum = lambda values, bit_index: swapped(
        values.astype(jnp.bfloat16), "col", bit_index
    ).astype(values.dtype)
    pass_solution_spread = lambda values, bit_index: swapped(values, "col", bit_index)
    full_rhs = [
        spread(right_sides[tree_level], group_bits[tree_level], pass_rhs, column)
        for tree_level in range(4)
    ]
    own_routes = [None]
    for tree_level in range(1, 4):
        parent_order = orders[tree_level - 1]
        parent_update = parent_order if tree_level > 1 else 0
        front_here = column // groups[tree_level]
        own_routes.append(
            route_tables(
                parent_maps[tree_level], front_here, parent_order, parent_update, strips, row_here
            )
        )
    pivots = [None] * 4
    incoming = None
    for tree_level in (3, 2, 1, 0):
        sep_rows = inverses[tree_level].shape[1]
        if incoming is None:
            separator = full_rhs[tree_level]
            own_update = None
        else:
            separator = (full_rhs[tree_level].astype(jnp.float32) + incoming[:sep_rows]).astype(
                jnp.bfloat16
            )
            own_update = lax.optimization_barrier(incoming[sep_rows:].astype(jnp.bfloat16))
        partial_value = jnp.dot(inverses[tree_level], separator, preferred_element_type=jnp.float32)
        solved = lax.psum(partial_value.astype(jnp.bfloat16), "row")
        pivots[tree_level] = solved
        if tree_level > 0:
            coupled = jnp.dot(couplings[tree_level], solved, preferred_element_type=jnp.float32)
            reduced = shrink(coupled, group_bits[tree_level], pass_update_sum, column)
            if own_update is None:
                portion = (-reduced).astype(jnp.bfloat16)
            else:
                start_at = column % groups[tree_level] * reduced.shape[1]
                kept_rows = lax.dynamic_slice_in_dim(own_update, start_at, reduced.shape[1], 1)
                portion = (kept_rows.astype(jnp.float32) - reduced).astype(jnp.bfloat16)
            updated = spread(portion, group_bits[tree_level], pass_update_spread, column)
            own_target, own_slots, own_lookup, capacity, block_len = own_routes[tree_level]
            got_own = lax.all_to_all(
                pack_rows(updated, own_target, own_slots, strips, capacity),
                "row",
                split_axis=0,
                concat_axis=0,
                tiled=True,
            )
            own_part = unpack_rows(got_own, own_lookup, block_len)
            partner = swapped(own_part.astype(jnp.bfloat16), "col", group_bits[tree_level])
            incoming = own_part + partner.astype(jnp.float32)
    solutions = [None] * 4
    parent_solution = None
    parent_gathered = None
    for tree_level in range(4):
        solved = pivots[tree_level]
        gathered = None
        if tree_level == 0:
            residual = solved
        else:
            own_target, own_slots, own_lookup, capacity, block_len = own_routes[tree_level]
            pieces = [parent_solution]
            if parent_gathered is not None:
                pieces.append(parent_gathered)
            pieces.append(jnp.zeros((1, parent_solution.shape[1]), jnp.bfloat16))
            parent_rows = jnp.concatenate(pieces, axis=0)
            returned = lax.all_to_all(
                parent_rows[own_lookup], "row", split_axis=0, concat_axis=0, tiled=True
            )
            gathered = returned[own_target, own_slots]
            coupling_term = jnp.dot(
                couplings[tree_level].T, gathered, preferred_element_type=jnp.float32
            )
            residual = (
                solved.astype(jnp.float32)
                - lax.psum(coupling_term.astype(jnp.bfloat16), "row").astype(jnp.float32)
            ).astype(jnp.bfloat16)
        contribution = jnp.dot(inverses[tree_level].T, residual, preferred_element_type=jnp.float32)
        if tree_level == 0:
            summed = lax.psum(contribution.astype(jnp.bfloat16), "col")
            solution = summed
            rhs_width = solution.shape[1] // groups[0]
            solutions[0] = lax.dynamic_slice_in_dim(
                solution, column % groups[0] * rhs_width, rhs_width, 1
            )
        else:
            portion = shrink(
                contribution, group_bits[tree_level], pass_solution_sum, column
            ).astype(jnp.bfloat16)
            solutions[tree_level] = portion
            if tree_level < 3:
                solution = spread(portion, group_bits[tree_level], pass_solution_spread, column)
        parent_solution = solution
        parent_gathered = gathered
    return (solutions[0], solutions[1], solutions[2], solutions[3])


MESH = pl.DeviceIdType.MESH
VMEM_LIMIT = 56 * 2**20


def dot_nn(left, right):
    return lax.dot_general(left, right, (((1,), (0,)), ((), ())), preferred_element_type=jnp.float32)


def dot_nt(left, right):
    return lax.dot_general(left, right, (((1,), (1,)), ((), ())), preferred_element_type=jnp.float32)


def eye(size):
    rows = lax.broadcasted_iota(jnp.int32, (size, size), 0)
    columns = lax.broadcasted_iota(jnp.int32, (size, size), 1)
    return jnp.where(rows == columns, 1.0, 0.0).astype(jnp.bfloat16)


def flipped(value, mask):
    result = value
    bit = 1
    while bit <= mask:
        if mask & bit:
            result = result + bit * (1 - 2 * ((value // bit) % 2))
        bit *= 2
    return result


class Plan:
    def __init__(self, rows, cols, inverse_shapes, rhs_top_shape, map_shape):
        self.rows, self.cols = rows, cols
        self.strip = [shape[1] for shape in inverse_shapes]
        self.order = [shape[1] * rows for shape in inverse_shapes]
        self.local = [shape[0] for shape in inverse_shapes]
        self.group = [cols >> level for level in range(4)]
        self.columns = rhs_top_shape[1] * cols
        self.width = [self.columns // group if group else 0 for group in self.group]
        self.mine = self.columns // rows
        self.map_shape = map_shape

    def total(self, level):
        return self.order[level] * (2 if level else 1)

    def span_rows(self):
        n, order, width = self.mine, self.order, self.width
        shared = 7 * (n // 4) * order[1] + 10 * (n // 2) * (order[0] // 4) + n // 2 * order[1]
        inner = 2 * n * order[3] + 4 * n * order[2] + 7 * (n // 4) * order[1]
        return max(shared, inner, 7 * width[0] * order[0], 3 * n * order[2]) // 128

    def fits(self):
        table = sum(
            2 * self.total(level) * self.order[level + 1] * 2 for level in range(3)
        )
        if self.rows != 4 or self.group[3] != 1 or self.mine * self.rows != self.columns or table > 24 * 2**20:
            return False
        if self.group != [8, 4, 2, 1] or self.mine % 64:
            return False
        for level in range(4):
            if self.strip[level] % 64 or self.order[level] % 128 or self.local[level] % 64:
                return False
        if not packed((self.mine, self.strip[1])):
            return False
        return narrow(self.strip[3]) and not any(narrow(strip) for strip in self.strip[:3])


def elements(shape):
    count = 1
    for extent in shape:
        count *= extent
    return count


def packed(shape):
    return shape[1] > 128 and shape[1] % 128 == 64


def packed_shape(shape):
    return (shape[0] * (shape[1] // 128) + shape[0] // 2, 128)


def narrow(size):
    return size < 128


def phase(number):
    return jax.named_scope(str(number))


def build_kernel(plan):
    R, CC, N = plan.rows, plan.cols, plan.mine
    S, K, L, G, W = plan.order, plan.strip, plan.local, plan.group, plan.width
    N2, NH, NQ, chips = 2 * N, N // 2, N // G[1], G[0] // 2
    bf = jnp.bfloat16
    scratch = []

    def ref(shape, dtype=bf):
        scratch.append(pltpu.VMEM(shape, dtype))
        return len(scratch) - 1

    def sems(*shape):
        scratch.append(pltpu.SemaphoreType.DMA(shape) if shape else pltpu.SemaphoreType.DMA)
        return len(scratch) - 1

    levels, lower = range(4), (1, 2, 3)
    z_shape = [(S[3], L[3]) if l == 3 else (L[l], S[l]) for l in levels]
    c_shape = [None] + [(S[l], L[l]) for l in lower]
    Z = [ref(z_shape[l]) for l in levels]
    C = [None] + [ref(c_shape[l]) for l in lower]
    Zm = [None] + [ref(z_shape[l]) for l in lower]
    Cm = [None] + [ref(c_shape[l]) for l in lower]
    Zp = [ref((R,) + packed_shape((L[l], K[l]))) if l < 3 and packed((L[l], K[l])) else None for l in levels]
    Cp = [None] + [ref((R,) + packed_shape((K[l], L[l]))) if packed((K[l], L[l])) else None for l in lower]
    Zraw = [ref((L[l], K[l])) if Zp[l] is not None else None for l in levels]
    Craw = [None] + [ref((K[l], L[l])) if Cp[l] is not None else None for l in lower]
    Zr, Zs = [sems(R) for _ in levels], [sems() for _ in levels]
    Cr, Cs = [sems(R) for _ in levels], [sems() for _ in levels]
    Zmr, Zms = [sems() for _ in levels], [sems() for _ in levels]
    Cmr, Cms = [sems() for _ in levels], [sems() for _ in levels]
    table = [ref((2, plan.total(l), S[l + 1])) for l in range(3)]
    held_map = [None] + [ref(plan.map_shape[l - 1], jnp.int32) for l in lower]
    local = sems(8)
    B = [ref((N, S[0])), ref((2, R) + packed_shape((N, K[1]))), ref((S[2], N2)), ref((S[3], N2))]
    B1, rhs_raw, rhs_packed = ref((N2, S[1])), ref((N, K[1])), ref(packed_shape((N, K[1])))
    Bs, Br = [sems() for _ in levels], [sems() for _ in levels]
    Ds, Dr = [sems(), sems(G[1]), sems()], [sems(2), sems(2), sems()]
    y = [ref((N, L[0]))] + [ref((4, NH, L[l])) for l in lower]
    yb = [None] + [ref((2, NH, L[l])) for l in lower]
    ys, yr = [sems() for _ in levels], [sems() for _ in levels]
    u = [None, ref((2, G[1], NQ, S[1])), ref((2, 2, G[1], NQ, S[2])), ref((2, N2, S[3]))]
    ur = [sems() for _ in levels]
    up1, ut1, ut1r = ref((2, G[1], NQ, S[1])), ref((G[1], NQ, S[1])), sems()
    h1 = ref((2, NQ, S[1]))
    up2, ut2, ut2r = ref((2, N, S[2])), ref((N, S[2])), sems()
    xp0, xr0, xr0r = ref((chips, 2, NH, S[0] // chips)), ref((CC, NH, S[0] // chips)), sems()
    xs0, xs0r = ref((chips, NH, S[0] // chips)), sems()
    xp1, xr1, xr1r = ref((NH, S[1])), ref((NH, S[1])), sems()
    v = [None] + [ref((NH, S[l])) for l in (1, 2)]
    x1, x2 = ref((NH, S[1])), ref((NH, S[2]))
    f1, f3 = ref((R, NH, K[1])), ref((2 * R, NH, K[3]))
    Os, Or = [sems() for _ in levels], [sems() for _ in levels]
    plane, inner = sems(), sems()
    span = ref((plan.span_rows(), 128))

    def kernel(*refs):
        inverse = refs[0:4]
        coupling = (None,) + tuple(refs[4:7])
        rhs = refs[7:11]
        maps = (None,) + tuple(refs[11:14])
        outs = refs[14:18]
        held = refs[18:]
        at = lambda index: held[index]
        z = lax.axis_index("row")
        c = lax.axis_index("col")
        core, chip = c % 2, c // 2
        middle = jnp.logical_and(z > 0, z < R - 1)
        border = jnp.logical_not(middle)
        half = z % 2
        pair = z + 1 - 2 * half
        across = R - 1 - z
        beyond = R - 1 - pair
        sent = {}

        def remote(src, dst, ssem, rsem, z_to, c_to):
            return pltpu.make_async_remote_copy(
                src_ref=src, dst_ref=dst, send_sem=ssem, recv_sem=rsem,
                device_id=(z_to, c_to), device_id_type=MESH,
            )

        def push(src, dst, ssem, rsem, z_to, c_to):
            remote(src, dst, ssem, rsem, z_to, c_to).start()

        def counted(src, dst, index, rsem, z_to, c_to):
            push(src, dst, at(index), rsem, z_to, c_to)
            sent[index] = sent.get(index, 0) + elements(src.shape)

        def arrived(dst, rsem):
            pltpu.make_async_copy(dst, dst, rsem).wait()

        def take(sem, count):
            view = at(span).at[pl.ds(0, count // 128)]
            pltpu.make_async_copy(view, view, sem).wait()

        barrier = pltpu.get_barrier_semaphore()
        friends = [(z, flipped(c, m)) for m in range(1, CC)]
        for d in range(1, R):
            friends += [((z + d) % R, c), ((z + d) % R, flipped(c, 1))]
        friends += [(pair, flipped(c, m)) for m in range(2, G[1])]
        for friend in friends:
            pl.semaphore_signal(barrier, inc=1, device_id=friend, device_id_type=MESH)

        raws = []
        for l in levels:
            if Zp[l] is not None:
                raws.append((inverse[l], at(Zraw[l])))
            if l and Cp[l] is not None:
                raws.append((coupling[l], at(Craw[l])))
        raws.append((rhs[1], at(rhs_raw)))
        loads = raws + [(maps[l], at(held_map[l])) for l in lower]
        for i, (src, dst) in enumerate(loads):
            pltpu.make_async_copy(src, dst, at(local).at[i]).start()

        def slot(kind, l, r):
            if kind == 0:
                if Zp[l] is not None:
                    return at(Zp[l]).at[r], at(Zr[l]).at[r]
                if l == 3:
                    low = pl.multiple_of(r * K[l], 16)
                    return at(Z[l]).at[pl.ds(low, K[l])], at(Zr[l]).at[r]
                low = pl.multiple_of(r * K[l], 128)
                return at(Z[l]).at[:, pl.ds(low, K[l])], at(Zr[l]).at[r]
            if Cp[l] is not None:
                return at(Cp[l]).at[r], at(Cr[l]).at[r]
            low = pl.multiple_of(r * K[l], 16)
            return at(C[l]).at[pl.ds(low, K[l])], at(Cr[l]).at[r]

        def is_packed(kind, l):
            return (Zp, Cp)[kind][l] is not None

        def source(kind, l):
            if is_packed(kind, l):
                return slot(kind, l, z)[0]
            return (inverse, coupling)[kind][l]

        def send_sem(kind, l):
            return at((Zs, Cs)[kind][l])

        def own_load(kind, l):
            if not is_packed(kind, l):
                dst, sem = slot(kind, l, z)
                pltpu.make_async_copy(source(kind, l), dst, sem).start()

        def own_send(kind, l):
            dst, sem = slot(kind, l, z)
            push(source(kind, l), dst, send_sem(kind, l), sem, jnp.where(middle, across, pair), c)

            @pl.when(border)
            def _():
                push(source(kind, l), dst, send_sem(kind, l), sem, beyond, c)

        def own_out(kind, l):
            dst, sem = slot(kind, l, z)
            push(source(kind, l), dst, send_sem(kind, l), sem, pair, c)

        def pass_on(kind, l):
            for r in (across, beyond):
                dst, sem = slot(kind, l, r)
                push(dst, dst, send_sem(kind, l), sem, pair, c)

        def settle(kind, l, which):
            for r in which:
                arrived(*slot(kind, l, r))

        def settle_all(kind, l):
            settle(kind, l, (pair, across, beyond) if is_packed(kind, l) else (z, pair, across, beyond))
            if is_packed(kind, l):
                unpack(kind, l)

        def unpacked(block, rows, lanes):
            whole = lanes // 128 * rows
            rest = block[whole:]
            rest = jnp.concatenate([rest[:, :lanes % 128], rest[:, lanes % 128:]], axis=0)
            return jnp.concatenate([block[i:i + rows] for i in range(0, whole, rows)] + [rest], axis=1)

        def unpack(kind, l):
            rows, lanes = (L[l], K[l]) if kind == 0 else (K[l], L[l])
            for r in range(R):
                value = unpacked(at((Zp, Cp)[kind][l])[r], rows, lanes)
                if kind == 0:
                    at(Z[l])[:, r * lanes:(r + 1) * lanes] = value
                else:
                    at(C[l])[r * rows:(r + 1) * rows, :] = value

        def pack(raw):
            value = raw[...]
            rows, lanes = value.shape
            whole = lanes - lanes % 128
            pieces = [value[:, i:i + 128] for i in range(0, whole, 128)]
            rest = value[:, whole:]
            rest = jnp.concatenate([rest[:rows // 2], rest[rows // 2:]], axis=1)
            return jnp.concatenate(pieces + [rest], axis=0)

        def drain(kind, l):
            if is_packed(kind, l):
                whole = at((Zp, Cp)[kind][l])
                part = whole.at[pl.ds(0, R // 2)]
            else:
                whole = at((Z, C)[kind][l])
                if kind == 0 and l < 3:
                    part = whole.at[:, pl.ds(0, S[l] // 2)]
                else:
                    part = whole.at[pl.ds(0, S[l] // 2)]

            @pl.when(middle)
            def _():
                arrived(whole, send_sem(kind, l))

            @pl.when(border)
            def _():
                arrived(part, send_sem(kind, l))

        def rhs_pieces(l):
            q = c % G[l]
            if l == 3:
                return [
                    (rhs[3].at[:, pl.ds(i * N2, N2)], at(B[3]).at[pl.ds(pl.multiple_of(z * K[3], 16), K[3])], 1 + i)
                    for i in range(2)
                ]
            if l == 2:
                return [(rhs[2], at(B[2]).at[pl.ds(pl.multiple_of(z * K[2], 16), K[2])], 1 + q)]
            if l == 1:
                return [(at(rhs_packed), at(B[1]).at[q % 2, z], 1 + q // 2)]
            rows = pl.ds(pl.multiple_of((q % 2) * W[0], W[0]), W[0])
            lanes = pl.ds(pl.multiple_of(z * K[0], 128), K[0])
            return [(rhs[0], at(B[0]).at[rows, lanes], q // 2)]

        def start_rhs(l):
            for src, dst, z_to in rhs_pieces(l):
                @pl.when(z_to == z)
                def _():
                    pltpu.make_async_copy(src, dst, at(Br[l])).start()

                @pl.when(z_to != z)
                def _():
                    push(src, dst, at(Bs[l]), at(Br[l]), z_to, c)

        def drain_rhs(l):
            pieces = rhs_pieces(l)
            if l == 3:
                @pl.when(middle)
                def _():
                    arrived(at(B[3]).at[pl.ds(0, K[3])], at(Bs[3]))

                @pl.when(border)
                def _():
                    arrived(at(B[3]).at[pl.ds(0, 2 * K[3])], at(Bs[3]))
                return
            src, dst, z_to = pieces[0]

            @pl.when(z_to != z)
            def _():
                arrived(dst, at(Bs[l]))

        def rhs_spread(l):
            q = c % G[l]
            if l == 2:
                return z == 1 + q, at(B[2]), at(Dr[2])
            if l == 1:
                return z == 1 + q // 2, at(B[1]).at[q % 2], at(Dr[1]).at[q % 2]
            rows = pl.ds(pl.multiple_of((q % 2) * W[0], W[0]), W[0])
            return z == q // 2, at(B[0]).at[rows], at(Dr[0]).at[q % 2]

        def spread_rhs(l):
            holds, here, rsem = rhs_spread(l)

            @pl.when(holds)
            def _():
                arrived(here, at(Br[l]))
                for m in range(1, G[l]):
                    ssem = at(Ds[l]).at[m] if l == 1 else at(Ds[l])
                    push(here, here, ssem, rsem, z, flipped(c, m))

        def drain_spread(l):
            holds, here, _ = rhs_spread(l)

            @pl.when(holds)
            def _():
                if l == 1:
                    for m in range(1, G[l]):
                        arrived(here, at(Ds[l]).at[m])
                else:
                    take(at(Ds[l]), (G[l] - 1) * elements(here.shape))

        def wait_rhs(l):
            holds, here, rsem = rhs_spread(l)
            if l == 2:
                @pl.when(jnp.logical_not(holds))
                def _():
                    arrived(here, rsem)
                return
            for part in range(2):
                @pl.when(jnp.logical_not(jnp.logical_and(holds, c % 2 == part)))
                def _():
                    view = at(B[1]).at[part] if l == 1 else at(B[0]).at[pl.ds(part * W[0], W[0])]
                    arrived(view, at(Dr[l]).at[part])

        def make_table(l):
            front = c // G[l]
            step = K[l]
            for child in range(2):
                row = at(held_map[l + 1])[pl.ds(2 * front + child, 1), :]

                def body(i, carry):
                    start = pl.multiple_of(i * step, 16)
                    at_row = lax.broadcasted_iota(jnp.int32, (step, S[l + 1]), 0) + start
                    at(table[l])[child, pl.ds(start, step), :] = jnp.where(
                        at_row == row, 1.0, 0.0
                    ).astype(bf)
                    return carry

                lax.fori_loop(0, plan.total(l) // step, body, 0)

        def gathered(l, low, size, first, second):
            value = dot_nt(first, at(table[l])[0, low:low + size, :])
            return value + dot_nt(second, at(table[l])[1, low:low + size, :])

        def forward(kind, l):
            own, copy = at((Z, C)[kind][l]), at((Zm, Cm)[kind][l])
            push(
                own, copy, at((Zms, Cms)[kind][l]), at((Zmr, Cmr)[kind][l]), z, flipped(c, 1)
            )

        with phase(1):
            for i, (src, dst) in enumerate(loads):
                pltpu.make_async_copy(src, dst, at(local).at[i]).wait()
            for l in levels:
                if Zp[l] is not None:
                    at(Zp[l])[z] = pack(at(Zraw[l]))
                if l and Cp[l] is not None:
                    at(Cp[l])[z] = pack(at(Craw[l]))
            at(rhs_packed)[...] = pack(at(rhs_raw))
        with phase(2):
            pl.semaphore_wait(barrier, len(friends))

        with phase(3):
            own_send(0, 3)
            start_rhs(3)
            own_send(1, 3)
            for l in (2, 1, 0):
                start_rhs(l)
            own_send(0, 2)
            own_send(1, 2)
            own_send(0, 1)
            own_send(1, 1)
            own_send(0, 0)
            for l in levels:
                own_load(0, l)
                if l:
                    own_load(1, l)

            @pl.when(middle)
            def _():
                own_out(0, 0)
                for l in (3, 2, 1):
                    own_out(0, l)
                    own_out(1, l)
        make_table(2)

        @pl.when(middle)
        def _():
            with phase(31):
                arrived(at(B[3]), at(Br[3]))
                right = dot_nt(eye(N2), at(B[3])[...]).astype(bf)
                settle_all(0, 3)
            with phase(32):
                solved = dot_nn(right, at(Z[3])[...]).astype(bf)
                at(y[3])[...] = solved.reshape(4, NH, L[3])
                settle_all(1, 3)
            with phase(33):
                at(u[3])[core] = (-dot_nt(solved, at(C[3])[...])).astype(bf)
                here = at(u[3]).at[core]
                counted(here, here, inner, at(ur[3]), z, flipped(c, 1))
                pass_on(0, 3)
                pass_on(1, 3)
        for l in (2, 1, 0):
            spread_rhs(l)
        make_table(1)

        @pl.when(middle)
        def _():
            with phase(21):
                arrived(at(u[3]).at[0], at(ur[3]))
                wait_rhs(2)
            with phase(22):
                pair_of = at(u[3])[0], at(u[3])[1]
                right = dot_nt(eye(N2), at(B[2])[...]) + gathered(2, 0, S[2], *pair_of)
                right = right.astype(bf)
                lower_part = pl.ds(pl.multiple_of(core * N, N), N)
                pair_of = at(u[3])[0, lower_part, :], at(u[3])[1, lower_part, :]
                kept = gathered(2, S[2], S[2], *pair_of)
            with phase(23):
                settle_all(0, 2)
                pass_on(0, 2)
            with phase(24):
                solved = dot_nt(right, at(Z[2])[...]).astype(bf)
                at(y[2])[...] = solved.reshape(4, NH, L[2])
            with phase(25):
                settle_all(1, 2)
                pass_on(1, 2)
            with phase(26):
                at(up2)[...] = dot_nt(solved, at(C[2])[...]).astype(bf).reshape(2, N, S[2])
                counted(at(up2).at[1 - core], at(ut2), inner, at(ut2r), z, flipped(c, 1))
            with phase(27):
                own = at(up2)[core].astype(jnp.float32)
                arrived(at(ut2), at(ut2r))
                own = kept - (own + at(ut2)[...].astype(jnp.float32))
                child = (c // G[2]) % 2
                at(u[2])[child, core] = own.astype(bf).reshape(G[1], NQ, S[2])
                here = at(u[2]).at[child, core]
                for m in range(1, G[1]):
                    counted(here, here, inner, at(ur[2]), z, flipped(c, m))
        make_table(0)
        q, child = c % G[1], (c // G[1]) % 2

        @pl.when(middle)
        def _():
            with phase(11):
                wait_rhs(1)
                for part in range(2):
                    for r in range(R):
                        value = unpacked(at(B[1])[part, r], N, K[1])
                        at(B1)[part * N:(part + 1) * N, r * K[1]:(r + 1) * K[1]] = value
            with phase(12):
                take(at(ur[2]), 3 * N * S[2])
            with phase(13):
                pair_of = [at(u[2])[i].reshape(N2, S[2]) for i in range(2)]
                right = at(B1)[...].astype(jnp.float32) + gathered(1, 0, S[1], *pair_of)
                right = right.astype(bf)
                pair_of = [at(u[2])[i, :, q].reshape(2 * NQ, S[2]) for i in range(2)]
                kept = gathered(1, S[1], S[1], *pair_of)
                at(h1)[...] = kept.astype(bf).reshape(2, NQ, S[1])
            with phase(14):
                settle_all(0, 1)
            with phase(15):
                solved = dot_nt(right, at(Z[1])[...]).astype(bf)
                at(y[1])[...] = solved.reshape(4, NH, L[1])
            with phase(16):
                settle_all(1, 1)
            with phase(17):
                coupled = dot_nt(solved, at(C[1])[...])
                at(up1)[...] = coupled.astype(bf).reshape(2, G[1], NQ, S[1])
                at(up1)[1 - half, q] = (
                    at(up1)[1 - half, q].astype(jnp.float32) - at(h1)[1 - half].astype(jnp.float32)
                ).astype(bf)
                for m in range(G[1]):
                    src = at(up1).at[1 - half, flipped(q, m)]
                    counted(src, at(ut1).at[m], inner, at(ut1r), pair, flipped(c, m))
                for m in range(1, G[1]):
                    src = at(up1).at[half, flipped(q, m)]
                    counted(src, at(ut1).at[m], inner, at(ut1r), z, flipped(c, m))

        @pl.when(border)
        def _():
            with phase(18):
                for l in (3, 2):
                    for kind in range(2):
                        settle_all(kind, l)
                        forward(kind, l)
                arrived(at(ut1), at(ut1r))
                value = at(ut1)[0].astype(jnp.float32)
                for m in range(1, G[1]):
                    value = value + at(ut1)[m].astype(jnp.float32)
                at(u[1])[child, q] = (-value).astype(bf)

        @pl.when(middle)
        def _():
            with phase(19):
                value = at(up1)[half, q].astype(jnp.float32)
                arrived(at(ut1).at[pl.ds(1, G[1] - 1)], at(ut1r))
                for m in range(1, G[1]):
                    value = value + at(ut1)[m].astype(jnp.float32)
                at(u[1])[child, q] = (at(h1)[half].astype(jnp.float32) - value).astype(bf)
        here = at(u[1]).at[child, q]
        for m in range(1, CC):
            counted(here, here, plane, at(ur[1]), z, flipped(c, m))

        @pl.when(middle)
        def _():
            with phase(20):
                for l in lower:
                    at(yb[l])[0] = at(y[l])[2 * half + core]
                    src = at(y[l]).at[2 * half + 1 - core]
                    push(src, at(yb[l]).at[1], at(ys[l]), at(yr[l]), z, flipped(c, 1))
                    src = at(y[l]).at[2 * (1 - half) + core]
                    push(src, at(yb[l]).at[0], at(ys[l]), at(yr[l]), pair, c)
                    src = at(y[l]).at[2 * (1 - half) + 1 - core]
                    push(src, at(yb[l]).at[1], at(ys[l]), at(yr[l]), pair, flipped(c, 1))
                for l in lower:
                    for kind in range(2):
                        forward(kind, l)
                settle(0, 0, (across, beyond))
                pass_on(0, 0)
                pass_on(0, 1)
                pass_on(1, 1)
        with phase(41):
            take(at(ur[1]), (CC - 1) * NQ * S[1])
            wait_rhs(0)
        with phase(42):
            pair_of = [at(u[1])[i].reshape(N, S[1]) for i in range(2)]
            right = at(B[0])[...].astype(jnp.float32) + gathered(0, 0, S[0], *pair_of)
            right = right.astype(bf)
        with phase(43):
            settle(0, 0, (z, pair))

            @pl.when(border)
            def _():
                settle(0, 0, (across, beyond))
        with phase(44):
            solved = dot_nt(right, at(Z[0])[...]).astype(bf)
            value = dot_nn(solved, at(Z[0])[...]).astype(bf)
            wide = S[0] // chips
            for j in range(chips):
                at(xp0)[j] = value[:, j * wide:(j + 1) * wide].reshape(2, NH, wide)
            for m in range(1, CC):
                to = flipped(c, m)
                counted(at(xp0).at[to // 2, to % 2], at(xr0).at[m], plane, at(xr0r), z, to)

        @pl.when(border)
        def _():
            with phase(45):
                for kind in range(2):
                    settle_all(kind, 1)
                    forward(kind, 1)
        with phase(46):
            value = at(xp0)[chip, core].astype(jnp.float32)
            arrived(at(xr0).at[pl.ds(1, CC - 1)], at(xr0r))
            for m in range(1, CC):
                value = value + at(xr0)[m].astype(jnp.float32)
            at(xs0)[chip] = value.astype(bf)
            here = at(xs0).at[chip]
            for m in range(2, CC, 2):
                counted(here, here, plane, at(xs0r), z, flipped(c, m))
        with phase(47):
            arrived(at(xs0).at[pl.ds(1, chips - 1)], at(xs0r))

        def leave(l, piece, dst, c_to):
            @pl.when(c_to == c)
            def _():
                pltpu.make_async_copy(piece(z), dst, at(Or[l])).start()

            @pl.when(c_to != c)
            def _():
                push(piece(z), dst, at(Os[l]), at(Or[l]), z, c_to)
            for d in (2, 1, 3):
                r = (z + d) % R
                push(piece(r), dst, at(Os[l]), at(Or[l]), r, c_to)

        top_here, one_here = chip == z, q // 2 == z // 2
        one_to, two_to = 2 * chip + z % 2, 2 * chip + z // 2

        @pl.when(top_here)
        def _():
            leave(0, lambda r: at(xs0).at[r], outs[0], c)

        def placed(l, low):
            return outs[l].at[pl.ds(pl.multiple_of(low, 16), NH)]

        with phase(51):
            value = None
            for r in range(chips):
                part = dot_nn(at(xs0)[r], at(table[0])[child, r * wide:(r + 1) * wide, :])
                value = part if value is None else value + part
            at(v[1])[...] = value.astype(bf)
            low = at(v[1])[...]

        def residual(l, index, coupled, low):
            return (at(yb[l])[index].astype(jnp.float32) - dot_nn(low, at(coupled[l])[...])).astype(bf)

        def wait_mate(l):
            @pl.when(middle)
            def _():
                arrived(at(yb[l]).at[1], at(yr[l]))

            @pl.when(border)
            def _():
                arrived(at(yb[l]), at(yr[l]))
            arrived(at(Zm[l]), at(Zmr[l]))
            arrived(at(Cm[l]), at(Cmr[l]))

        with phase(52):
            wait_mate(1)
        with phase(53):
            value = dot_nn(residual(1, 0, C, low), at(Z[1])[...])
            value = value + dot_nn(residual(1, 1, Cm, low), at(Zm[1])[...])
            at(xp1)[...] = value.astype(bf)
            counted(at(xp1), at(xr1), plane, at(xr1r), z, flipped(c, 2))
        side = chip % 2
        with phase(54):
            early = dot_nn(low, at(table[1])[side, S[1]:, :])
            arrived(at(xr1), at(xr1r))
        with phase(55):
            value = (at(xp1)[...].astype(jnp.float32) + at(xr1)[...].astype(jnp.float32)).astype(bf)
            at(v[2])[...] = (dot_nn(value, at(table[1])[side, :S[1], :]) + early).astype(bf)
            at(x1)[...] = value
            low = at(v[2])[...]
        with phase(56):
            wait_mate(2)
        with phase(57):
            value = dot_nn(residual(2, 0, C, low), at(Z[2])[...])
            value = value + dot_nn(residual(2, 1, Cm, low), at(Zm[2])[...])
            at(x2)[...] = value.astype(bf)
            high = at(x2)[...]
        with phase(58):
            @pl.when(one_here)
            def _():
                for r in range(R):
                    at(f1)[r] = at(x1)[:, r * K[1]:(r + 1) * K[1]]
                leave(1, lambda r: at(f1).at[r], placed(1, core * NH), one_to)

            def two_piece(r):
                return at(x2).at[:, pl.ds(pl.multiple_of(r * K[2], 128), K[2])]

            leave(2, two_piece, placed(2, half * N + core * NH), two_to)
        with phase(59):
            wait_mate(3)
        with phase(60):
            for mate in range(2):
                leaf = core if mate == 0 else 1 - core
                below = dot_nn(high, at(table[2])[leaf, :S[2], :])
                below = (below + dot_nn(low, at(table[2])[leaf, S[2]:, :])).astype(bf)
                left, right = ((C, Z), (Cm, Zm))[mate]
                value = dot_nt(residual(3, mate, left, below), at(right[3])[...]).astype(bf)
                for r in range(R):
                    at(f3)[mate * R + r] = value[:, r * K[3]:(r + 1) * K[3]]
                leave(
                    3, lambda r: at(f3).at[mate * R + r], placed(3, z * N + core * NH),
                    c if mate == 0 else flipped(c, 1),
                )
        with phase(61):
            for l in levels:
                drain(0, l)
                if l:
                    drain(1, l)
                    arrived(at(Zm[l]), at(Zms[l]))
                    arrived(at(Cm[l]), at(Cms[l]))
                drain_rhs(l)
                if l < 3:
                    drain_spread(l)

            @pl.when(middle)
            def _():
                for l in lower:
                    arrived(at(y[l]).at[pl.ds(0, 3)], at(ys[l]))
                take(at(inner), sent[inner])
            take(at(plane), sent[plane])

            @pl.when(top_here)
            def _():
                arrived(at(xs0).at[pl.ds(0, R - 1)], at(Os[0]))

            @pl.when(jnp.logical_and(one_here, one_to == c))
            def _():
                arrived(at(f1).at[pl.ds(0, R - 1)], at(Os[1]))

            @pl.when(jnp.logical_and(one_here, one_to != c))
            def _():
                arrived(at(f1), at(Os[1]))

            @pl.when(two_to == c)
            def _():
                arrived(at(x2).at[:, pl.ds(0, S[2] - K[2])], at(Os[2]))

            @pl.when(two_to != c)
            def _():
                arrived(at(x2), at(Os[2]))
            arrived(at(f3).at[pl.ds(0, 2 * R - 1)], at(Os[3]))
        with phase(62):
            for l in levels:
                arrived(outs[l], at(Or[l]))

    return kernel, scratch


def hand_on(turned, *refs):
    for turn, source, target in zip(turned, refs[:4], refs[4:]):
        if turn:
            target[...] = dot_nt(eye(target.shape[0]), source[...]).astype(target.dtype)
        else:
            target[...] = source[...]


def fused_device(*blocks):
    plan = Plan(
        lax.axis_size("row"), lax.axis_size("col"),
        [block.shape for block in blocks[:4]], blocks[7].shape,
        [block.shape for block in blocks[11:14]],
    )
    if not plan.fits():
        return per_device(*blocks)
    kernel, scratch = build_kernel(plan)
    blocks = list(blocks)
    for at in (0, 1, 2, 3, 7, 8, 9, 10):
        if narrow(blocks[at].shape[1]):
            blocks[at] = blocks[at].T
    vmem = pl.BlockSpec(memory_space=pltpu.VMEM)
    anywhere = pl.BlockSpec(memory_space=pltpu.HBM)
    solved = pl.pallas_call(
        kernel,
        out_shape=tuple(
            jax.ShapeDtypeStruct((width, strip), blocks[0].dtype)
            for width, strip in zip(plan.width, plan.strip)
        ),
        in_specs=[anywhere] * 14,
        out_specs=(anywhere,) * 4,
        scratch_shapes=scratch,
        compiler_params=pltpu.CompilerParams(
            collective_id=0, has_side_effects=True, vmem_limit_bytes=VMEM_LIMIT
        ),
    )(*blocks)
    turned = [not narrow(width) for width in plan.width]
    solved = pl.pallas_call(
        functools.partial(hand_on, turned),
        out_shape=tuple(
            jax.ShapeDtypeStruct(block.shape[::-1] if turn else block.shape, block.dtype)
            for block, turn in zip(solved, turned)
        ),
        in_specs=[vmem] * 4,
        out_specs=(vmem,) * 4,
    )(*solved)
    return tuple(block if turn else block.T for block, turn in zip(solved, turned))


def solution(mesh):
    in_specs = (
        P("col", "row"),
        P("col", "row"),
        P("col", "row"),
        P("col", "row"),
        P("row", "col"),
        P("row", "col"),
        P("row", "col"),
        P("row", "col"),
        P("row", "col"),
        P("row", "col"),
        P("row", "col"),
        P(),
        P(),
        P(),
    )
    out_specs = (P("row", "col"), P("row", "col"), P("row", "col"), P("row", "col"))
    return jax.shard_map(
        fused_device, mesh=mesh, in_specs=in_specs, out_specs=out_specs, check_vma=False
    )
```

```python
import functools

import jax
import jax.numpy as jnp
from jax import lax
from jax.experimental import pallas as pl
from jax.experimental.pallas import tpu as pltpu
from jax.sharding import PartitionSpec as P


def swapped(value, axis, stride):
    mask = 2**stride
    pairs = [(source, source ^ mask) for source in range(lax.axis_size(axis))]
    return lax.ppermute(value, axis, pairs)


def route_tables(mapping, child_index, parent_sep, parent_upd, strips, row_index):
    positions = lax.dynamic_index_in_dim(mapping, child_index, 0, keepdims=False)
    sep_rows = parent_sep // strips
    in_separator = positions < parent_sep
    if parent_upd > 0:
        upd_rows = parent_upd // strips
        target = jnp.where(
            in_separator, positions // sep_rows, (positions - parent_sep) // upd_rows
        )
        offset = jnp.where(
            in_separator, positions % sep_rows, sep_rows + (positions - parent_sep) % upd_rows
        )
    else:
        target = positions // sep_rows
        offset = positions % sep_rows
    block_rows = positions.shape[0] // strips
    blocks = target.reshape(strips, block_rows)
    matches = (blocks[:, :, None] == jnp.arange(strips, dtype=jnp.int32)[None, None, :]).astype(
        jnp.int32
    )
    slot_of = jnp.sum((jnp.cumsum(matches, axis=1) - 1) * matches, axis=2).reshape(-1)
    block_len = sep_rows + parent_upd // strips
    capacity = 2 * positions.shape[0] // (strips * strips)
    source = jnp.arange(positions.shape[0], dtype=jnp.int32) // block_rows
    mine_here = target == row_index
    column_at = jnp.where(mine_here, slot_of, capacity)
    lookup = jnp.full((strips, capacity + 1), block_len, jnp.int32)
    lookup = lookup.at[source, column_at].set(jnp.where(mine_here, offset, block_len))[:, :capacity]
    local_target = lax.dynamic_slice_in_dim(target, row_index * block_rows, block_rows)
    local_slots = lax.dynamic_slice_in_dim(slot_of, row_index * block_rows, block_rows)
    return (local_target, local_slots, lookup, capacity, block_len)


def pack_rows(values, local_target, local_slots, strips, capacity):
    buffer = jnp.zeros((strips, capacity, values.shape[1]), values.dtype)
    return buffer.at[local_target, local_slots].set(values)


def unpack_rows(received, lookup, block_len):
    summed = jnp.zeros((block_len + 1, received.shape[2]), jnp.float32)
    return summed.at[lookup].add(received.astype(jnp.float32))[:block_len]


def spread(portion, depth_bits, pass_on, column):
    for bit_index in range(depth_bits):
        partner = pass_on(portion, bit_index)
        is_upper = column >> bit_index & 1 == 1
        portion = jnp.where(
            is_upper,
            jnp.concatenate([partner, portion], axis=-1),
            jnp.concatenate([portion, partner], axis=-1),
        )
    return portion


def shrink(entire, depth_bits, pass_on, column):
    for bit_index in reversed(range(depth_bits)):
        half_width = entire.shape[-1] // 2
        low_part = entire[..., :half_width]
        high_part = entire[..., half_width:]
        is_upper = column >> bit_index & 1 == 1
        kept_part = jnp.where(is_upper, high_part, low_part)
        sent_part = jnp.where(is_upper, low_part, high_part)
        entire = kept_part + pass_on(sent_part, bit_index)
    return entire


def per_device(
    inverse_top,
    inverse_one,
    inverse_two,
    inverse_leaf,
    coupling_one,
    coupling_two,
    coupling_leaf,
    rhs_top,
    rhs_one,
    rhs_two,
    rhs_leaf,
    parent_map_one,
    parent_map_two,
    parent_map_leaf,
):
    strips = lax.axis_size("row")
    col_count = lax.axis_size("col")
    row_here = lax.axis_index("row")
    column = lax.axis_index("col")
    inverses = [inverse_top, inverse_one, inverse_two, inverse_leaf]
    couplings = [None, coupling_one, coupling_two, coupling_leaf]
    right_sides = [rhs_top, rhs_one, rhs_two, rhs_leaf]
    parent_maps = [None, parent_map_one, parent_map_two, parent_map_leaf]
    orders = [inverse.shape[1] * strips for inverse in inverses]
    groups = [col_count >> tree_level for tree_level in range(4)]
    group_bits = [group_size.bit_length() - 1 for group_size in groups]
    pass_rhs = lambda values, bit_index: swapped(values, "col", bit_index)
    pass_update_sum = lambda values, bit_index: swapped(
        values.astype(jnp.bfloat16), "col", bit_index
    ).astype(values.dtype)
    pass_update_spread = lambda values, bit_index: swapped(values, "col", bit_index)
    pass_solution_sum = lambda values, bit_index: swapped(
        values.astype(jnp.bfloat16), "col", bit_index
    ).astype(values.dtype)
    pass_solution_spread = lambda values, bit_index: swapped(values, "col", bit_index)
    full_rhs = [
        spread(right_sides[tree_level], group_bits[tree_level], pass_rhs, column)
        for tree_level in range(4)
    ]
    own_routes = [None]
    for tree_level in range(1, 4):
        parent_order = orders[tree_level - 1]
        parent_update = parent_order if tree_level > 1 else 0
        front_here = column // groups[tree_level]
        own_routes.append(
            route_tables(
                parent_maps[tree_level], front_here, parent_order, parent_update, strips, row_here
            )
        )
    pivots = [None] * 4
    incoming = None
    for tree_level in (3, 2, 1, 0):
        sep_rows = inverses[tree_level].shape[1]
        if incoming is None:
            separator = full_rhs[tree_level]
            own_update = None
        else:
            separator = (full_rhs[tree_level].astype(jnp.float32) + incoming[:sep_rows]).astype(
                jnp.bfloat16
            )
            own_update = lax.optimization_barrier(incoming[sep_rows:].astype(jnp.bfloat16))
        partial_value = jnp.dot(inverses[tree_level], separator, preferred_element_type=jnp.float32)
        solved = lax.psum(partial_value.astype(jnp.bfloat16), "row")
        pivots[tree_level] = solved
        if tree_level > 0:
            coupled = jnp.dot(couplings[tree_level], solved, preferred_element_type=jnp.float32)
            reduced = shrink(coupled, group_bits[tree_level], pass_update_sum, column)
            if own_update is None:
                portion = (-reduced).astype(jnp.bfloat16)
            else:
                start_at = column % groups[tree_level] * reduced.shape[1]
                kept_rows = lax.dynamic_slice_in_dim(own_update, start_at, reduced.shape[1], 1)
                portion = (kept_rows.astype(jnp.float32) - reduced).astype(jnp.bfloat16)
            updated = spread(portion, group_bits[tree_level], pass_update_spread, column)
            own_target, own_slots, own_lookup, capacity, block_len = own_routes[tree_level]
            got_own = lax.all_to_all(
                pack_rows(updated, own_target, own_slots, strips, capacity),
                "row",
                split_axis=0,
                concat_axis=0,
                tiled=True,
            )
            own_part = unpack_rows(got_own, own_lookup, block_len)
            partner = swapped(own_part.astype(jnp.bfloat16), "col", group_bits[tree_level])
            incoming = own_part + partner.astype(jnp.float32)
    solutions = [None] * 4
    parent_solution = None
    parent_gathered = None
    for tree_level in range(4):
        solved = pivots[tree_level]
        gathered = None
        if tree_level == 0:
            residual = solved
        else:
            own_target, own_slots, own_lookup, capacity, block_len = own_routes[tree_level]
            pieces = [parent_solution]
            if parent_gathered is not None:
                pieces.append(parent_gathered)
            pieces.append(jnp.zeros((1, parent_solution.shape[1]), jnp.bfloat16))
            parent_rows = jnp.concatenate(pieces, axis=0)
            returned = lax.all_to_all(
                parent_rows[own_lookup], "row", split_axis=0, concat_axis=0, tiled=True
            )
            gathered = returned[own_target, own_slots]
            coupling_term = jnp.dot(
                couplings[tree_level].T, gathered, preferred_element_type=jnp.float32
            )
            residual = (
                solved.astype(jnp.float32)
                - lax.psum(coupling_term.astype(jnp.bfloat16), "row").astype(jnp.float32)
            ).astype(jnp.bfloat16)
        contribution = jnp.dot(inverses[tree_level].T, residual, preferred_element_type=jnp.float32)
        if tree_level == 0:
            summed = lax.psum(contribution.astype(jnp.bfloat16), "col")
            solution = summed
            rhs_width = solution.shape[1] // groups[0]
            solutions[0] = lax.dynamic_slice_in_dim(
                solution, column % groups[0] * rhs_width, rhs_width, 1
            )
        else:
            portion = shrink(
                contribution, group_bits[tree_level], pass_solution_sum, column
            ).astype(jnp.bfloat16)
            solutions[tree_level] = portion
            if tree_level < 3:
                solution = spread(portion, group_bits[tree_level], pass_solution_spread, column)
        parent_solution = solution
        parent_gathered = gathered
    return (solutions[0], solutions[1], solutions[2], solutions[3])


MESH = pl.DeviceIdType.MESH
VMEM_LIMIT = 32 * 2**20


def dot_nn(left, right):
    return lax.dot_general(left, right, (((1,), (0,)), ((), ())), preferred_element_type=jnp.float32)


def dot_nt(left, right):
    return lax.dot_general(left, right, (((1,), (1,)), ((), ())), preferred_element_type=jnp.float32)


def eye(size):
    rows = lax.broadcasted_iota(jnp.int32, (size, size), 0)
    columns = lax.broadcasted_iota(jnp.int32, (size, size), 1)
    return jnp.where(rows == columns, 1.0, 0.0).astype(jnp.bfloat16)


def flipped(value, mask):
    result = value
    bit = 1
    while bit <= mask:
        if mask & bit:
            result = result + bit * (1 - 2 * ((value // bit) % 2))
        bit *= 2
    return result


class Plan:
    def __init__(self, rows, cols, inverse_shapes, rhs_top_shape, map_shape):
        self.rows, self.cols = rows, cols
        self.strip = [shape[1] for shape in inverse_shapes]
        self.order = [shape[1] * rows for shape in inverse_shapes]
        self.local = [shape[0] for shape in inverse_shapes]
        self.group = [cols >> level for level in range(4)]
        self.columns = rhs_top_shape[1] * cols
        self.width = [self.columns // group if group else 0 for group in self.group]
        self.mine = self.columns // rows
        self.map_shape = map_shape

    def total(self, level):
        return self.order[level] * (2 if level else 1)

    def span_rows(self):
        n, order, width = self.mine, self.order, self.width
        shared = 3 * (n // 4) * order[1] + 3 * (n // 2) * order[0] + n // 2 * order[1]
        inner = 2 * n * order[3] + 4 * n * order[2] + 8 * (n // 4) * order[1]
        return max(shared, inner, 3 * width[0] * order[0], 3 * n * order[2]) // 128

    def fits(self):
        table = sum(
            2 * self.total(level) * self.order[level + 1] * 2 for level in range(3)
        )
        if self.rows != 4 or self.group[3] != 1 or self.mine * self.rows != self.columns or table > 24 * 2**20:
            return False
        if self.group != [8, 4, 2, 1] or self.mine % 64:
            return False
        for level in range(4):
            if self.strip[level] % 64 or self.order[level] % 128 or self.local[level] % 64:
                return False
        if not packed((self.mine, self.strip[1])):
            return False
        return narrow(self.strip[3]) and not any(narrow(strip) for strip in self.strip[:3])


def elements(shape):
    count = 1
    for extent in shape:
        count *= extent
    return count


def packed(shape):
    return shape[1] > 128 and shape[1] % 128 == 64


def packed_shape(shape):
    return (shape[0] * (shape[1] // 128) + shape[0] // 2, 128)


def narrow(size):
    return size < 128


def phase(number):
    return jax.named_scope(str(number))


def build_kernel(plan):
    R, CC, N = plan.rows, plan.cols, plan.mine
    S, K, L, G, W = plan.order, plan.strip, plan.local, plan.group, plan.width
    N2, NH, NQ, chips = 2 * N, N // 2, N // G[1], G[0] // 2
    bf = jnp.bfloat16
    scratch = []

    def ref(shape, dtype=bf):
        scratch.append(pltpu.VMEM(shape, dtype))
        return len(scratch) - 1

    def sems(*shape):
        scratch.append(pltpu.SemaphoreType.DMA(shape) if shape else pltpu.SemaphoreType.DMA)
        return len(scratch) - 1

    levels, lower = range(4), (1, 2, 3)
    z_shape = [(S[3], L[3]) if l == 3 else (L[l], S[l]) for l in levels]
    c_shape = [None] + [(S[l], L[l]) for l in lower]
    Z = [ref(z_shape[l]) for l in levels]
    C = [None] + [ref(c_shape[l]) for l in lower]
    Zm = [ref(z_shape[l]) for l in levels]
    Cm = [None] + [ref(c_shape[l]) for l in lower]
    Zp = [ref((R,) + packed_shape((L[l], K[l]))) if l < 3 and packed((L[l], K[l])) else None for l in levels]
    Cp = [None] + [ref((R,) + packed_shape((K[l], L[l]))) if packed((K[l], L[l])) else None for l in lower]
    Zraw = [ref((L[l], K[l])) if Zp[l] is not None else None for l in levels]
    Craw = [None] + [ref((K[l], L[l])) if Cp[l] is not None else None for l in lower]
    Zr, Zs = [sems(R) for _ in levels], [sems() for _ in levels]
    Cr, Cs = [None] + [sems(R) for _ in lower], [None] + [sems() for _ in lower]
    Zmr, Zms = [sems() for _ in levels], [sems() for _ in levels]
    Cmr, Cms = [None] + [sems() for _ in lower], [None] + [sems() for _ in lower]
    table = [ref((2, plan.total(l), S[l + 1])) for l in range(3)]
    held_map = [None] + [ref(plan.map_shape[l - 1], jnp.int32) for l in lower]
    local = sems(6)
    B = [ref((NH, S[0])), ref((2, R) + packed_shape((N, K[1]))), ref((S[2], N2)), ref((S[3], N2))]
    B1, rhs_raw, rhs_packed = ref((N2, S[1])), ref((N, K[1])), ref(packed_shape((N, K[1])))
    Bs, Br = [sems() for _ in levels], [sems() for _ in levels]
    Ds, Dr = [sems(), sems(G[1]), sems()], [sems(), sems(2), sems()]
    y = [None] + [ref((4, NH, L[l])) for l in lower]
    yb = [None] + [ref((2, NH, L[l])) for l in lower]
    ys, yr = [None] + [sems() for _ in lower], [None] + [sems() for _ in lower]
    u = [None, ref((2, G[1], NQ, S[1])), ref((2, 2, G[1], NQ, S[2])), ref((2, N2, S[3]))]
    ur = [None] + [sems() for _ in lower]
    up1, ut1, ut1r = ref((2, G[1], NQ, S[1])), ref((G[1] + 1, NQ, S[1])), sems()
    h1 = ref((2, NQ, S[1]))
    folded, early1 = ref((2, L[1], S[2])), ref((N2, L[1]), jnp.float32)
    up2, ut2, ut2r = ref((2, N, S[2])), ref((N, S[2])), sems()
    xp0, xr0, xr0r = ref((NH, S[0])), ref((chips, NH, S[0])), sems()
    x0 = ref((NH, S[0]))
    xp1, xr1, xr1r = ref((NH, S[1])), ref((NH, S[1])), sems()
    v = [None] + [ref((NH, S[l])) for l in (1, 2)]
    x1, x2 = ref((NH, S[1])), ref((NH, S[2]))
    f1, f3 = ref((R, NH, K[1])), ref((2 * R, NH, K[3]))
    Os, Or = [sems() for _ in levels], [sems() for _ in levels]
    plane, inner, beside = sems(), sems(), sems()
    span = ref((plan.span_rows(), 128))

    def kernel(*refs):
        inverse = refs[0:4]
        coupling = (None,) + tuple(refs[4:7])
        rhs = refs[7:11]
        maps = (None,) + tuple(refs[11:14])
        outs = refs[14:18]
        held = refs[18:]
        at = lambda index: held[index]
        z = lax.axis_index("row")
        c = lax.axis_index("col")
        core, chip = c % 2, c // 2
        middle = jnp.logical_and(z > 0, z < R - 1)
        border = jnp.logical_not(middle)
        half = z % 2
        pair = z + 1 - 2 * half
        across = R - 1 - z
        beyond = R - 1 - pair
        sent = {}

        def remote(src, dst, ssem, rsem, z_to, c_to):
            return pltpu.make_async_remote_copy(
                src_ref=src, dst_ref=dst, send_sem=ssem, recv_sem=rsem,
                device_id=(z_to, c_to), device_id_type=MESH,
            )

        def push(src, dst, ssem, rsem, z_to, c_to):
            remote(src, dst, ssem, rsem, z_to, c_to).start()

        def counted(src, dst, index, rsem, z_to, c_to):
            push(src, dst, at(index), rsem, z_to, c_to)
            sent[index] = sent.get(index, 0) + elements(src.shape)

        def arrived(dst, rsem):
            pltpu.make_async_copy(dst, dst, rsem).wait()

        def take(sem, count):
            view = at(span).at[pl.ds(0, count // 128)]
            pltpu.make_async_copy(view, view, sem).wait()

        barrier = pltpu.get_barrier_semaphore()
        friends = [(z, flipped(c, m)) for m in range(1, CC)]
        for d in range(1, R):
            friends += [((z + d) % R, c), ((z + d) % R, flipped(c, 1))]
        friends += [(pair, flipped(c, m)) for m in range(2, G[1])]
        for friend in friends:
            pl.semaphore_signal(barrier, inc=1, device_id=friend, device_id_type=MESH)

        raws = [(rhs[1], at(rhs_raw))]
        for l in levels:
            if Zp[l] is not None:
                raws.append((inverse[l], at(Zraw[l])))
            if l and Cp[l] is not None:
                raws.append((coupling[l], at(Craw[l])))
        loads = raws + [(maps[l], at(held_map[l])) for l in lower]
        for i, (src, dst) in enumerate(loads):
            pltpu.make_async_copy(src, dst, at(local).at[i]).start()

        def slot(kind, l, r):
            if kind == 0:
                if Zp[l] is not None:
                    return at(Zp[l]).at[r], at(Zr[l]).at[r]
                if l == 3:
                    low = pl.multiple_of(r * K[l], 16)
                    return at(Z[l]).at[pl.ds(low, K[l])], at(Zr[l]).at[r]
                low = pl.multiple_of(r * K[l], 128)
                return at(Z[l]).at[:, pl.ds(low, K[l])], at(Zr[l]).at[r]
            if Cp[l] is not None:
                return at(Cp[l]).at[r], at(Cr[l]).at[r]
            low = pl.multiple_of(r * K[l], 16)
            return at(C[l]).at[pl.ds(low, K[l])], at(Cr[l]).at[r]

        def is_packed(kind, l):
            return (Zp, Cp)[kind][l] is not None

        def source(kind, l):
            if is_packed(kind, l):
                return slot(kind, l, z)[0]
            return (inverse, coupling)[kind][l]

        def send_sem(kind, l):
            return at((Zs, Cs)[kind][l])

        def own_load(kind, l):
            if not is_packed(kind, l):
                dst, sem = slot(kind, l, z)
                pltpu.make_async_copy(source(kind, l), dst, sem).start()

        def own_send(kind, l):
            dst, sem = slot(kind, l, z)
            push(source(kind, l), dst, send_sem(kind, l), sem, jnp.where(middle, across, pair), c)

            @pl.when(border)
            def _():
                push(source(kind, l), dst, send_sem(kind, l), sem, beyond, c)

        def own_out(kind, l):
            dst, sem = slot(kind, l, z)
            push(source(kind, l), dst, send_sem(kind, l), sem, pair, c)

        def pass_on(kind, l):
            for r in (across, beyond):
                dst, sem = slot(kind, l, r)
                push(dst, dst, send_sem(kind, l), sem, pair, c)

        def settle(kind, l, which):
            for r in which:
                arrived(*slot(kind, l, r))

        def settle_all(kind, l):
            settle(kind, l, (pair, across, beyond) if is_packed(kind, l) else (z, pair, across, beyond))
            if is_packed(kind, l):
                unpack(kind, l)

        def unpacked(block, rows, lanes):
            whole = lanes // 128 * rows
            rest = block[whole:]
            rest = jnp.concatenate([rest[:, :lanes % 128], rest[:, lanes % 128:]], axis=0)
            return jnp.concatenate([block[i:i + rows] for i in range(0, whole, rows)] + [rest], axis=1)

        def unpack(kind, l):
            rows, lanes = (L[l], K[l]) if kind == 0 else (K[l], L[l])
            for r in range(R):
                value = unpacked(at((Zp, Cp)[kind][l])[r], rows, lanes)
                if kind == 0:
                    at(Z[l])[:, r * lanes:(r + 1) * lanes] = value
                else:
                    at(C[l])[r * rows:(r + 1) * rows, :] = value

        def pack(raw):
            value = raw[...]
            rows, lanes = value.shape
            whole = lanes - lanes % 128
            pieces = [value[:, i:i + 128] for i in range(0, whole, 128)]
            rest = value[:, whole:]
            rest = jnp.concatenate([rest[:rows // 2], rest[rows // 2:]], axis=1)
            return jnp.concatenate(pieces + [rest], axis=0)

        def drain(kind, l):
            if is_packed(kind, l):
                whole = at((Zp, Cp)[kind][l])
                part = whole.at[pl.ds(0, R // 2)]
            else:
                whole = at((Z, C)[kind][l])
                if kind == 0 and l < 3:
                    part = whole.at[:, pl.ds(0, S[l] // 2)]
                else:
                    part = whole.at[pl.ds(0, S[l] // 2)]

            @pl.when(middle)
            def _():
                arrived(whole, send_sem(kind, l))

            @pl.when(border)
            def _():
                arrived(part, send_sem(kind, l))

        def rhs_pieces(l):
            q = c % G[l]
            if l == 3:
                return [
                    (rhs[3].at[:, pl.ds(i * N2, N2)], at(B[3]).at[pl.ds(pl.multiple_of(z * K[3], 16), K[3])], 1 + i)
                    for i in range(2)
                ]
            if l == 2:
                return [(rhs[2], at(B[2]).at[pl.ds(pl.multiple_of(z * K[2], 16), K[2])], 1 + q)]
            if l == 1:
                return [(at(rhs_packed), at(B[1]).at[q % 2, z], 1 + q // 2)]
            lanes = pl.ds(pl.multiple_of(z * K[0], 128), K[0])
            return [(rhs[0], at(B[0]).at[:, lanes], q // 2)]

        def start_rhs(l):
            for src, dst, z_to in rhs_pieces(l):
                @pl.when(z_to == z)
                def _():
                    pltpu.make_async_copy(src, dst, at(Br[l])).start()

                @pl.when(z_to != z)
                def _():
                    push(src, dst, at(Bs[l]), at(Br[l]), z_to, c)

        def drain_rhs(l):
            pieces = rhs_pieces(l)
            if l == 3:
                @pl.when(middle)
                def _():
                    arrived(at(B[3]).at[pl.ds(0, K[3])], at(Bs[3]))

                @pl.when(border)
                def _():
                    arrived(at(B[3]).at[pl.ds(0, 2 * K[3])], at(Bs[3]))
                return
            src, dst, z_to = pieces[0]

            @pl.when(z_to != z)
            def _():
                arrived(dst, at(Bs[l]))

        def rhs_spread(l):
            q = c % G[l]
            if l == 2:
                return z == 1 + q, at(B[2]), at(Dr[2])
            if l == 1:
                return z == 1 + q // 2, at(B[1]).at[q % 2], at(Dr[1]).at[q % 2]
            return z == q // 2, at(B[0]), at(Dr[0])

        def spread_rhs(l):
            holds, here, rsem = rhs_spread(l)

            @pl.when(holds)
            def _():
                arrived(here, at(Br[l]))
                for m in range(2, CC, 2) if l == 0 else range(1, G[l]):
                    ssem = at(Ds[l]).at[m] if l == 1 else at(Ds[l])
                    push(here, here, ssem, rsem, z, flipped(c, m))

        def drain_spread(l):
            holds, here, _ = rhs_spread(l)

            @pl.when(holds)
            def _():
                if l == 1:
                    for m in range(1, G[l]):
                        arrived(here, at(Ds[l]).at[m])
                else:
                    take(at(Ds[l]), (1 if l else chips - 1) * elements(here.shape))

        def wait_rhs(l):
            holds, here, rsem = rhs_spread(l)
            if l != 1:
                @pl.when(jnp.logical_not(holds))
                def _():
                    arrived(here, rsem)
                return
            for part in range(2):
                @pl.when(jnp.logical_not(jnp.logical_and(holds, c % 2 == part)))
                def _():
                    arrived(at(B[1]).at[part], at(Dr[1]).at[part])

        def make_table(l):
            front = c // G[l]
            step = K[l]
            for child in range(2):
                row = at(held_map[l + 1])[pl.ds(2 * front + child, 1), :]

                def body(i, carry):
                    start = pl.multiple_of(i * step, 16)
                    at_row = lax.broadcasted_iota(jnp.int32, (step, S[l + 1]), 0) + start
                    at(table[l])[child, pl.ds(start, step), :] = jnp.where(
                        at_row == row, 1.0, 0.0
                    ).astype(bf)
                    return carry

                lax.fori_loop(0, plan.total(l) // step, body, 0)

        def gathered(l, low, size, first, second):
            value = dot_nt(first, at(table[l])[0, low:low + size, :])
            return value + dot_nt(second, at(table[l])[1, low:low + size, :])

        def forward(kind, l):
            own, copy = at((Z, C)[kind][l]), at((Zm, Cm)[kind][l])
            push(
                own, copy, at((Zms, Cms)[kind][l]), at((Zmr, Cmr)[kind][l]), z, flipped(c, 1)
            )

        with phase(2):
            pl.semaphore_wait(barrier, len(friends))

        with phase(3):
            own_send(0, 3)
            start_rhs(3)
            own_send(1, 3)
            pltpu.make_async_copy(*loads[0], at(local).at[0]).wait()
            at(rhs_packed)[...] = pack(at(rhs_raw))
            start_rhs(2)
            start_rhs(1)
            own_send(0, 2)
            own_send(1, 2)
            for i, (src, dst) in enumerate(loads[1:]):
                pltpu.make_async_copy(src, dst, at(local).at[i + 1]).wait()
            for l in levels:
                if Zp[l] is not None:
                    at(Zp[l])[z] = pack(at(Zraw[l]))
                if l and Cp[l] is not None:
                    at(Cp[l])[z] = pack(at(Craw[l]))
            own_send(0, 1)
            own_send(1, 1)
            start_rhs(0)
            own_send(0, 0)
            for l in levels:
                own_load(0, l)
                if l:
                    own_load(1, l)

            @pl.when(middle)
            def _():
                own_out(0, 0)
                for l in (3, 2, 1):
                    own_out(0, l)
                    own_out(1, l)
        make_table(2)

        @pl.when(middle)
        def _():
            with phase(31):
                arrived(at(B[3]), at(Br[3]))
                right = dot_nt(eye(N2), at(B[3])[...]).astype(bf)
                settle_all(0, 3)
            with phase(32):
                solved = dot_nn(right, at(Z[3])[...]).astype(bf)
                at(y[3])[...] = solved.reshape(4, NH, L[3])
                settle_all(1, 3)
            with phase(33):
                at(u[3])[core] = (-dot_nt(solved, at(C[3])[...])).astype(bf)
                here = at(u[3]).at[core]
                counted(here, here, inner, at(ur[3]), z, flipped(c, 1))
                pass_on(0, 3)
                pass_on(1, 3)
        spread_rhs(2)
        spread_rhs(1)
        make_table(1)

        @pl.when(middle)
        def _():
            with phase(21):
                arrived(at(u[3]).at[0], at(ur[3]))
                wait_rhs(2)
            with phase(22):
                pair_of = at(u[3])[0], at(u[3])[1]
                right = dot_nt(eye(N2), at(B[2])[...]) + gathered(2, 0, S[2], *pair_of)
                right = right.astype(bf)
                lower_part = pl.ds(pl.multiple_of(core * N, N), N)
                pair_of = at(u[3])[0, lower_part, :], at(u[3])[1, lower_part, :]
                kept = gathered(2, S[2], S[2], *pair_of)
            with phase(23):
                settle_all(0, 2)
                pass_on(0, 2)
            with phase(24):
                solved = dot_nt(right, at(Z[2])[...]).astype(bf)
                at(y[2])[...] = solved.reshape(4, NH, L[2])
            with phase(25):
                settle_all(1, 2)
                pass_on(1, 2)
            with phase(26):
                at(up2)[...] = dot_nt(solved, at(C[2])[...]).astype(bf).reshape(2, N, S[2])
                counted(at(up2).at[1 - core], at(ut2), inner, at(ut2r), z, flipped(c, 1))
            with phase(27):
                own = at(up2)[core].astype(jnp.float32)
                arrived(at(ut2), at(ut2r))
                own = kept - (own + at(ut2)[...].astype(jnp.float32))
                child = (c // G[2]) % 2
                at(u[2])[child, core] = own.astype(bf).reshape(G[1], NQ, S[2])
                here = at(u[2]).at[child, core]
                for m in range(1, G[1]):
                    counted(here, here, inner, at(ur[2]), z, flipped(c, m))
        make_table(0)
        q, child = c % G[1], (c // G[1]) % 2

        @pl.when(middle)
        def _():
            with phase(11):
                wait_rhs(1)
                for part in range(2):
                    for r in range(R):
                        value = unpacked(at(B[1])[part, r], N, K[1])
                        at(B1)[part * N:(part + 1) * N, r * K[1]:(r + 1) * K[1]] = value
            with phase(14):
                settle_all(0, 1)
            with phase(10):
                at(early1)[...] = dot_nt(at(B1)[...], at(Z[1])[...])
                for i in range(2):
                    at(folded)[i] = dot_nn(at(Z[1])[...], at(table[1])[i, :S[1], :]).astype(bf)
            with phase(12):
                take(at(ur[2]), 3 * N * S[2])
            with phase(13):
                pair_of = [at(u[2])[i].reshape(N2, S[2]) for i in range(2)]
                solved = at(early1)[...]
                for i in range(2):
                    solved = solved + dot_nt(pair_of[i], at(folded)[i])
                solved = solved.astype(bf)
                at(y[1])[...] = solved.reshape(4, NH, L[1])
            with phase(16):
                settle_all(1, 1)
            with phase(17):
                coupled = dot_nt(solved, at(C[1])[...])
                at(up1)[...] = coupled.astype(bf).reshape(2, G[1], NQ, S[1])
                for m in range(G[1]):
                    src = at(up1).at[1 - half, flipped(q, m)]
                    counted(src, at(ut1).at[m], inner, at(ut1r), pair, flipped(c, m))
                for m in range(1, G[1]):
                    src = at(up1).at[half, flipped(q, m)]
                    counted(src, at(ut1).at[m], inner, at(ut1r), z, flipped(c, m))
                pair_of = [at(u[2])[i, :, q].reshape(2 * NQ, S[2]) for i in range(2)]
                kept = gathered(1, S[1], S[1], *pair_of)
                at(h1)[...] = kept.astype(bf).reshape(2, NQ, S[1])
                counted(at(h1).at[1 - half], at(ut1).at[G[1]], inner, at(ut1r), pair, c)
                spread_rhs(0)
                settle(0, 0, (z, pair, across, beyond))
                pass_on(0, 0)
                pass_on(0, 1)
                pass_on(1, 1)
                forward(0, 0)

        @pl.when(border)
        def _():
            with phase(18):
                for l in (3, 2):
                    for kind in range(2):
                        settle_all(kind, l)
                        forward(kind, l)
                spread_rhs(0)
                arrived(at(ut1), at(ut1r))
                value = at(ut1)[0].astype(jnp.float32)
                for m in range(1, G[1]):
                    value = value + at(ut1)[m].astype(jnp.float32)
                at(u[1])[child, q] = (at(ut1)[G[1]].astype(jnp.float32) - value).astype(bf)

        @pl.when(middle)
        def _():
            with phase(19):
                value = at(up1)[half, q].astype(jnp.float32)
                arrived(at(ut1).at[pl.ds(1, G[1] - 1)], at(ut1r))
                for m in range(1, G[1]):
                    value = value + at(ut1)[m].astype(jnp.float32)
                at(u[1])[child, q] = (at(h1)[half].astype(jnp.float32) - value).astype(bf)
        here = at(u[1]).at[child, q]
        kept_here = q // 2 == core
        for m in range(2, CC, 2):
            counted(here, here, plane, at(ur[1]), z, flipped(2 * chip + q // 2, m))

        @pl.when(jnp.logical_not(kept_here))
        def _():
            push(here, here, at(beside), at(ur[1]), z, flipped(c, 1))

        @pl.when(border)
        def _():
            with phase(40):
                settle(0, 0, (z, pair, across, beyond))
                forward(0, 0)

        @pl.when(middle)
        def _():
            with phase(20):
                for l in lower:
                    at(yb[l])[0] = at(y[l])[2 * half + core]
                    src = at(y[l]).at[2 * half + 1 - core]
                    push(src, at(yb[l]).at[1], at(ys[l]), at(yr[l]), z, flipped(c, 1))
                    src = at(y[l]).at[2 * (1 - half) + core]
                    push(src, at(yb[l]).at[0], at(ys[l]), at(yr[l]), pair, c)
                    src = at(y[l]).at[2 * (1 - half) + 1 - core]
                    push(src, at(yb[l]).at[1], at(ys[l]), at(yr[l]), pair, flipped(c, 1))
                for l in lower:
                    for kind in range(2):
                        forward(kind, l)
        with phase(41):
            @pl.when(kept_here)
            def _():
                take(at(ur[1]), 3 * NQ * S[1])

            @pl.when(jnp.logical_not(kept_here))
            def _():
                take(at(ur[1]), 4 * NQ * S[1])
            wait_rhs(0)
        with phase(42):
            columns = pl.ds(pl.multiple_of(2 * core, 2), 2)
            pair_of = [at(u[1])[i, columns].reshape(NH, S[1]) for i in range(2)]
            right = at(B[0])[...].astype(jnp.float32) + gathered(0, 0, S[0], *pair_of)
            right = right.astype(bf)
        with phase(43):
            arrived(at(Zm[0]), at(Zmr[0]))
        with phase(44):
            value = 0.0
            for blocks in (Z, Zm):
                solved = dot_nt(right, at(blocks[0])[...]).astype(bf)
                value = value + dot_nn(solved, at(blocks[0])[...])
            value = value.astype(bf)
            at(xp0)[...] = value
            for m in (3, 1, 2):
                counted(at(xp0), at(xr0).at[m], plane, at(xr0r), z, flipped(c, 2 * m))

        @pl.when(border)
        def _():
            with phase(45):
                settle_all(0, 1)
                forward(0, 1)

        @pl.when(border)
        def _():
            with phase(48):
                settle_all(1, 1)
                forward(1, 1)
        with phase(46):
            arrived(at(xr0).at[pl.ds(1, chips - 1)], at(xr0r))
        with phase(47):
            value = at(xp0)[...].astype(jnp.float32)
            for m in range(1, chips):
                value = value + at(xr0)[m].astype(jnp.float32)
            value = value.astype(bf)
            at(x0)[...] = value

        def leave(l, piece, dst, c_to):
            @pl.when(c_to == c)
            def _():
                pltpu.make_async_copy(piece(z), dst, at(Or[l])).start()

            @pl.when(c_to != c)
            def _():
                push(piece(z), dst, at(Os[l]), at(Or[l]), z, c_to)
            for d in (2, 1, 3):
                r = (z + d) % R
                push(piece(r), dst, at(Os[l]), at(Or[l]), r, c_to)

        top_here, one_here = chip == z, q // 2 == z // 2
        one_to, two_to = 2 * chip + z % 2, 2 * chip + z // 2

        def top_piece(r):
            return at(x0).at[:, pl.ds(pl.multiple_of(r * K[0], 128), K[0])]

        @pl.when(top_here)
        def _():
            leave(0, top_piece, outs[0], c)

        def placed(l, low):
            return outs[l].at[pl.ds(pl.multiple_of(low, 16), NH)]

        with phase(51):
            at(v[1])[...] = dot_nn(value, at(table[0])[child]).astype(bf)
            low = at(v[1])[...]

        def residual(l, index, coupled, low):
            return (at(yb[l])[index].astype(jnp.float32) - dot_nn(low, at(coupled[l])[...])).astype(bf)

        def wait_mate(l):
            @pl.when(middle)
            def _():
                arrived(at(yb[l]).at[1], at(yr[l]))

            @pl.when(border)
            def _():
                arrived(at(yb[l]), at(yr[l]))
            arrived(at(Zm[l]), at(Zmr[l]))
            arrived(at(Cm[l]), at(Cmr[l]))

        with phase(52):
            wait_mate(1)
        with phase(53):
            value = dot_nn(residual(1, 0, C, low), at(Z[1])[...])
            value = value + dot_nn(residual(1, 1, Cm, low), at(Zm[1])[...])
            at(xp1)[...] = value.astype(bf)
            counted(at(xp1), at(xr1), plane, at(xr1r), z, flipped(c, 2))
        side = chip % 2
        with phase(54):
            early = dot_nn(low, at(table[1])[side, S[1]:, :])
            arrived(at(xr1), at(xr1r))
        with phase(55):
            value = (at(xp1)[...].astype(jnp.float32) + at(xr1)[...].astype(jnp.float32)).astype(bf)
            at(v[2])[...] = (dot_nn(value, at(table[1])[side, :S[1], :]) + early).astype(bf)
            at(x1)[...] = value
            low = at(v[2])[...]
        with phase(56):
            wait_mate(2)
        with phase(57):
            value = dot_nn(residual(2, 0, C, low), at(Z[2])[...])
            value = value + dot_nn(residual(2, 1, Cm, low), at(Zm[2])[...])
            at(x2)[...] = value.astype(bf)
            high = at(x2)[...]
        with phase(58):
            @pl.when(one_here)
            def _():
                for r in range(R):
                    at(f1)[r] = at(x1)[:, r * K[1]:(r + 1) * K[1]]
                leave(1, lambda r: at(f1).at[r], placed(1, core * NH), one_to)

            def two_piece(r):
                return at(x2).at[:, pl.ds(pl.multiple_of(r * K[2], 128), K[2])]

            leave(2, two_piece, placed(2, half * N + core * NH), two_to)
        with phase(59):
            wait_mate(3)
        with phase(60):
            for mate in range(2):
                leaf = core if mate == 0 else 1 - core
                below = dot_nn(high, at(table[2])[leaf, :S[2], :])
                below = (below + dot_nn(low, at(table[2])[leaf, S[2]:, :])).astype(bf)
                left, right = ((C, Z), (Cm, Zm))[mate]
                value = dot_nt(residual(3, mate, left, below), at(right[3])[...]).astype(bf)
                for r in range(R):
                    at(f3)[mate * R + r] = value[:, r * K[3]:(r + 1) * K[3]]
                leave(
                    3, lambda r: at(f3).at[mate * R + r], placed(3, z * N + core * NH),
                    c if mate == 0 else flipped(c, 1),
                )
        with phase(61):
            for l in levels:
                drain(0, l)
                arrived(at(Zm[l]), at(Zms[l]))
                if l:
                    drain(1, l)
                    arrived(at(Cm[l]), at(Cms[l]))
                drain_rhs(l)
                if l < 3:
                    drain_spread(l)

            @pl.when(middle)
            def _():
                for l in lower:
                    arrived(at(y[l]).at[pl.ds(0, 3)], at(ys[l]))
                take(at(inner), sent[inner])
            take(at(plane), sent[plane])

            @pl.when(jnp.logical_not(kept_here))
            def _():
                arrived(at(u[1]).at[child, q], at(beside))

            @pl.when(top_here)
            def _():
                arrived(at(x0).at[:, pl.ds(0, S[0] - K[0])], at(Os[0]))

            @pl.when(jnp.logical_and(one_here, one_to == c))
            def _():
                arrived(at(f1).at[pl.ds(0, R - 1)], at(Os[1]))

            @pl.when(jnp.logical_and(one_here, one_to != c))
            def _():
                arrived(at(f1), at(Os[1]))

            @pl.when(two_to == c)
            def _():
                arrived(at(x2).at[:, pl.ds(0, S[2] - K[2])], at(Os[2]))

            @pl.when(two_to != c)
            def _():
                arrived(at(x2), at(Os[2]))
            arrived(at(f3).at[pl.ds(0, 2 * R - 1)], at(Os[3]))
        with phase(62):
            for l in levels:
                arrived(outs[l], at(Or[l]))

    return kernel, scratch


def hand_on(turned, *refs):
    arriving = refs[12]
    for i in range(4):
        pltpu.make_async_copy(refs[i], refs[8 + i], arriving.at[i]).start()
    for i, (turn, source, target) in enumerate(zip(turned, refs[8:12], refs[4:8])):
        pltpu.make_async_copy(refs[i], source, arriving.at[i]).wait()
        if turn:
            target[...] = dot_nt(eye(target.shape[0]), source[...]).astype(target.dtype)
        else:
            target[...] = source[...]


def fused_device(*blocks):
    plan = Plan(
        lax.axis_size("row"), lax.axis_size("col"),
        [block.shape for block in blocks[:4]], blocks[7].shape,
        [block.shape for block in blocks[11:14]],
    )
    if not plan.fits():
        return per_device(*blocks)
    kernel, scratch = build_kernel(plan)
    blocks = list(blocks)
    for at in (0, 1, 2, 3, 7, 8, 9, 10):
        if narrow(blocks[at].shape[1]):
            blocks[at] = blocks[at].T
    blocks = [pltpu.with_memory_space_constraint(block, pltpu.HBM) for block in blocks]
    vmem = pl.BlockSpec(memory_space=pltpu.VMEM)
    anywhere = pl.BlockSpec(memory_space=pltpu.HBM)
    solved = pl.pallas_call(
        kernel,
        out_shape=tuple(
            jax.ShapeDtypeStruct((width, strip), blocks[0].dtype)
            for width, strip in zip(plan.width, plan.strip)
        ),
        in_specs=[anywhere] * 14,
        out_specs=(pl.BlockSpec(memory_space=pl.ANY),) * 4,
        scratch_shapes=scratch,
        compiler_params=pltpu.CompilerParams(
            collective_id=0, has_side_effects=True, vmem_limit_bytes=VMEM_LIMIT
        ),
    )(*blocks)
    turned = [not narrow(width) for width in plan.width]
    solved = pl.pallas_call(
        functools.partial(hand_on, turned),
        out_shape=tuple(
            jax.ShapeDtypeStruct(block.shape[::-1] if turn else block.shape, block.dtype)
            for block, turn in zip(solved, turned)
        ),
        in_specs=[pl.BlockSpec(memory_space=pl.ANY)] * 4,
        out_specs=(vmem,) * 4,
        scratch_shapes=[pltpu.VMEM(block.shape, block.dtype) for block in solved]
        + [pltpu.SemaphoreType.DMA((4,))],
        compiler_params=pltpu.CompilerParams(vmem_limit_bytes=2**20),
    )(*solved)
    return tuple(block if turn else block.T for block, turn in zip(solved, turned))


def solution(mesh):
    in_specs = (
        P("col", "row"),
        P("col", "row"),
        P("col", "row"),
        P("col", "row"),
        P("row", "col"),
        P("row", "col"),
        P("row", "col"),
        P("row", "col"),
        P("row", "col"),
        P("row", "col"),
        P("row", "col"),
        P(),
        P(),
        P(),
    )
    out_specs = (P("row", "col"), P("row", "col"), P("row", "col"), P("row", "col"))
    return jax.shard_map(
        fused_device, mesh=mesh, in_specs=in_specs, out_specs=out_specs, check_vma=False
    )
```

```python
import functools

import jax
import jax.numpy as jnp
from jax import lax
from jax.experimental import pallas as pl
from jax.experimental.pallas import tpu as pltpu
from jax.sharding import PartitionSpec as P


def swapped(value, axis, stride):
    mask = 2**stride
    pairs = [(source, source ^ mask) for source in range(lax.axis_size(axis))]
    return lax.ppermute(value, axis, pairs)


def route_tables(mapping, child_index, parent_sep, parent_upd, strips, row_index):
    positions = lax.dynamic_index_in_dim(mapping, child_index, 0, keepdims=False)
    sep_rows = parent_sep // strips
    in_separator = positions < parent_sep
    if parent_upd > 0:
        upd_rows = parent_upd // strips
        target = jnp.where(
            in_separator, positions // sep_rows, (positions - parent_sep) // upd_rows
        )
        offset = jnp.where(
            in_separator, positions % sep_rows, sep_rows + (positions - parent_sep) % upd_rows
        )
    else:
        target = positions // sep_rows
        offset = positions % sep_rows
    block_rows = positions.shape[0] // strips
    blocks = target.reshape(strips, block_rows)
    matches = (blocks[:, :, None] == jnp.arange(strips, dtype=jnp.int32)[None, None, :]).astype(
        jnp.int32
    )
    slot_of = jnp.sum((jnp.cumsum(matches, axis=1) - 1) * matches, axis=2).reshape(-1)
    block_len = sep_rows + parent_upd // strips
    capacity = 2 * positions.shape[0] // (strips * strips)
    source = jnp.arange(positions.shape[0], dtype=jnp.int32) // block_rows
    mine_here = target == row_index
    column_at = jnp.where(mine_here, slot_of, capacity)
    lookup = jnp.full((strips, capacity + 1), block_len, jnp.int32)
    lookup = lookup.at[source, column_at].set(jnp.where(mine_here, offset, block_len))[:, :capacity]
    local_target = lax.dynamic_slice_in_dim(target, row_index * block_rows, block_rows)
    local_slots = lax.dynamic_slice_in_dim(slot_of, row_index * block_rows, block_rows)
    return (local_target, local_slots, lookup, capacity, block_len)


def pack_rows(values, local_target, local_slots, strips, capacity):
    buffer = jnp.zeros((strips, capacity, values.shape[1]), values.dtype)
    return buffer.at[local_target, local_slots].set(values)


def unpack_rows(received, lookup, block_len):
    summed = jnp.zeros((block_len + 1, received.shape[2]), jnp.float32)
    return summed.at[lookup].add(received.astype(jnp.float32))[:block_len]


def spread(portion, depth_bits, pass_on, column):
    for bit_index in range(depth_bits):
        partner = pass_on(portion, bit_index)
        is_upper = column >> bit_index & 1 == 1
        portion = jnp.where(
            is_upper,
            jnp.concatenate([partner, portion], axis=-1),
            jnp.concatenate([portion, partner], axis=-1),
        )
    return portion


def shrink(entire, depth_bits, pass_on, column):
    for bit_index in reversed(range(depth_bits)):
        half_width = entire.shape[-1] // 2
        low_part = entire[..., :half_width]
        high_part = entire[..., half_width:]
        is_upper = column >> bit_index & 1 == 1
        kept_part = jnp.where(is_upper, high_part, low_part)
        sent_part = jnp.where(is_upper, low_part, high_part)
        entire = kept_part + pass_on(sent_part, bit_index)
    return entire


def per_device(
    inverse_top,
    inverse_one,
    inverse_two,
    inverse_leaf,
    coupling_one,
    coupling_two,
    coupling_leaf,
    rhs_top,
    rhs_one,
    rhs_two,
    rhs_leaf,
    parent_map_one,
    parent_map_two,
    parent_map_leaf,
):
    strips = lax.axis_size("row")
    col_count = lax.axis_size("col")
    row_here = lax.axis_index("row")
    column = lax.axis_index("col")
    inverses = [inverse_top, inverse_one, inverse_two, inverse_leaf]
    couplings = [None, coupling_one, coupling_two, coupling_leaf]
    right_sides = [rhs_top, rhs_one, rhs_two, rhs_leaf]
    parent_maps = [None, parent_map_one, parent_map_two, parent_map_leaf]
    orders = [inverse.shape[1] * strips for inverse in inverses]
    groups = [col_count >> tree_level for tree_level in range(4)]
    group_bits = [group_size.bit_length() - 1 for group_size in groups]
    pass_rhs = lambda values, bit_index: swapped(values, "col", bit_index)
    pass_update_sum = lambda values, bit_index: swapped(
        values.astype(jnp.bfloat16), "col", bit_index
    ).astype(values.dtype)
    pass_update_spread = lambda values, bit_index: swapped(values, "col", bit_index)
    pass_solution_sum = lambda values, bit_index: swapped(
        values.astype(jnp.bfloat16), "col", bit_index
    ).astype(values.dtype)
    pass_solution_spread = lambda values, bit_index: swapped(values, "col", bit_index)
    full_rhs = [
        spread(right_sides[tree_level], group_bits[tree_level], pass_rhs, column)
        for tree_level in range(4)
    ]
    own_routes = [None]
    for tree_level in range(1, 4):
        parent_order = orders[tree_level - 1]
        parent_update = parent_order if tree_level > 1 else 0
        front_here = column // groups[tree_level]
        own_routes.append(
            route_tables(
                parent_maps[tree_level], front_here, parent_order, parent_update, strips, row_here
            )
        )
    pivots = [None] * 4
    incoming = None
    for tree_level in (3, 2, 1, 0):
        sep_rows = inverses[tree_level].shape[1]
        if incoming is None:
            separator = full_rhs[tree_level]
            own_update = None
        else:
            separator = (full_rhs[tree_level].astype(jnp.float32) + incoming[:sep_rows]).astype(
                jnp.bfloat16
            )
            own_update = lax.optimization_barrier(incoming[sep_rows:].astype(jnp.bfloat16))
        partial_value = jnp.dot(inverses[tree_level], separator, preferred_element_type=jnp.float32)
        solved = lax.psum(partial_value.astype(jnp.bfloat16), "row")
        pivots[tree_level] = solved
        if tree_level > 0:
            coupled = jnp.dot(couplings[tree_level], solved, preferred_element_type=jnp.float32)
            reduced = shrink(coupled, group_bits[tree_level], pass_update_sum, column)
            if own_update is None:
                portion = (-reduced).astype(jnp.bfloat16)
            else:
                start_at = column % groups[tree_level] * reduced.shape[1]
                kept_rows = lax.dynamic_slice_in_dim(own_update, start_at, reduced.shape[1], 1)
                portion = (kept_rows.astype(jnp.float32) - reduced).astype(jnp.bfloat16)
            updated = spread(portion, group_bits[tree_level], pass_update_spread, column)
            own_target, own_slots, own_lookup, capacity, block_len = own_routes[tree_level]
            got_own = lax.all_to_all(
                pack_rows(updated, own_target, own_slots, strips, capacity),
                "row",
                split_axis=0,
                concat_axis=0,
                tiled=True,
            )
            own_part = unpack_rows(got_own, own_lookup, block_len)
            partner = swapped(own_part.astype(jnp.bfloat16), "col", group_bits[tree_level])
            incoming = own_part + partner.astype(jnp.float32)
    solutions = [None] * 4
    parent_solution = None
    parent_gathered = None
    for tree_level in range(4):
        solved = pivots[tree_level]
        gathered = None
        if tree_level == 0:
            residual = solved
        else:
            own_target, own_slots, own_lookup, capacity, block_len = own_routes[tree_level]
            pieces = [parent_solution]
            if parent_gathered is not None:
                pieces.append(parent_gathered)
            pieces.append(jnp.zeros((1, parent_solution.shape[1]), jnp.bfloat16))
            parent_rows = jnp.concatenate(pieces, axis=0)
            returned = lax.all_to_all(
                parent_rows[own_lookup], "row", split_axis=0, concat_axis=0, tiled=True
            )
            gathered = returned[own_target, own_slots]
            coupling_term = jnp.dot(
                couplings[tree_level].T, gathered, preferred_element_type=jnp.float32
            )
            residual = (
                solved.astype(jnp.float32)
                - lax.psum(coupling_term.astype(jnp.bfloat16), "row").astype(jnp.float32)
            ).astype(jnp.bfloat16)
        contribution = jnp.dot(inverses[tree_level].T, residual, preferred_element_type=jnp.float32)
        if tree_level == 0:
            summed = lax.psum(contribution.astype(jnp.bfloat16), "col")
            solution = summed
            rhs_width = solution.shape[1] // groups[0]
            solutions[0] = lax.dynamic_slice_in_dim(
                solution, column % groups[0] * rhs_width, rhs_width, 1
            )
        else:
            portion = shrink(
                contribution, group_bits[tree_level], pass_solution_sum, column
            ).astype(jnp.bfloat16)
            solutions[tree_level] = portion
            if tree_level < 3:
                solution = spread(portion, group_bits[tree_level], pass_solution_spread, column)
        parent_solution = solution
        parent_gathered = gathered
    return (solutions[0], solutions[1], solutions[2], solutions[3])


MESH = pl.DeviceIdType.MESH
VMEM_LIMIT = 32 * 2**20


def dot_nn(left, right):
    return lax.dot_general(left, right, (((1,), (0,)), ((), ())), preferred_element_type=jnp.float32)


def dot_nt(left, right):
    return lax.dot_general(left, right, (((1,), (1,)), ((), ())), preferred_element_type=jnp.float32)


def eye(size):
    rows = lax.broadcasted_iota(jnp.int32, (size, size), 0)
    columns = lax.broadcasted_iota(jnp.int32, (size, size), 1)
    return jnp.where(rows == columns, 1.0, 0.0).astype(jnp.bfloat16)


def flipped(value, mask):
    result = value
    bit = 1
    while bit <= mask:
        if mask & bit:
            result = result + bit * (1 - 2 * ((value // bit) % 2))
        bit *= 2
    return result


class Plan:
    def __init__(self, rows, cols, inverse_shapes, rhs_top_shape, map_shape):
        self.rows, self.cols = rows, cols
        self.strip = [shape[1] for shape in inverse_shapes]
        self.order = [shape[1] * rows for shape in inverse_shapes]
        self.local = [shape[0] for shape in inverse_shapes]
        self.group = [cols >> level for level in range(4)]
        self.columns = rhs_top_shape[1] * cols
        self.width = [self.columns // group if group else 0 for group in self.group]
        self.mine = self.columns // rows
        self.map_shape = map_shape

    def total(self, level):
        return self.order[level] * (2 if level else 1)

    def result_shapes(self):
        shapes = list(zip(self.width, self.strip))
        return shapes[:3] + [(self.width[3] // 2, 2 * self.strip[3])]

    def span_rows(self):
        n, order, width = self.mine, self.order, self.width
        shared = 3 * (n // 4) * order[1] + 3 * (n // 2) * order[0] + n // 2 * order[1]
        inner = 2 * n * order[3] + 4 * n * order[2] + 8 * (n // 4) * order[1]
        joined = sum(2 * order[level] * self.local[level] for level in (2, 3))
        joined += sum(order[level] * self.local[level] for level in (0, 1))
        return max(shared, inner, joined, 9 * n * order[1], 3 * width[0] * order[0], 3 * n * order[2]) // 128

    def fits(self):
        table = sum(
            2 * self.total(level) * self.order[level + 1] * 2 for level in range(3)
        )
        if self.rows != 4 or self.group[3] != 1 or self.mine * self.rows != self.columns or table > 24 * 2**20:
            return False
        if self.group != [8, 4, 2, 1] or self.mine % 64:
            return False
        for level in range(4):
            if self.strip[level] % 64 or self.order[level] % 128 or self.local[level] % 64:
                return False
        if not packed((self.mine, self.strip[1])):
            return False
        return narrow(self.strip[3]) and not any(narrow(strip) for strip in self.strip[:3])


def elements(shape):
    count = 1
    for extent in shape:
        count *= extent
    return count


def packed(shape):
    return shape[1] > 128 and shape[1] % 128 == 64


def packed_shape(shape):
    return (shape[0] * (shape[1] // 128) + shape[0] // 2, 128)


def narrow(size):
    return size < 128


def phase(number):
    return jax.named_scope(str(number))


def build_kernel(plan):
    R, CC, N = plan.rows, plan.cols, plan.mine
    S, K, L, G, W = plan.order, plan.strip, plan.local, plan.group, plan.width
    N2, NH, NQ, chips = 2 * N, N // 2, N // G[1], G[0] // 2
    bf = jnp.bfloat16
    scratch = []

    def ref(shape, dtype=bf):
        scratch.append(pltpu.VMEM(shape, dtype))
        return len(scratch) - 1

    def sems(*shape):
        scratch.append(pltpu.SemaphoreType.DMA(shape) if shape else pltpu.SemaphoreType.DMA)
        return len(scratch) - 1

    levels, lower = range(4), (1, 2, 3)
    z_shape = [(S[3], L[3]) if l == 3 else (L[l], S[l]) for l in levels]
    c_shape = [None] + [(S[l], L[l]) for l in lower]
    Z = [ref(z_shape[l]) for l in levels]
    C = [None] + [ref(c_shape[l]) for l in lower]
    Zm = [ref(z_shape[l]) for l in levels]
    Cm = [None] + [ref(c_shape[l]) for l in lower]
    Zp = [ref((R,) + packed_shape((L[l], K[l]))) if l < 3 and packed((L[l], K[l])) else None for l in levels]
    Cp = [None] + [ref((R,) + packed_shape((K[l], L[l]))) if packed((K[l], L[l])) else None for l in lower]
    Zraw = [ref((L[l], K[l])) if Zp[l] is not None else None for l in levels]
    Craw = [None] + [ref((K[l], L[l])) if Cp[l] is not None else None for l in lower]
    Zr, Zs = [sems() for _ in levels], [sems() for _ in levels]
    Cr, Cs = [None] + [sems() for _ in lower], [None] + [sems() for _ in lower]
    Zmr, Cmr, mates, mates1 = [sems() for _ in levels], [None] + [sems() for _ in lower], sems(), sems()
    table = [ref((2, plan.total(l), S[l + 1])) for l in range(3)]
    held_map = [None] + [ref(plan.map_shape[l - 1], jnp.int32) for l in lower]
    local = sems(6)
    B = [ref((NH, S[0])), ref((2, R) + packed_shape((N, K[1]))), ref((S[2], N2)), ref((S[3], N2))]
    B1, rhs_raw, rhs_packed = ref((N2, S[1])), ref((N, K[1])), ref(packed_shape((N, K[1])))
    Bs, Br = [sems() for _ in levels], [sems() for _ in levels]
    Ds, Dr = [sems(), sems(), sems()], [sems(), sems(2), sems()]
    y = [None] + [ref((4, NH, L[l])) for l in lower]
    yb = [None] + [ref((2, NH, L[l])) for l in lower]
    ys, yr = [None] + [sems() for _ in lower], [None] + [sems() for _ in lower]
    u = [None, ref((2, G[1], NQ, S[1])), ref((2, 2, G[1], NQ, S[2])), ref((2, N2, S[3]))]
    ur, ur1 = [None, None, sems(), sems()], sems(2)
    f0 = ref((NH, S[0]), jnp.float32)
    up1, ut1, ut1r = ref((2, G[1], NQ, S[1])), ref((G[1], NQ, S[1])), sems()
    h1 = ref((2, NQ, S[1]))
    folded, early1 = ref((2, L[1], S[2])), ref((N2, L[1]), jnp.float32)
    up2, ut2, ut2r = ref((2, N, S[2])), ref((N, S[2])), sems()
    xp0, xr0, xr0r = ref((NH, S[0])), ref((chips, NH, S[0])), sems()
    x0 = ref((NH, S[0]))
    xp1, xr1, xr1r = ref((NH, S[1])), ref((NH, S[1])), sems()
    v = [None] + [ref((NH, S[l])) for l in (1, 2)]
    x1, x2 = ref((NH, S[1])), ref((NH, S[2]))
    f1, f3 = ref((R, NH, K[1])), ref((2 * R, NH // 2, 2 * K[3]))
    folded3 = ref((2, 2 * S[2], L[3]))
    Os, Or = [sems() for _ in levels], [sems() for _ in levels]
    plane, inner, beside = sems(), sems(), sems()
    scratch.append(pltpu.SemaphoreType.REGULAR)
    ready = len(scratch) - 1
    span = ref((plan.span_rows(), 128))

    def kernel(*refs):
        inverse = refs[0:4]
        coupling = (None,) + tuple(refs[4:7])
        rhs = refs[7:11]
        maps = (None,) + tuple(refs[11:14])
        outs = refs[14:18]
        held = refs[18:]
        at = lambda index: held[index]
        z = lax.axis_index("row")
        c = lax.axis_index("col")
        core, chip = c % 2, c // 2
        middle = jnp.logical_and(z > 0, z < R - 1)
        border = jnp.logical_not(middle)
        half = z % 2
        pair = z + 1 - 2 * half
        across = R - 1 - z
        beyond = R - 1 - pair
        sent = {}

        def remote(src, dst, ssem, rsem, z_to, c_to):
            return pltpu.make_async_remote_copy(
                src_ref=src, dst_ref=dst, send_sem=ssem, recv_sem=rsem,
                device_id=(z_to, c_to), device_id_type=MESH,
            )

        def push(src, dst, ssem, rsem, z_to, c_to):
            remote(src, dst, ssem, rsem, z_to, c_to).start()

        def counted(src, dst, index, rsem, z_to, c_to):
            push(src, dst, at(index), rsem, z_to, c_to)
            sent[index] = sent.get(index, 0) + elements(src.shape)

        def arrived(dst, rsem):
            pltpu.make_async_copy(dst, dst, rsem).wait()

        def take(sem, count):
            view = at(span).at[pl.ds(0, count // 128)]
            pltpu.make_async_copy(view, view, sem).wait()

        barrier = pltpu.get_barrier_semaphore()
        mates_here = [(z, flipped(c, m)) for m in range(1, CC)]

        def greet(semaphore, *friends):
            for friend in friends:
                pl.semaphore_signal(semaphore, inc=1, device_id=friend, device_id_type=MESH)

        greet(barrier, (pair, c))

        @pl.when(middle)
        def _():
            greet(barrier, (across, c), (beyond, c), *mates_here)

        raws = [(rhs[1], at(rhs_raw))]
        for l in levels:
            if Zp[l] is not None:
                raws.append((inverse[l], at(Zraw[l])))
            if l and Cp[l] is not None:
                raws.append((coupling[l], at(Craw[l])))
        loads = raws + [(maps[l], at(held_map[l])) for l in lower]
        for i, (src, dst) in enumerate(loads):
            pltpu.make_async_copy(src, dst, at(local).at[i]).start()

        def slot(kind, l, r):
            if kind == 0:
                if Zp[l] is not None:
                    return at(Zp[l]).at[r], at(Zr[l])
                if l == 3:
                    low = pl.multiple_of(r * K[l], 16)
                    return at(Z[l]).at[pl.ds(low, K[l])], at(Zr[l])
                low = pl.multiple_of(r * K[l], 128)
                return at(Z[l]).at[:, pl.ds(low, K[l])], at(Zr[l])
            if Cp[l] is not None:
                return at(Cp[l]).at[r], at(Cr[l])
            low = pl.multiple_of(r * K[l], 16)
            return at(C[l]).at[pl.ds(low, K[l])], at(Cr[l])

        def is_packed(kind, l):
            return (Zp, Cp)[kind][l] is not None

        def source(kind, l):
            if is_packed(kind, l):
                return slot(kind, l, z)[0]
            return (inverse, coupling)[kind][l]

        def send_sem(kind, l):
            return at((Zs, Cs)[kind][l])

        def own_load(kind, l):
            if not is_packed(kind, l):
                dst, sem = slot(kind, l, z)
                pltpu.make_async_copy(source(kind, l), dst, sem).start()

        def own_send(kind, l):
            dst, sem = slot(kind, l, z)
            push(source(kind, l), dst, send_sem(kind, l), sem, jnp.where(middle, across, pair), c)

            @pl.when(border)
            def _():
                push(source(kind, l), dst, send_sem(kind, l), sem, beyond, c)

        def own_out(kind, l):
            dst, sem = slot(kind, l, z)
            push(source(kind, l), dst, send_sem(kind, l), sem, pair, c)

        def pass_on(kind, l, origins=(across, beyond)):
            for r in origins:
                dst, sem = slot(kind, l, r)
                push(dst, dst, send_sem(kind, l), sem, pair, c)

        def settle_all(kind, l):
            rsem = slot(kind, l, z)[1]
            if is_packed(kind, l):
                arrived(at((Zp, Cp)[kind][l]).at[pl.ds(0, R - 1)], rsem)
                unpack(kind, l)
            else:
                arrived(at((Z, C)[kind][l]), rsem)

        def unpacked(block, rows, lanes):
            whole = lanes // 128 * rows
            rest = block[whole:]
            rest = jnp.concatenate([rest[:, :lanes % 128], rest[:, lanes % 128:]], axis=0)
            return jnp.concatenate([block[i:i + rows] for i in range(0, whole, rows)] + [rest], axis=1)

        def unpack(kind, l):
            rows, lanes = (L[l], K[l]) if kind == 0 else (K[l], L[l])
            for r in range(R):
                value = unpacked(at((Zp, Cp)[kind][l])[r], rows, lanes)
                if kind == 0:
                    at(Z[l])[:, r * lanes:(r + 1) * lanes] = value
                else:
                    at(C[l])[r * rows:(r + 1) * rows, :] = value

        def pack(raw):
            value = raw[...]
            rows, lanes = value.shape
            whole = lanes - lanes % 128
            pieces = [value[:, i:i + 128] for i in range(0, whole, 128)]
            rest = value[:, whole:]
            rest = jnp.concatenate([rest[:rows // 2], rest[rows // 2:]], axis=1)
            return jnp.concatenate(pieces + [rest], axis=0)

        def drain(kind, l):
            if is_packed(kind, l):
                whole = at((Zp, Cp)[kind][l])
                part = whole.at[pl.ds(0, R // 2)]
            else:
                whole = at((Z, C)[kind][l])
                if kind == 0 and l < 3:
                    part = whole.at[:, pl.ds(0, S[l] // 2)]
                else:
                    part = whole.at[pl.ds(0, S[l] // 2)]

            @pl.when(middle)
            def _():
                arrived(whole, send_sem(kind, l))

            @pl.when(border)
            def _():
                arrived(part, send_sem(kind, l))

        def rhs_pieces(l):
            q = c % G[l]
            if l == 3:
                return [
                    (rhs[3].at[:, pl.ds(i * N2, N2)], at(B[3]).at[pl.ds(pl.multiple_of(z * K[3], 16), K[3])], 1 + i)
                    for i in range(2)
                ]
            if l == 2:
                return [(rhs[2], at(B[2]).at[pl.ds(pl.multiple_of(z * K[2], 16), K[2])], 1 + q)]
            if l == 1:
                return [(at(rhs_packed), at(B[1]).at[q % 2, z], 1 + q // 2)]
            lanes = pl.ds(pl.multiple_of(z * K[0], 128), K[0])
            return [(rhs[0], at(B[0]).at[:, lanes], q // 2)]

        def start_rhs(l):
            for src, dst, z_to in rhs_pieces(l):
                @pl.when(z_to == z)
                def _():
                    pltpu.make_async_copy(src, dst, at(Br[l])).start()

                @pl.when(z_to != z)
                def _():
                    push(src, dst, at(Bs[l]), at(Br[l]), z_to, c)

        def drain_rhs(l):
            pieces = rhs_pieces(l)
            if l == 3:
                @pl.when(middle)
                def _():
                    arrived(at(B[3]).at[pl.ds(0, K[3])], at(Bs[3]))

                @pl.when(border)
                def _():
                    arrived(at(B[3]).at[pl.ds(0, 2 * K[3])], at(Bs[3]))
                return
            src, dst, z_to = pieces[0]

            @pl.when(z_to != z)
            def _():
                arrived(dst, at(Bs[l]))

        def rhs_spread(l):
            q = c % G[l]
            if l == 2:
                return z == 1 + q, at(B[2]), at(Dr[2])
            if l == 1:
                return z == 1 + q // 2, at(B[1]).at[q % 2], at(Dr[1]).at[q % 2]
            return z == q // 2, at(B[0]), at(Dr[0])

        def spread_rhs(l):
            holds, here, rsem = rhs_spread(l)

            @pl.when(holds)
            def _():
                arrived(here, at(Br[l]))
                for m in range(2, CC, 2) if l == 0 else range(1, G[l]):
                    push(here, here, at(Ds[l]), rsem, z, flipped(c, m))

        def drain_spread(l):
            holds, here, _ = rhs_spread(l)

            @pl.when(holds)
            def _():
                take(at(Ds[l]), (chips - 1, G[1] - 1, 1)[l] * elements(here.shape))

        def wait_rhs(l):
            holds, here, rsem = rhs_spread(l)
            if l != 1:
                @pl.when(jnp.logical_not(holds))
                def _():
                    arrived(here, rsem)
                return
            for part in range(2):
                @pl.when(jnp.logical_not(jnp.logical_and(holds, c % 2 == part)))
                def _():
                    arrived(at(B[1]).at[part], at(Dr[1]).at[part])

        def make_table(l):
            front = c // G[l]
            step = K[l]
            for child in range(2):
                row = at(held_map[l + 1])[pl.ds(2 * front + child, 1), :]

                def body(i, carry):
                    start = pl.multiple_of(i * step, 16)
                    at_row = lax.broadcasted_iota(jnp.int32, (step, S[l + 1]), 0) + start
                    at(table[l])[child, pl.ds(start, step), :] = jnp.where(
                        at_row == row, 1.0, 0.0
                    ).astype(bf)
                    return carry

                lax.fori_loop(0, plan.total(l) // step, body, 0)

        def gathered(l, low, size, first, second):
            value = dot_nt(first, at(table[l])[0, low:low + size, :])
            return value + dot_nt(second, at(table[l])[1, low:low + size, :])

        def forward(kind, l):
            own, copy = at((Z, C)[kind][l]), at((Zm, Cm)[kind][l])
            ssem = at(mates1 if own.shape[1] % 128 else mates)
            push(own, copy, ssem, at((Zmr, Cmr)[kind][l]), z, flipped(c, 1))

        def hand_over(l):
            at(yb[l])[0] = at(y[l])[2 * half + core]
            src = at(y[l]).at[2 * half + 1 - core]
            push(src, at(yb[l]).at[1], at(ys[l]), at(yr[l]), z, flipped(c, 1))
            src = at(y[l]).at[2 * (1 - half) + core]
            push(src, at(yb[l]).at[0], at(ys[l]), at(yr[l]), pair, c)
            src = at(y[l]).at[2 * (1 - half) + 1 - core]
            push(src, at(yb[l]).at[1], at(ys[l]), at(yr[l]), pair, flipped(c, 1))

        with phase(2):
            @pl.when(middle)
            def _():
                pl.semaphore_wait(barrier, CC + 1)

            @pl.when(border)
            def _():
                pl.semaphore_wait(barrier, 2)

        with phase(3):
            own_send(0, 3)
            start_rhs(3)
            own_send(1, 3)
            pltpu.make_async_copy(*loads[0], at(local).at[0]).wait()
            at(rhs_packed)[...] = pack(at(rhs_raw))
            start_rhs(2)
            start_rhs(1)
            own_send(0, 2)
            own_send(1, 2)
            for i, (src, dst) in enumerate(loads[1:]):
                pltpu.make_async_copy(src, dst, at(local).at[i + 1]).wait()
            for l in levels:
                if Zp[l] is not None:
                    at(Zp[l])[z] = pack(at(Zraw[l]))
                if l and Cp[l] is not None:
                    at(Cp[l])[z] = pack(at(Craw[l]))
            own_send(0, 1)
            own_send(1, 1)
            for l in levels:
                own_load(0, l)
                if l:
                    own_load(1, l)

            @pl.when(middle)
            def _():
                own_out(0, 0)
                for l in (3, 2, 1):
                    own_out(0, l)
                    own_out(1, l)
                greet(at(ready), *mates_here)
        make_table(2)

        @pl.when(middle)
        def _():
            with phase(31):
                arrived(at(B[3]), at(Br[3]))
                right = dot_nt(eye(N2), at(B[3])[...]).astype(bf)
                settle_all(0, 3)
                start_rhs(0)
                own_send(0, 0)
                pl.semaphore_wait(at(ready), CC - 1)
                greet(at(ready), (pair, c))
            with phase(32):
                solved = dot_nn(right, at(Z[3])[...]).astype(bf)
                at(y[3])[...] = solved.reshape(4, NH, L[3])
                settle_all(1, 3)
            with phase(33):
                at(u[3])[core] = (-dot_nt(solved, at(C[3])[...])).astype(bf)
                here = at(u[3]).at[core]
                counted(here, here, inner, at(ur[3]), z, flipped(c, 1))
                pass_on(0, 3)
                pass_on(1, 3)
        spread_rhs(2)
        spread_rhs(1)
        make_table(1)

        @pl.when(middle)
        def _():
            with phase(21):
                arrived(at(u[3]).at[0], at(ur[3]))
                wait_rhs(2)
            with phase(22):
                pair_of = at(u[3])[0], at(u[3])[1]
                right = dot_nt(eye(N2), at(B[2])[...]) + gathered(2, 0, S[2], *pair_of)
                right = right.astype(bf)
                lower_part = pl.ds(pl.multiple_of(core * N, N), N)
                pair_of = at(u[3])[0, lower_part, :], at(u[3])[1, lower_part, :]
                kept = gathered(2, S[2], S[2], *pair_of)
            with phase(23):
                settle_all(0, 2)
                pass_on(0, 2)
            with phase(24):
                solved = dot_nt(right, at(Z[2])[...]).astype(bf)
                at(y[2])[...] = solved.reshape(4, NH, L[2])
            with phase(25):
                settle_all(1, 2)
            with phase(26):
                at(up2)[...] = dot_nt(solved, at(C[2])[...]).astype(bf).reshape(2, N, S[2])
                counted(at(up2).at[1 - core], at(ut2), inner, at(ut2r), z, flipped(c, 1))
            with phase(27):
                own = at(up2)[core].astype(jnp.float32)
                arrived(at(ut2), at(ut2r))
                own = kept - (own + at(ut2)[...].astype(jnp.float32))
                child = (c // G[2]) % 2
                at(u[2])[child, core] = own.astype(bf).reshape(G[1], NQ, S[2])
                here = at(u[2]).at[child, core]
                for m in range(1, G[1]):
                    counted(here, here, inner, at(ur[2]), z, flipped(c, m))
        make_table(0)
        q, child = c % G[1], (c // G[1]) % 2

        @pl.when(middle)
        def _():
            with phase(11):
                wait_rhs(1)
                for part in range(2):
                    for r in range(R):
                        value = unpacked(at(B[1])[part, r], N, K[1])
                        at(B1)[part * N:(part + 1) * N, r * K[1]:(r + 1) * K[1]] = value
            with phase(14):
                settle_all(0, 1)
                pass_on(0, 1)
            with phase(10):
                at(early1)[...] = dot_nt(at(B1)[...], at(Z[1])[...])
                for i in range(2):
                    at(folded)[i] = dot_nn(at(Z[1])[...], at(table[1])[i, :S[1], :]).astype(bf)
            with phase(12):
                take(at(ur[2]), 3 * N * S[2])
            with phase(13):
                pair_of = [at(u[2])[i].reshape(N2, S[2]) for i in range(2)]
                solved = at(early1)[...]
                for i in range(2):
                    solved = solved + dot_nt(pair_of[i], at(folded)[i])
                solved = solved.astype(bf)
                at(y[1])[...] = solved.reshape(4, NH, L[1])
            with phase(16):
                settle_all(1, 1)
            with phase(17):
                coupled = dot_nt(solved, at(C[1])[...])
                at(up1)[...] = coupled.astype(bf).reshape(2, G[1], NQ, S[1])
                for m in range(1, G[1]):
                    src = at(up1).at[1 - half, flipped(q, m)]
                    counted(src, at(ut1).at[m], inner, at(ut1r), pair, flipped(c, m))
                for m in range(1, G[1]):
                    src = at(up1).at[half, flipped(q, m)]
                    counted(src, at(ut1).at[m], inner, at(ut1r), z, flipped(c, m))
                pair_of = [at(u[2])[i, :, q].reshape(2 * NQ, S[2]) for i in range(2)]
                kept = gathered(1, S[1], S[1], *pair_of)
                at(h1)[...] = kept.astype(bf).reshape(2, NQ, S[1])
                at(up1)[1 - half, q] = (
                    at(up1)[1 - half, q].astype(jnp.float32) - at(h1)[1 - half].astype(jnp.float32)
                ).astype(bf)
                counted(at(up1).at[1 - half, q], at(ut1).at[0], inner, at(ut1r), pair, c)
                spread_rhs(0)
                settle_all(0, 0)
                pass_on(0, 0)
                pass_on(1, 1)
                hand_over(1)
                pass_on(1, 2)
                hand_over(2)
                hand_over(3)
                forward(0, 0)

        @pl.when(border)
        def _():
            with phase(18):
                pl.semaphore_wait(at(ready), 1)
                for kind, l in ((0, 3), (1, 3), (0, 2)):
                    settle_all(kind, l)
                    if (kind, l) == (0, 3):
                        start_rhs(0)
                        own_send(0, 0)
                    forward(kind, l)
                spread_rhs(0)
                arrived(at(ut1), at(ut1r))
                value = at(ut1)[0].astype(jnp.float32)
                for m in range(1, G[1]):
                    value = value + at(ut1)[m].astype(jnp.float32)
                at(u[1])[child, q] = (-value).astype(bf)

        @pl.when(middle)
        def _():
            with phase(19):
                value = at(up1)[half, q].astype(jnp.float32)
                arrived(at(ut1).at[pl.ds(1, G[1] - 1)], at(ut1r))
                for m in range(1, G[1]):
                    value = value + at(ut1)[m].astype(jnp.float32)
                at(u[1])[child, q] = (at(h1)[half].astype(jnp.float32) - value).astype(bf)
        here = at(u[1]).at[child, q]
        kept_here = q // 2 == core
        for m in range(2, CC, 2):
            rsem = at(ur1).at[0 if m == 2 else 1]
            counted(here, here, plane, rsem, z, flipped(2 * chip + q // 2, m))

        @pl.when(jnp.logical_not(kept_here))
        def _():
            push(here, here, at(beside), at(ur1).at[0], z, flipped(c, 1))

        @pl.when(border)
        def _():
            with phase(40):
                settle_all(0, 0)
                forward(0, 0)

        @pl.when(middle)
        def _():
            with phase(20):
                for l in lower:
                    for kind in range(2):
                        forward(kind, l)
        with phase(41):
            @pl.when(kept_here)
            def _():
                take(at(ur1).at[0], NQ * S[1])

            @pl.when(jnp.logical_not(kept_here))
            def _():
                take(at(ur1).at[0], 2 * NQ * S[1])
            wait_rhs(0)
        columns = pl.ds(pl.multiple_of(2 * core, 2), 2)
        with phase(42):
            part = dot_nt(at(u[1])[child, columns].reshape(NH, S[1]), at(table[0])[child])
            at(f0)[...] = at(B[0])[...].astype(jnp.float32) + part
            take(at(ur1).at[1], 2 * NQ * S[1])
        with phase(49):
            part = dot_nt(at(u[1])[1 - child, columns].reshape(NH, S[1]), at(table[0])[1 - child])
            right = (at(f0)[...] + part).astype(bf)
        with phase(43):
            arrived(at(Zm[0]), at(Zmr[0]))
        with phase(44):
            value = 0.0
            for blocks in (Z, Zm):
                solved = dot_nt(right, at(blocks[0])[...]).astype(bf)
                value = value + dot_nn(solved, at(blocks[0])[...])
            value = value.astype(bf)
            at(xp0)[...] = value
            for m in (3, 1, 2):
                counted(at(xp0), at(xr0).at[m], plane, at(xr0r), z, flipped(c, 2 * m))

        @pl.when(border)
        def _():
            with phase(45):
                settle_all(0, 1)
                forward(0, 1)
        def wait_mate(l):
            @pl.when(middle)
            def _():
                arrived(at(yb[l]).at[1], at(yr[l]))

            @pl.when(border)
            def _():
                arrived(at(yb[l]), at(yr[l]))
            if l < 3:
                arrived(at(Zm[l]), at(Zmr[l]))
                arrived(at(Cm[l]), at(Cmr[l]))

        with phase(50):
            arrived(at(Zm[3]), at(Zmr[3]))
            arrived(at(Cm[3]), at(Cmr[3]))
            for mate in range(2):
                leaf = core if mate == 0 else 1 - core
                block = at((C, Cm)[mate][3])[...]
                at(folded3)[mate] = dot_nn(at(table[2])[leaf], block).astype(bf)

        @pl.when(border)
        def _():
            with phase(48):
                settle_all(1, 1)
                forward(1, 1)
        with phase(46):
            arrived(at(xr0).at[pl.ds(1, chips - 1)], at(xr0r))
        with phase(47):
            value = at(xp0)[...].astype(jnp.float32)
            for m in range(1, chips):
                value = value + at(xr0)[m].astype(jnp.float32)
            value = value.astype(bf)
            at(x0)[...] = value

        farthest = jnp.where(border, across, beyond)
        second = jnp.where(border, beyond, across)

        def leave(l, piece, dst, c_to):
            for r in (farthest, second, pair):
                push(piece(r), dst, at(Os[l]), at(Or[l]), r, c_to)

            @pl.when(c_to == c)
            def _():
                pltpu.make_async_copy(piece(z), dst, at(Or[l])).start()

            @pl.when(c_to != c)
            def _():
                push(piece(z), dst, at(Os[l]), at(Or[l]), z, c_to)

        top_here, one_here = chip == z, q // 2 == z // 2
        one_to, two_to = 2 * chip + z % 2, 2 * chip + z // 2

        def top_piece(r):
            return at(x0).at[:, pl.ds(pl.multiple_of(r * K[0], 128), K[0])]

        @pl.when(top_here)
        def _():
            leave(0, top_piece, outs[0], c)

        def placed(l, low):
            return outs[l].at[pl.ds(pl.multiple_of(low, 16), NH)]

        with phase(51):
            at(v[1])[...] = dot_nn(value, at(table[0])[child]).astype(bf)
            low = at(v[1])[...]

        def residual(l, index, coupled, low):
            return (at(yb[l])[index].astype(jnp.float32) - dot_nn(low, at(coupled[l])[...])).astype(bf)

        with phase(52):
            wait_mate(1)
        with phase(53):
            value = dot_nn(residual(1, 0, C, low), at(Z[1])[...])
            value = value + dot_nn(residual(1, 1, Cm, low), at(Zm[1])[...])
            at(xp1)[...] = value.astype(bf)
            counted(at(xp1), at(xr1), plane, at(xr1r), z, flipped(c, 2))
        side = chip % 2
        @pl.when(border)
        def _():
            with phase(56):
                settle_all(1, 2)
                forward(1, 2)
        with phase(54):
            early = dot_nn(low, at(table[1])[side, S[1]:, :])
            arrived(at(xr1), at(xr1r))
        with phase(55):
            value = (at(xp1)[...].astype(jnp.float32) + at(xr1)[...].astype(jnp.float32)).astype(bf)
            at(v[2])[...] = (dot_nn(value, at(table[1])[side, :S[1], :]) + early).astype(bf)
            at(x1)[...] = value
            low = at(v[2])[...]
        wait_mate(2)
        with phase(57):
            value = dot_nn(residual(2, 0, C, low), at(Z[2])[...])
            value = value + dot_nn(residual(2, 1, Cm, low), at(Zm[2])[...])
            at(x2)[...] = value.astype(bf)
            high = at(x2)[...]
        with phase(58):
            @pl.when(one_here)
            def _():
                for r in range(R):
                    at(f1)[r] = at(x1)[:, r * K[1]:(r + 1) * K[1]]
                leave(1, lambda r: at(f1).at[r], placed(1, core * NH), one_to)

            def two_piece(r):
                return at(x2).at[:, pl.ds(pl.multiple_of(r * K[2], 128), K[2])]

            leave(2, two_piece, placed(2, half * N + core * NH), two_to)
        with phase(59):
            wait_mate(3)
        with phase(60):
            for mate in range(2):
                below = dot_nn(high, at(folded3)[mate, :S[2], :])
                below = below + dot_nn(low, at(folded3)[mate, S[2]:, :])
                below = (at(yb[3])[mate].astype(jnp.float32) - below).astype(bf)
                value = dot_nt(below, at((Z, Zm)[mate][3])[...]).astype(bf)
                for r in range(R):
                    piece = value[:, r * K[3]:(r + 1) * K[3]]
                    at(f3)[mate * R + r] = jnp.concatenate([piece[:NH // 2], piece[NH // 2:]], axis=1)
            low_row = pl.multiple_of((z * N + core * NH) // 2, 16)
            leaf_out = outs[3].at[pl.ds(low_row, NH // 2)]
            for mate in range(2):
                leave(3, lambda r: at(f3).at[mate * R + r], leaf_out, c if mate == 0 else flipped(c, 1))
        with phase(61):
            for l in levels:
                drain(0, l)
                if l:
                    drain(1, l)
                drain_rhs(l)
                if l < 3:
                    drain_spread(l)

            @pl.when(middle)
            def _():
                for l in lower:
                    arrived(at(y[l]).at[pl.ds(0, 3)], at(ys[l]))
                take(at(inner), sent[inner])
            take(at(plane), sent[plane])
            joined = [shape for shape in z_shape + c_shape[1:] if shape[1] % 128 == 0]
            take(at(mates), sum(elements(shape) for shape in joined))
            for shape, copy in zip(c_shape[1:], Cm[1:]):
                if shape[1] % 128:
                    arrived(at(copy), at(mates1))

            @pl.when(jnp.logical_not(kept_here))
            def _():
                arrived(at(u[1]).at[child, q], at(beside))

            @pl.when(top_here)
            def _():
                arrived(at(x0).at[:, pl.ds(0, S[0] - K[0])], at(Os[0]))

            @pl.when(jnp.logical_and(one_here, one_to == c))
            def _():
                arrived(at(f1).at[pl.ds(0, R - 1)], at(Os[1]))

            @pl.when(jnp.logical_and(one_here, one_to != c))
            def _():
                arrived(at(f1), at(Os[1]))

            @pl.when(two_to == c)
            def _():
                arrived(at(x2).at[:, pl.ds(0, S[2] - K[2])], at(Os[2]))

            @pl.when(two_to != c)
            def _():
                arrived(at(x2), at(Os[2]))
            arrived(at(f3).at[pl.ds(0, 2 * R - 1)], at(Os[3]))
        with phase(62):
            for l in levels:
                arrived(outs[l], at(Or[l]))

    return kernel, scratch


def hand_on(turned, *refs):
    arriving = refs[12]
    for i in range(4):
        pltpu.make_async_copy(refs[i], refs[8 + i], arriving.at[i]).start()
    for i, (turn, source, target) in enumerate(zip(turned, refs[8:12], refs[4:8])):
        pltpu.make_async_copy(refs[i], source, arriving.at[i]).wait()
        rows, lanes = source.shape
        if not turn:
            target[...] = source[...]
        elif target.shape == (lanes, rows):
            target[...] = dot_nt(eye(lanes), source[...]).astype(target.dtype)
        else:
            both = dot_nt(eye(lanes), source[...]).astype(target.dtype)
            pieces = []
            for low in range(0, rows, 16):
                pieces += [both[:lanes // 2, low:low + 16], both[lanes // 2:, low:low + 16]]
            target[...] = jnp.concatenate(pieces, axis=1)


def fused_device(*blocks):
    plan = Plan(
        lax.axis_size("row"), lax.axis_size("col"),
        [block.shape for block in blocks[:4]], blocks[7].shape,
        [block.shape for block in blocks[11:14]],
    )
    if not plan.fits():
        return per_device(*blocks)
    kernel, scratch = build_kernel(plan)
    blocks = list(blocks)
    for at in (0, 1, 2, 3, 7, 8, 9, 10):
        if narrow(blocks[at].shape[1]):
            blocks[at] = blocks[at].T
    blocks = [pltpu.with_memory_space_constraint(block, pltpu.HBM) for block in blocks]
    vmem = pl.BlockSpec(memory_space=pltpu.VMEM)
    anywhere = pl.BlockSpec(memory_space=pltpu.HBM)
    solved = pl.pallas_call(
        kernel,
        out_shape=tuple(
            jax.ShapeDtypeStruct(shape, blocks[0].dtype) for shape in plan.result_shapes()
        ),
        in_specs=[anywhere] * 14,
        out_specs=(pl.BlockSpec(memory_space=pl.ANY),) * 4,
        scratch_shapes=scratch,
        compiler_params=pltpu.CompilerParams(
            collective_id=0, has_side_effects=True, vmem_limit_bytes=VMEM_LIMIT
        ),
    )(*blocks)
    turned = [not narrow(width) for width in plan.width]
    solved = pl.pallas_call(
        functools.partial(hand_on, turned),
        out_shape=tuple(
            jax.ShapeDtypeStruct((strip, width) if turn else (width, strip), blocks[0].dtype)
            for width, strip, turn in zip(plan.width, plan.strip, turned)
        ),
        in_specs=[pl.BlockSpec(memory_space=pl.ANY)] * 4,
        out_specs=(vmem,) * 4,
        scratch_shapes=[pltpu.VMEM(block.shape, block.dtype) for block in solved]
        + [pltpu.SemaphoreType.DMA((4,))],
        compiler_params=pltpu.CompilerParams(vmem_limit_bytes=2**20),
    )(*solved)
    return tuple(block if turn else block.T for block, turn in zip(solved, turned))


def solution(mesh):
    in_specs = (
        P("col", "row"),
        P("col", "row"),
        P("col", "row"),
        P("col", "row"),
        P("row", "col"),
        P("row", "col"),
        P("row", "col"),
        P("row", "col"),
        P("row", "col"),
        P("row", "col"),
        P("row", "col"),
        P(),
        P(),
        P(),
    )
    out_specs = (P("row", "col"), P("row", "col"), P("row", "col"), P("row", "col"))
    return jax.shard_map(
        fused_device, mesh=mesh, in_specs=in_specs, out_specs=out_specs, check_vma=False
    )
```

```python
import functools

import jax
import jax.numpy as jnp
from jax import lax
from jax.experimental import pallas as pl
from jax.experimental.pallas import tpu as pltpu
from jax.sharding import PartitionSpec as P


def swapped(value, axis, stride):
    mask = 2**stride
    pairs = [(source, source ^ mask) for source in range(lax.axis_size(axis))]
    return lax.ppermute(value, axis, pairs)


def route_tables(mapping, child_index, parent_sep, parent_upd, strips, row_index):
    positions = lax.dynamic_index_in_dim(mapping, child_index, 0, keepdims=False)
    sep_rows = parent_sep // strips
    in_separator = positions < parent_sep
    if parent_upd > 0:
        upd_rows = parent_upd // strips
        target = jnp.where(
            in_separator, positions // sep_rows, (positions - parent_sep) // upd_rows
        )
        offset = jnp.where(
            in_separator, positions % sep_rows, sep_rows + (positions - parent_sep) % upd_rows
        )
    else:
        target = positions // sep_rows
        offset = positions % sep_rows
    block_rows = positions.shape[0] // strips
    blocks = target.reshape(strips, block_rows)
    matches = (blocks[:, :, None] == jnp.arange(strips, dtype=jnp.int32)[None, None, :]).astype(
        jnp.int32
    )
    slot_of = jnp.sum((jnp.cumsum(matches, axis=1) - 1) * matches, axis=2).reshape(-1)
    block_len = sep_rows + parent_upd // strips
    capacity = 2 * positions.shape[0] // (strips * strips)
    source = jnp.arange(positions.shape[0], dtype=jnp.int32) // block_rows
    mine_here = target == row_index
    column_at = jnp.where(mine_here, slot_of, capacity)
    lookup = jnp.full((strips, capacity + 1), block_len, jnp.int32)
    lookup = lookup.at[source, column_at].set(jnp.where(mine_here, offset, block_len))[:, :capacity]
    local_target = lax.dynamic_slice_in_dim(target, row_index * block_rows, block_rows)
    local_slots = lax.dynamic_slice_in_dim(slot_of, row_index * block_rows, block_rows)
    return (local_target, local_slots, lookup, capacity, block_len)


def pack_rows(values, local_target, local_slots, strips, capacity):
    buffer = jnp.zeros((strips, capacity, values.shape[1]), values.dtype)
    return buffer.at[local_target, local_slots].set(values)


def unpack_rows(received, lookup, block_len):
    summed = jnp.zeros((block_len + 1, received.shape[2]), jnp.float32)
    return summed.at[lookup].add(received.astype(jnp.float32))[:block_len]


def spread(portion, depth_bits, pass_on, column):
    for bit_index in range(depth_bits):
        partner = pass_on(portion, bit_index)
        is_upper = column >> bit_index & 1 == 1
        portion = jnp.where(
            is_upper,
            jnp.concatenate([partner, portion], axis=-1),
            jnp.concatenate([portion, partner], axis=-1),
        )
    return portion


def shrink(entire, depth_bits, pass_on, column):
    for bit_index in reversed(range(depth_bits)):
        half_width = entire.shape[-1] // 2
        low_part = entire[..., :half_width]
        high_part = entire[..., half_width:]
        is_upper = column >> bit_index & 1 == 1
        kept_part = jnp.where(is_upper, high_part, low_part)
        sent_part = jnp.where(is_upper, low_part, high_part)
        entire = kept_part + pass_on(sent_part, bit_index)
    return entire


def per_device(
    inverse_top,
    inverse_one,
    inverse_two,
    inverse_leaf,
    coupling_one,
    coupling_two,
    coupling_leaf,
    rhs_top,
    rhs_one,
    rhs_two,
    rhs_leaf,
    parent_map_one,
    parent_map_two,
    parent_map_leaf,
):
    strips = lax.axis_size("row")
    col_count = lax.axis_size("col")
    row_here = lax.axis_index("row")
    column = lax.axis_index("col")
    inverses = [inverse_top, inverse_one, inverse_two, inverse_leaf]
    couplings = [None, coupling_one, coupling_two, coupling_leaf]
    right_sides = [rhs_top, rhs_one, rhs_two, rhs_leaf]
    parent_maps = [None, parent_map_one, parent_map_two, parent_map_leaf]
    orders = [inverse.shape[1] * strips for inverse in inverses]
    groups = [col_count >> tree_level for tree_level in range(4)]
    group_bits = [group_size.bit_length() - 1 for group_size in groups]
    pass_rhs = lambda values, bit_index: swapped(values, "col", bit_index)
    pass_update_sum = lambda values, bit_index: swapped(
        values.astype(jnp.bfloat16), "col", bit_index
    ).astype(values.dtype)
    pass_update_spread = lambda values, bit_index: swapped(values, "col", bit_index)
    pass_solution_sum = lambda values, bit_index: swapped(
        values.astype(jnp.bfloat16), "col", bit_index
    ).astype(values.dtype)
    pass_solution_spread = lambda values, bit_index: swapped(values, "col", bit_index)
    full_rhs = [
        spread(right_sides[tree_level], group_bits[tree_level], pass_rhs, column)
        for tree_level in range(4)
    ]
    own_routes = [None]
    for tree_level in range(1, 4):
        parent_order = orders[tree_level - 1]
        parent_update = parent_order if tree_level > 1 else 0
        front_here = column // groups[tree_level]
        own_routes.append(
            route_tables(
                parent_maps[tree_level], front_here, parent_order, parent_update, strips, row_here
            )
        )
    pivots = [None] * 4
    incoming = None
    for tree_level in (3, 2, 1, 0):
        sep_rows = inverses[tree_level].shape[1]
        if incoming is None:
            separator = full_rhs[tree_level]
            own_update = None
        else:
            separator = (full_rhs[tree_level].astype(jnp.float32) + incoming[:sep_rows]).astype(
                jnp.bfloat16
            )
            own_update = lax.optimization_barrier(incoming[sep_rows:].astype(jnp.bfloat16))
        partial_value = jnp.dot(inverses[tree_level], separator, preferred_element_type=jnp.float32)
        solved = lax.psum(partial_value.astype(jnp.bfloat16), "row")
        pivots[tree_level] = solved
        if tree_level > 0:
            coupled = jnp.dot(couplings[tree_level], solved, preferred_element_type=jnp.float32)
            reduced = shrink(coupled, group_bits[tree_level], pass_update_sum, column)
            if own_update is None:
                portion = (-reduced).astype(jnp.bfloat16)
            else:
                start_at = column % groups[tree_level] * reduced.shape[1]
                kept_rows = lax.dynamic_slice_in_dim(own_update, start_at, reduced.shape[1], 1)
                portion = (kept_rows.astype(jnp.float32) - reduced).astype(jnp.bfloat16)
            updated = spread(portion, group_bits[tree_level], pass_update_spread, column)
            own_target, own_slots, own_lookup, capacity, block_len = own_routes[tree_level]
            got_own = lax.all_to_all(
                pack_rows(updated, own_target, own_slots, strips, capacity),
                "row",
                split_axis=0,
                concat_axis=0,
                tiled=True,
            )
            own_part = unpack_rows(got_own, own_lookup, block_len)
            partner = swapped(own_part.astype(jnp.bfloat16), "col", group_bits[tree_level])
            incoming = own_part + partner.astype(jnp.float32)
    solutions = [None] * 4
    parent_solution = None
    parent_gathered = None
    for tree_level in range(4):
        solved = pivots[tree_level]
        gathered = None
        if tree_level == 0:
            residual = solved
        else:
            own_target, own_slots, own_lookup, capacity, block_len = own_routes[tree_level]
            pieces = [parent_solution]
            if parent_gathered is not None:
                pieces.append(parent_gathered)
            pieces.append(jnp.zeros((1, parent_solution.shape[1]), jnp.bfloat16))
            parent_rows = jnp.concatenate(pieces, axis=0)
            returned = lax.all_to_all(
                parent_rows[own_lookup], "row", split_axis=0, concat_axis=0, tiled=True
            )
            gathered = returned[own_target, own_slots]
            coupling_term = jnp.dot(
                couplings[tree_level].T, gathered, preferred_element_type=jnp.float32
            )
            residual = (
                solved.astype(jnp.float32)
                - lax.psum(coupling_term.astype(jnp.bfloat16), "row").astype(jnp.float32)
            ).astype(jnp.bfloat16)
        contribution = jnp.dot(inverses[tree_level].T, residual, preferred_element_type=jnp.float32)
        if tree_level == 0:
            summed = lax.psum(contribution.astype(jnp.bfloat16), "col")
            solution = summed
            rhs_width = solution.shape[1] // groups[0]
            solutions[0] = lax.dynamic_slice_in_dim(
                solution, column % groups[0] * rhs_width, rhs_width, 1
            )
        else:
            portion = shrink(
                contribution, group_bits[tree_level], pass_solution_sum, column
            ).astype(jnp.bfloat16)
            solutions[tree_level] = portion
            if tree_level < 3:
                solution = spread(portion, group_bits[tree_level], pass_solution_spread, column)
        parent_solution = solution
        parent_gathered = gathered
    return (solutions[0], solutions[1], solutions[2], solutions[3])


MESH = pl.DeviceIdType.MESH
VMEM_LIMIT = 32 * 2**20


def dot_nn(left, right):
    return lax.dot_general(left, right, (((1,), (0,)), ((), ())), preferred_element_type=jnp.float32)


def dot_nt(left, right):
    return lax.dot_general(left, right, (((1,), (1,)), ((), ())), preferred_element_type=jnp.float32)


def eye(size):
    rows = lax.broadcasted_iota(jnp.int32, (size, size), 0)
    columns = lax.broadcasted_iota(jnp.int32, (size, size), 1)
    return jnp.where(rows == columns, 1.0, 0.0).astype(jnp.bfloat16)


def flipped(value, mask):
    result = value
    bit = 1
    while bit <= mask:
        if mask & bit:
            result = result + bit * (1 - 2 * ((value // bit) % 2))
        bit *= 2
    return result


class Plan:
    def __init__(self, rows, cols, inverse_shapes, rhs_top_shape, map_shape):
        self.rows, self.cols = rows, cols
        self.strip = [shape[1] for shape in inverse_shapes]
        self.order = [shape[1] * rows for shape in inverse_shapes]
        self.local = [shape[0] for shape in inverse_shapes]
        self.group = [cols >> level for level in range(4)]
        self.columns = rhs_top_shape[1] * cols
        self.width = [self.columns // group if group else 0 for group in self.group]
        self.mine = self.columns // rows
        self.map_shape = map_shape

    def total(self, level):
        return self.order[level] * (2 if level else 1)

    def result_shapes(self):
        shapes = list(zip(self.width, self.strip))
        return shapes[:3] + [(self.width[3] // 2, 2 * self.strip[3])]

    def span_rows(self):
        n, order, width = self.mine, self.order, self.width
        shared = 3 * (n // 4) * order[1] + 3 * (n // 2) * order[0] + n // 2 * order[1]
        inner = 2 * n * order[3] + 4 * n * order[2] + 8 * (n // 4) * order[1]
        joined = sum(2 * order[level] * self.local[level] for level in (2, 3))
        joined += sum(order[level] * self.local[level] for level in (0, 1))
        return max(shared, inner, joined, 9 * n * order[1], 3 * width[0] * order[0], 3 * n * order[2]) // 128

    def fits(self):
        table = sum(
            2 * self.total(level) * self.order[level + 1] * 2 for level in range(3)
        )
        if self.rows != 4 or self.group[3] != 1 or self.mine * self.rows != self.columns or table > 24 * 2**20:
            return False
        if self.group != [8, 4, 2, 1] or self.mine % 64:
            return False
        for level in range(4):
            if self.strip[level] % 64 or self.order[level] % 128 or self.local[level] % 64:
                return False
        if not packed((self.mine, self.strip[1])):
            return False
        return narrow(self.strip[3]) and not any(narrow(strip) for strip in self.strip[:3])


def elements(shape):
    count = 1
    for extent in shape:
        count *= extent
    return count


def packed(shape):
    return shape[1] > 128 and shape[1] % 128 == 64


def packed_shape(shape):
    return (shape[0] * (shape[1] // 128) + shape[0] // 2, 128)


def narrow(size):
    return size < 128


def phase(number):
    return jax.named_scope(str(number))


def build_kernel(plan):
    R, CC, N = plan.rows, plan.cols, plan.mine
    S, K, L, G, W = plan.order, plan.strip, plan.local, plan.group, plan.width
    N2, NH, NQ, chips = 2 * N, N // 2, N // G[1], G[0] // 2
    bf = jnp.bfloat16
    scratch = []

    def ref(shape, dtype=bf):
        scratch.append(pltpu.VMEM(shape, dtype))
        return len(scratch) - 1

    def sems(*shape):
        scratch.append(pltpu.SemaphoreType.DMA(shape) if shape else pltpu.SemaphoreType.DMA)
        return len(scratch) - 1

    levels, lower = range(4), (1, 2, 3)
    z_shape = [(S[3], L[3]) if l == 3 else (L[l], S[l]) for l in levels]
    c_shape = [None] + [(S[l], L[l]) for l in lower]
    Z = [ref(z_shape[l]) for l in levels]
    C = [None] + [ref(c_shape[l]) for l in lower]
    Zm = [ref(z_shape[l]) for l in levels]
    Cm = [None] + [ref(c_shape[l]) for l in lower]
    Zp = [ref((R,) + packed_shape((L[l], K[l]))) if l < 3 and packed((L[l], K[l])) else None for l in levels]
    Cp = [None] + [ref((R,) + packed_shape((K[l], L[l]))) if packed((K[l], L[l])) else None for l in lower]
    Zraw = [ref((L[l], K[l])) if Zp[l] is not None else None for l in levels]
    Craw = [None] + [ref((K[l], L[l])) if Cp[l] is not None else None for l in lower]
    Zr, Zs = [sems() for _ in levels], [sems() for _ in levels]
    Cr, Cs = [None] + [sems() for _ in lower], [None] + [sems() for _ in lower]
    Zmr, Cmr, mates, mates1 = [sems() for _ in levels], [None] + [sems() for _ in lower], sems(), sems()
    table = [ref((2, plan.total(l), S[l + 1])) for l in range(3)]
    held_map = [None] + [ref(plan.map_shape[l - 1], jnp.int32) for l in lower]
    local = sems(6)
    B = [ref((NH, S[0])), ref((2, R) + packed_shape((N, K[1]))), ref((S[2], N2)), ref((S[3], N2))]
    B1, rhs_raw, rhs_packed = ref((N2, S[1])), ref((N, K[1])), ref(packed_shape((N, K[1])))
    Bs, Br = [sems() for _ in levels], [sems() for _ in levels]
    Ds, Dr = [sems(), sems(), sems()], [sems(), sems(2), sems()]
    y = [None] + [ref((4, NH, L[l])) for l in lower]
    yb = [None] + [ref((2, NH, L[l])) for l in lower]
    ys, yr = [None] + [sems() for _ in lower], [None] + [sems() for _ in lower]
    u = [None, ref((2, G[1], NQ, S[1])), ref((2, 2, G[1], NQ, S[2])), ref((2, N2, S[3]))]
    ur, ur1 = [None, None, sems(), sems()], sems(2)
    f0 = ref((NH, S[0]), jnp.float32)
    up1, ut1, ut1r = ref((2, G[1], NQ, S[1])), ref((G[1], NQ, S[1])), sems()
    h1 = ref((2, NQ, S[1]))
    folded, early1 = ref((2, L[1], S[2])), ref((N2, L[1]), jnp.float32)
    up2, ut2, ut2r = ref((2, N, S[2])), ref((N, S[2])), sems()
    xp0, xr0, xr0r = ref((NH, S[0])), ref((chips, NH, S[0])), sems()
    x0 = ref((NH, S[0]))
    xp1, xr1, xr1r = ref((NH, S[1])), ref((NH, S[1])), sems()
    v = [None] + [ref((NH, S[l])) for l in (1, 2)]
    x1, x2 = ref((NH, S[1])), ref((NH, S[2]))
    f1, f3 = ref((R, NH, K[1])), ref((2 * R, NH // 2, 2 * K[3]))
    folded3 = ref((2, 2 * S[2], L[3]))
    Os, Or = [sems() for _ in levels], [sems() for _ in levels]
    plane, inner, beside = sems(), sems(), sems()
    scratch.append(pltpu.SemaphoreType.REGULAR)
    ready = len(scratch) - 1
    scratch.append(pltpu.SemaphoreType.REGULAR)
    ready_group = len(scratch) - 1
    span = ref((plan.span_rows(), 128))

    def kernel(*refs):
        inverse = refs[0:4]
        coupling = (None,) + tuple(refs[4:7])
        rhs = refs[7:11]
        maps = (None,) + tuple(refs[11:14])
        outs = refs[14:18]
        held = refs[18:]
        at = lambda index: held[index]
        z = lax.axis_index("row")
        c = lax.axis_index("col")
        core, chip = c % 2, c // 2
        middle = jnp.logical_and(z > 0, z < R - 1)
        border = jnp.logical_not(middle)
        half = z % 2
        pair = z + 1 - 2 * half
        across = R - 1 - z
        beyond = R - 1 - pair
        sent = {}

        def remote(src, dst, ssem, rsem, z_to, c_to):
            return pltpu.make_async_remote_copy(
                src_ref=src, dst_ref=dst, send_sem=ssem, recv_sem=rsem,
                device_id=(z_to, c_to), device_id_type=MESH,
            )

        def push(src, dst, ssem, rsem, z_to, c_to):
            remote(src, dst, ssem, rsem, z_to, c_to).start()

        def counted(src, dst, index, rsem, z_to, c_to):
            push(src, dst, at(index), rsem, z_to, c_to)
            sent[index] = sent.get(index, 0) + elements(src.shape)

        def arrived(dst, rsem):
            pltpu.make_async_copy(dst, dst, rsem).wait()

        def take(sem, count):
            view = at(span).at[pl.ds(0, count // 128)]
            pltpu.make_async_copy(view, view, sem).wait()

        barrier = pltpu.get_barrier_semaphore()
        group_here = [(z, flipped(c, m)) for m in range(1, G[1])]
        opposite = (z, flipped(c, G[1]))

        def greet(semaphore, *friends):
            for friend in friends:
                pl.semaphore_signal(semaphore, inc=1, device_id=friend, device_id_type=MESH)

        greet(barrier, (pair, c))

        @pl.when(middle)
        def _():
            greet(barrier, (across, c), (beyond, c), *group_here)

        @pl.when(border)
        def _():
            greet(barrier, opposite)

        raws = [(rhs[1], at(rhs_raw))]
        for l in levels:
            if Zp[l] is not None:
                raws.append((inverse[l], at(Zraw[l])))
            if l and Cp[l] is not None:
                raws.append((coupling[l], at(Craw[l])))
        loads = raws + [(maps[l], at(held_map[l])) for l in lower]
        for i, (src, dst) in enumerate(loads):
            pltpu.make_async_copy(src, dst, at(local).at[i]).start()

        def slot(kind, l, r):
            if kind == 0:
                if Zp[l] is not None:
                    return at(Zp[l]).at[r], at(Zr[l])
                if l == 3:
                    low = pl.multiple_of(r * K[l], 16)
                    return at(Z[l]).at[pl.ds(low, K[l])], at(Zr[l])
                low = pl.multiple_of(r * K[l], 128)
                return at(Z[l]).at[:, pl.ds(low, K[l])], at(Zr[l])
            if Cp[l] is not None:
                return at(Cp[l]).at[r], at(Cr[l])
            low = pl.multiple_of(r * K[l], 16)
            return at(C[l]).at[pl.ds(low, K[l])], at(Cr[l])

        def is_packed(kind, l):
            return (Zp, Cp)[kind][l] is not None

        def source(kind, l):
            if is_packed(kind, l):
                return slot(kind, l, z)[0]
            return (inverse, coupling)[kind][l]

        def send_sem(kind, l):
            return at((Zs, Cs)[kind][l])

        def own_load(kind, l):
            if not is_packed(kind, l):
                dst, sem = slot(kind, l, z)
                pltpu.make_async_copy(source(kind, l), dst, sem).start()

        def own_send(kind, l):
            dst, sem = slot(kind, l, z)
            push(source(kind, l), dst, send_sem(kind, l), sem, jnp.where(middle, across, pair), c)

            @pl.when(border)
            def _():
                push(source(kind, l), dst, send_sem(kind, l), sem, beyond, c)

        def own_out(kind, l):
            dst, sem = slot(kind, l, z)
            push(source(kind, l), dst, send_sem(kind, l), sem, pair, c)

        def pass_on(kind, l, origins=(across, beyond)):
            for r in origins:
                dst, sem = slot(kind, l, r)
                push(dst, dst, send_sem(kind, l), sem, pair, c)

        def settle_all(kind, l):
            rsem = slot(kind, l, z)[1]
            if is_packed(kind, l):
                arrived(at((Zp, Cp)[kind][l]).at[pl.ds(0, R - 1)], rsem)
                unpack(kind, l)
            else:
                arrived(at((Z, C)[kind][l]), rsem)

        def unpacked(block, rows, lanes):
            whole = lanes // 128 * rows
            rest = block[whole:]
            rest = jnp.concatenate([rest[:, :lanes % 128], rest[:, lanes % 128:]], axis=0)
            return jnp.concatenate([block[i:i + rows] for i in range(0, whole, rows)] + [rest], axis=1)

        def unpack(kind, l):
            rows, lanes = (L[l], K[l]) if kind == 0 else (K[l], L[l])
            for r in range(R):
                value = unpacked(at((Zp, Cp)[kind][l])[r], rows, lanes)
                if kind == 0:
                    at(Z[l])[:, r * lanes:(r + 1) * lanes] = value
                else:
                    at(C[l])[r * rows:(r + 1) * rows, :] = value

        def pack(raw):
            value = raw[...]
            rows, lanes = value.shape
            whole = lanes - lanes % 128
            pieces = [value[:, i:i + 128] for i in range(0, whole, 128)]
            rest = value[:, whole:]
            rest = jnp.concatenate([rest[:rows // 2], rest[rows // 2:]], axis=1)
            return jnp.concatenate(pieces + [rest], axis=0)

        def drain(kind, l):
            if is_packed(kind, l):
                whole = at((Zp, Cp)[kind][l])
                part = whole.at[pl.ds(0, R // 2)]
            else:
                whole = at((Z, C)[kind][l])
                if kind == 0 and l < 3:
                    part = whole.at[:, pl.ds(0, S[l] // 2)]
                else:
                    part = whole.at[pl.ds(0, S[l] // 2)]

            @pl.when(middle)
            def _():
                arrived(whole, send_sem(kind, l))

            @pl.when(border)
            def _():
                arrived(part, send_sem(kind, l))

        def rhs_pieces(l):
            q = c % G[l]
            if l == 3:
                return [
                    (rhs[3].at[:, pl.ds(i * N2, N2)], at(B[3]).at[pl.ds(pl.multiple_of(z * K[3], 16), K[3])], 1 + i)
                    for i in range(2)
                ]
            if l == 2:
                return [(rhs[2], at(B[2]).at[pl.ds(pl.multiple_of(z * K[2], 16), K[2])], 1 + q)]
            if l == 1:
                return [(at(rhs_packed), at(B[1]).at[q % 2, z], 1 + q // 2)]
            lanes = pl.ds(pl.multiple_of(z * K[0], 128), K[0])
            return [(rhs[0], at(B[0]).at[:, lanes], q // 2)]

        def start_rhs(l):
            for src, dst, z_to in rhs_pieces(l):
                @pl.when(z_to == z)
                def _():
                    pltpu.make_async_copy(src, dst, at(Br[l])).start()

                @pl.when(z_to != z)
                def _():
                    push(src, dst, at(Bs[l]), at(Br[l]), z_to, c)

        def drain_rhs(l):
            pieces = rhs_pieces(l)
            if l == 3:
                @pl.when(middle)
                def _():
                    arrived(at(B[3]).at[pl.ds(0, K[3])], at(Bs[3]))

                @pl.when(border)
                def _():
                    arrived(at(B[3]).at[pl.ds(0, 2 * K[3])], at(Bs[3]))
                return
            src, dst, z_to = pieces[0]

            @pl.when(z_to != z)
            def _():
                arrived(dst, at(Bs[l]))

        def rhs_spread(l):
            q = c % G[l]
            if l == 2:
                return z == 1 + q, at(B[2]), at(Dr[2])
            if l == 1:
                return z == 1 + q // 2, at(B[1]).at[q % 2], at(Dr[1]).at[q % 2]
            return z == q // 2, at(B[0]), at(Dr[0])

        def spread_rhs(l):
            holds, here, rsem = rhs_spread(l)

            @pl.when(holds)
            def _():
                arrived(here, at(Br[l]))
                for m in range(2, CC, 2) if l == 0 else range(1, G[l]):
                    push(here, here, at(Ds[l]), rsem, z, flipped(c, m))

        def drain_spread(l):
            holds, here, _ = rhs_spread(l)

            @pl.when(holds)
            def _():
                take(at(Ds[l]), (chips - 1, G[1] - 1, 1)[l] * elements(here.shape))

        def wait_rhs(l):
            holds, here, rsem = rhs_spread(l)
            if l != 1:
                @pl.when(jnp.logical_not(holds))
                def _():
                    arrived(here, rsem)
                return
            for part in range(2):
                @pl.when(jnp.logical_not(jnp.logical_and(holds, c % 2 == part)))
                def _():
                    arrived(at(B[1]).at[part], at(Dr[1]).at[part])

        def make_table(l):
            front = c // G[l]
            step = K[l]
            for child in range(2):
                row = at(held_map[l + 1])[pl.ds(2 * front + child, 1), :]

                def body(i, carry):
                    start = pl.multiple_of(i * step, 16)
                    at_row = lax.broadcasted_iota(jnp.int32, (step, S[l + 1]), 0) + start
                    at(table[l])[child, pl.ds(start, step), :] = jnp.where(
                        at_row == row, 1.0, 0.0
                    ).astype(bf)
                    return carry

                lax.fori_loop(0, plan.total(l) // step, body, 0)

        def gathered(l, low, size, first, second):
            value = dot_nt(first, at(table[l])[0, low:low + size, :])
            return value + dot_nt(second, at(table[l])[1, low:low + size, :])

        def forward(kind, l):
            own, copy = at((Z, C)[kind][l]), at((Zm, Cm)[kind][l])
            ssem = at(mates1 if own.shape[1] % 128 else mates)
            push(own, copy, ssem, at((Zmr, Cmr)[kind][l]), z, flipped(c, 1))

        def hand_over(l):
            at(yb[l])[0] = at(y[l])[2 * half + core]
            src = at(y[l]).at[2 * half + 1 - core]
            push(src, at(yb[l]).at[1], at(ys[l]), at(yr[l]), z, flipped(c, 1))
            src = at(y[l]).at[2 * (1 - half) + core]
            push(src, at(yb[l]).at[0], at(ys[l]), at(yr[l]), pair, c)
            src = at(y[l]).at[2 * (1 - half) + 1 - core]
            push(src, at(yb[l]).at[1], at(ys[l]), at(yr[l]), pair, flipped(c, 1))

        with phase(2):
            @pl.when(middle)
            def _():
                pl.semaphore_wait(barrier, G[1] + 1)

            @pl.when(border)
            def _():
                pl.semaphore_wait(barrier, 3)

        with phase(3):
            own_send(0, 3)
            start_rhs(3)
            own_send(1, 3)
            pltpu.make_async_copy(*loads[0], at(local).at[0]).wait()
            at(rhs_packed)[...] = pack(at(rhs_raw))
            start_rhs(2)
            start_rhs(1)
            own_send(0, 2)
            own_send(1, 2)
            for i, (src, dst) in enumerate(loads[1:]):
                pltpu.make_async_copy(src, dst, at(local).at[i + 1]).wait()
            for l in levels:
                if Zp[l] is not None:
                    at(Zp[l])[z] = pack(at(Zraw[l]))
                if l and Cp[l] is not None:
                    at(Cp[l])[z] = pack(at(Craw[l]))
            own_send(0, 1)
            own_send(1, 1)
            for l in levels:
                own_load(0, l)
                if l:
                    own_load(1, l)

            @pl.when(middle)
            def _():
                own_out(0, 0)
                for l in (3, 2, 1):
                    own_out(0, l)
                    own_out(1, l)

            @pl.when(border)
            def _():
                greet(at(ready), opposite)
                pl.semaphore_wait(at(ready), 1)
                greet(at(ready), (pair, c))

        def last_send(turn):
            @pl.when(turn)
            def _():
                own_send(0, 0)

        make_table(2)

        @pl.when(middle)
        def _():
            with phase(31):
                arrived(at(B[3]), at(Br[3]))
                right = dot_nt(eye(N2), at(B[3])[...]).astype(bf)
                settle_all(0, 3)
                start_rhs(0)
                last_send(core == 0)
                pl.semaphore_wait(at(ready), 1)
                greet(at(ready_group), *group_here)
            with phase(32):
                solved = dot_nn(right, at(Z[3])[...]).astype(bf)
                at(y[3])[...] = solved.reshape(4, NH, L[3])
                settle_all(1, 3)
            with phase(33):
                at(u[3])[core] = (-dot_nt(solved, at(C[3])[...])).astype(bf)
                here = at(u[3]).at[core]
                counted(here, here, inner, at(ur[3]), z, flipped(c, 1))
                pl.semaphore_wait(at(ready_group), G[1] - 1)
                greet(at(ready), (pair, c))
                pass_on(0, 3)
                pass_on(1, 3)
        spread_rhs(2)
        spread_rhs(1)
        make_table(1)

        @pl.when(middle)
        def _():
            with phase(21):
                arrived(at(u[3]).at[0], at(ur[3]))
                wait_rhs(2)
            with phase(22):
                pair_of = at(u[3])[0], at(u[3])[1]
                right = dot_nt(eye(N2), at(B[2])[...]) + gathered(2, 0, S[2], *pair_of)
                right = right.astype(bf)
                lower_part = pl.ds(pl.multiple_of(core * N, N), N)
                pair_of = at(u[3])[0, lower_part, :], at(u[3])[1, lower_part, :]
                kept = gathered(2, S[2], S[2], *pair_of)
            with phase(23):
                settle_all(0, 2)
                pass_on(0, 2)
            with phase(24):
                solved = dot_nt(right, at(Z[2])[...]).astype(bf)
                at(y[2])[...] = solved.reshape(4, NH, L[2])
            with phase(25):
                settle_all(1, 2)
            with phase(26):
                at(up2)[...] = dot_nt(solved, at(C[2])[...]).astype(bf).reshape(2, N, S[2])
                counted(at(up2).at[1 - core], at(ut2), inner, at(ut2r), z, flipped(c, 1))
            with phase(27):
                own = at(up2)[core].astype(jnp.float32)
                arrived(at(ut2), at(ut2r))
                own = kept - (own + at(ut2)[...].astype(jnp.float32))
                child = (c // G[2]) % 2
                at(u[2])[child, core] = own.astype(bf).reshape(G[1], NQ, S[2])
                here = at(u[2]).at[child, core]
                for m in (3, 2, 1):
                    counted(here, here, inner, at(ur[2]), z, flipped(c, m))
        make_table(0)
        q, child = c % G[1], (c // G[1]) % 2

        @pl.when(middle)
        def _():
            with phase(11):
                wait_rhs(1)
                for part in range(2):
                    for r in range(R):
                        value = unpacked(at(B[1])[part, r], N, K[1])
                        at(B1)[part * N:(part + 1) * N, r * K[1]:(r + 1) * K[1]] = value
            with phase(14):
                settle_all(0, 1)
                pass_on(0, 1)
            with phase(10):
                at(early1)[...] = dot_nt(at(B1)[...], at(Z[1])[...])
                for i in range(2):
                    at(folded)[i] = dot_nn(at(Z[1])[...], at(table[1])[i, :S[1], :]).astype(bf)
            with phase(12):
                take(at(ur[2]), 3 * N * S[2])
            with phase(13):
                pair_of = [at(u[2])[i].reshape(N2, S[2]) for i in range(2)]
                solved = at(early1)[...]
                for i in range(2):
                    solved = solved + dot_nt(pair_of[i], at(folded)[i])
                solved = solved.astype(bf)
                at(y[1])[...] = solved.reshape(4, NH, L[1])
            with phase(16):
                settle_all(1, 1)
            with phase(17):
                coupled = dot_nt(solved, at(C[1])[...])
                at(up1)[...] = coupled.astype(bf).reshape(2, G[1], NQ, S[1])
                for m in (3, 2, 1):
                    src = at(up1).at[1 - half, flipped(q, m)]
                    counted(src, at(ut1).at[m], inner, at(ut1r), pair, flipped(c, m))
                for m in (3, 2, 1):
                    src = at(up1).at[half, flipped(q, m)]
                    counted(src, at(ut1).at[m], inner, at(ut1r), z, flipped(c, m))
                last_send(core == 1)
                pair_of = [at(u[2])[i, :, q].reshape(2 * NQ, S[2]) for i in range(2)]
                kept = gathered(1, S[1], S[1], *pair_of)
                at(h1)[...] = kept.astype(bf).reshape(2, NQ, S[1])
                at(up1)[1 - half, q] = (
                    at(up1)[1 - half, q].astype(jnp.float32) - at(h1)[1 - half].astype(jnp.float32)
                ).astype(bf)
                counted(at(up1).at[1 - half, q], at(ut1).at[0], inner, at(ut1r), pair, c)
                spread_rhs(0)
                settle_all(0, 0)
                pass_on(0, 0)
                pass_on(1, 1)
                hand_over(1)
                pass_on(1, 2)
                hand_over(2)
                hand_over(3)
                forward(0, 0)

        @pl.when(border)
        def _():
            with phase(18):
                pl.semaphore_wait(at(ready), 1)
                for kind, l in ((0, 3), (1, 3), (0, 2)):
                    settle_all(kind, l)
                    if (kind, l) == (0, 3):
                        start_rhs(0)
                    if (kind, l) != (1, 3):
                        last_send(core == (0 if l == 3 else 1))
                    forward(kind, l)
                spread_rhs(0)
                arrived(at(ut1), at(ut1r))
                value = at(ut1)[0].astype(jnp.float32)
                for m in range(1, G[1]):
                    value = value + at(ut1)[m].astype(jnp.float32)
                at(u[1])[child, q] = (-value).astype(bf)

        @pl.when(middle)
        def _():
            with phase(19):
                value = at(up1)[half, q].astype(jnp.float32)
                arrived(at(ut1).at[pl.ds(1, G[1] - 1)], at(ut1r))
                for m in range(1, G[1]):
                    value = value + at(ut1)[m].astype(jnp.float32)
                at(u[1])[child, q] = (at(h1)[half].astype(jnp.float32) - value).astype(bf)
        here = at(u[1]).at[child, q]
        kept_here = q // 2 == core
        for m in (6, 4, 2):
            rsem = at(ur1).at[0 if m == 2 else 1]
            counted(here, here, plane, rsem, z, flipped(2 * chip + q // 2, m))

        @pl.when(jnp.logical_not(kept_here))
        def _():
            push(here, here, at(beside), at(ur1).at[0], z, flipped(c, 1))

        @pl.when(border)
        def _():
            with phase(40):
                settle_all(0, 0)
                forward(0, 0)

        @pl.when(middle)
        def _():
            with phase(20):
                for l in lower:
                    for kind in range(2):
                        forward(kind, l)
        with phase(41):
            @pl.when(kept_here)
            def _():
                take(at(ur1).at[0], NQ * S[1])

            @pl.when(jnp.logical_not(kept_here))
            def _():
                take(at(ur1).at[0], 2 * NQ * S[1])
            wait_rhs(0)
        columns = pl.ds(pl.multiple_of(2 * core, 2), 2)
        with phase(42):
            part = dot_nt(at(u[1])[child, columns].reshape(NH, S[1]), at(table[0])[child])
            at(f0)[...] = at(B[0])[...].astype(jnp.float32) + part
            take(at(ur1).at[1], 2 * NQ * S[1])
        with phase(49):
            part = dot_nt(at(u[1])[1 - child, columns].reshape(NH, S[1]), at(table[0])[1 - child])
            right = (at(f0)[...] + part).astype(bf)
        with phase(43):
            arrived(at(Zm[0]), at(Zmr[0]))
        with phase(44):
            value = 0.0
            for blocks in (Z, Zm):
                solved = dot_nt(right, at(blocks[0])[...]).astype(bf)
                value = value + dot_nn(solved, at(blocks[0])[...])
            value = value.astype(bf)
            at(xp0)[...] = value
            for m in (3, 1, 2):
                counted(at(xp0), at(xr0).at[m], plane, at(xr0r), z, flipped(c, 2 * m))

        @pl.when(border)
        def _():
            with phase(45):
                settle_all(0, 1)
                forward(0, 1)
        def wait_mate(l):
            @pl.when(middle)
            def _():
                arrived(at(yb[l]).at[1], at(yr[l]))

            @pl.when(border)
            def _():
                arrived(at(yb[l]), at(yr[l]))
            if l < 3:
                arrived(at(Zm[l]), at(Zmr[l]))
                arrived(at(Cm[l]), at(Cmr[l]))

        with phase(50):
            arrived(at(Zm[3]), at(Zmr[3]))
            arrived(at(Cm[3]), at(Cmr[3]))
            for mate in range(2):
                leaf = core if mate == 0 else 1 - core
                block = at((C, Cm)[mate][3])[...]
                at(folded3)[mate] = dot_nn(at(table[2])[leaf], block).astype(bf)

        @pl.when(border)
        def _():
            with phase(48):
                settle_all(1, 1)
                forward(1, 1)
        with phase(46):
            arrived(at(xr0).at[pl.ds(1, chips - 1)], at(xr0r))
        with phase(47):
            value = at(xp0)[...].astype(jnp.float32)
            for m in range(1, chips):
                value = value + at(xr0)[m].astype(jnp.float32)
            value = value.astype(bf)
            at(x0)[...] = value

        farthest = jnp.where(border, across, beyond)
        second = jnp.where(border, beyond, across)

        def leave(l, piece, dst, c_to, kept=None):
            for r in (farthest, second, pair):
                push(piece(r), dst, at(Os[l]), at(Or[l]), r, c_to)

            keep = lambda: pltpu.make_async_copy(piece(z), dst, at(Or[l])).start()
            give = lambda: push(piece(z), dst, at(Os[l]), at(Or[l]), z, c_to)
            if kept is None:
                pl.when(c_to == c)(keep)
                pl.when(c_to != c)(give)
            elif kept:
                keep()
            else:
                give()

        top_here, one_here = chip == z, q // 2 == z // 2
        one_to, two_to = 2 * chip + z % 2, 2 * chip + z // 2

        def top_piece(r):
            return at(x0).at[:, pl.ds(pl.multiple_of(r * K[0], 128), K[0])]

        @pl.when(top_here)
        def _():
            leave(0, top_piece, outs[0], c, True)

        def placed(l, low):
            return outs[l].at[pl.ds(pl.multiple_of(low, 16), NH)]

        with phase(51):
            at(v[1])[...] = dot_nn(value, at(table[0])[child]).astype(bf)
            low = at(v[1])[...]

        def residual(l, index, coupled, low):
            return (at(yb[l])[index].astype(jnp.float32) - dot_nn(low, at(coupled[l])[...])).astype(bf)

        with phase(52):
            wait_mate(1)
        with phase(53):
            value = dot_nn(residual(1, 0, C, low), at(Z[1])[...])
            value = value + dot_nn(residual(1, 1, Cm, low), at(Zm[1])[...])
            at(xp1)[...] = value.astype(bf)
            counted(at(xp1), at(xr1), plane, at(xr1r), z, flipped(c, 2))
        side = chip % 2
        @pl.when(border)
        def _():
            with phase(56):
                settle_all(1, 2)
                forward(1, 2)
        with phase(54):
            early = dot_nn(low, at(table[1])[side, S[1]:, :])
            arrived(at(xr1), at(xr1r))
        with phase(55):
            value = (at(xp1)[...].astype(jnp.float32) + at(xr1)[...].astype(jnp.float32)).astype(bf)
            at(v[2])[...] = (dot_nn(value, at(table[1])[side, :S[1], :]) + early).astype(bf)
            at(x1)[...] = value
            low = at(v[2])[...]
        wait_mate(2)
        with phase(57):
            value = dot_nn(residual(2, 0, C, low), at(Z[2])[...])
            value = value + dot_nn(residual(2, 1, Cm, low), at(Zm[2])[...])
            at(x2)[...] = value.astype(bf)
            high = at(x2)[...]
        with phase(58):
            @pl.when(one_here)
            def _():
                for r in range(R):
                    at(f1)[r] = at(x1)[:, r * K[1]:(r + 1) * K[1]]
                leave(1, lambda r: at(f1).at[r], placed(1, core * NH), one_to)

            def two_piece(r):
                return at(x2).at[:, pl.ds(pl.multiple_of(r * K[2], 128), K[2])]

            leave(2, two_piece, placed(2, half * N + core * NH), two_to)
        with phase(59):
            wait_mate(3)
        with phase(60):
            for mate in range(2):
                below = dot_nn(high, at(folded3)[mate, :S[2], :])
                below = below + dot_nn(low, at(folded3)[mate, S[2]:, :])
                below = (at(yb[3])[mate].astype(jnp.float32) - below).astype(bf)
                value = dot_nt(below, at((Z, Zm)[mate][3])[...]).astype(bf)
                for r in range(R):
                    piece = value[:, r * K[3]:(r + 1) * K[3]]
                    at(f3)[mate * R + r] = jnp.concatenate([piece[:NH // 2], piece[NH // 2:]], axis=1)
            low_row = pl.multiple_of((z * N + core * NH) // 2, 16)
            leaf_out = outs[3].at[pl.ds(low_row, NH // 2)]
            for mate in range(2):
                leave(3, lambda r: at(f3).at[mate * R + r], leaf_out, flipped(c, mate), mate == 0)
        with phase(61):
            for l in levels:
                drain(0, l)
                if l:
                    drain(1, l)
                drain_rhs(l)
                if l < 3:
                    drain_spread(l)

            @pl.when(middle)
            def _():
                for l in lower:
                    arrived(at(y[l]).at[pl.ds(0, 3)], at(ys[l]))
                take(at(inner), sent[inner])
            take(at(plane), sent[plane])
            joined = [shape for shape in z_shape + c_shape[1:] if shape[1] % 128 == 0]
            take(at(mates), sum(elements(shape) for shape in joined))
            for shape, copy in zip(c_shape[1:], Cm[1:]):
                if shape[1] % 128:
                    arrived(at(copy), at(mates1))

            @pl.when(jnp.logical_not(kept_here))
            def _():
                arrived(at(u[1]).at[child, q], at(beside))

            @pl.when(top_here)
            def _():
                arrived(at(x0).at[:, pl.ds(0, S[0] - K[0])], at(Os[0]))

            @pl.when(jnp.logical_and(one_here, one_to == c))
            def _():
                arrived(at(f1).at[pl.ds(0, R - 1)], at(Os[1]))

            @pl.when(jnp.logical_and(one_here, one_to != c))
            def _():
                arrived(at(f1), at(Os[1]))

            @pl.when(two_to == c)
            def _():
                arrived(at(x2).at[:, pl.ds(0, S[2] - K[2])], at(Os[2]))

            @pl.when(two_to != c)
            def _():
                arrived(at(x2), at(Os[2]))
            arrived(at(f3).at[pl.ds(0, 2 * R - 1)], at(Os[3]))
        with phase(62):
            for l in levels:
                arrived(outs[l], at(Or[l]))

    return kernel, scratch


def hand_on(turned, *refs):
    given, results, staged, made = refs[:4], refs[4:8], refs[8:12], refs[12:16]
    arriving, leaving = refs[16], refs[17]
    copies = []
    for i in (3, 2, 1, 0):
        if turned[i]:
            pltpu.make_async_copy(given[i], staged[i], arriving.at[i]).start()
        else:
            copies.append(pltpu.make_async_copy(given[i], results[i], leaving.at[i]))
            copies[-1].start()
    for i in (3, 2):
        pltpu.make_async_copy(given[i], staged[i], arriving.at[i]).wait()
        rows, lanes = staged[i].shape
        both = dot_nt(eye(lanes), staged[i][...]).astype(made[i].dtype)
        if made[i].shape != (lanes, rows):
            pieces = []
            for low in range(0, rows, 16):
                pieces += [both[:lanes // 2, low:low + 16], both[lanes // 2:, low:low + 16]]
            both = jnp.concatenate(pieces, axis=1)
        made[i][...] = both
        copies.append(pltpu.make_async_copy(made[i], results[i], leaving.at[i]))
        copies[-1].start()
    for copy in copies:
        copy.wait()


def fused_device(*blocks):
    plan = Plan(
        lax.axis_size("row"), lax.axis_size("col"),
        [block.shape for block in blocks[:4]], blocks[7].shape,
        [block.shape for block in blocks[11:14]],
    )
    if not plan.fits():
        return per_device(*blocks)
    kernel, scratch = build_kernel(plan)
    blocks = list(blocks)
    for at in (0, 1, 2, 3, 7, 8, 9, 10):
        if narrow(blocks[at].shape[1]):
            blocks[at] = blocks[at].T
    blocks = [pltpu.with_memory_space_constraint(block, pltpu.HBM) for block in blocks]
    anywhere = pl.BlockSpec(memory_space=pltpu.HBM)
    solved = pl.pallas_call(
        kernel,
        out_shape=tuple(
            jax.ShapeDtypeStruct(shape, blocks[0].dtype) for shape in plan.result_shapes()
        ),
        in_specs=[anywhere] * 14,
        out_specs=(pl.BlockSpec(memory_space=pl.ANY),) * 4,
        scratch_shapes=scratch,
        compiler_params=pltpu.CompilerParams(
            collective_id=0, has_side_effects=True, vmem_limit_bytes=VMEM_LIMIT
        ),
    )(*blocks)
    turned = [not narrow(width) for width in plan.width]
    final = [
        (strip, width) if turn else (width, strip)
        for width, strip, turn in zip(plan.width, plan.strip, turned)
    ]
    solved = pl.pallas_call(
        functools.partial(hand_on, turned),
        out_shape=tuple(jax.ShapeDtypeStruct(shape, blocks[0].dtype) for shape in final),
        in_specs=[pl.BlockSpec(memory_space=pl.ANY)] * 4,
        out_specs=(pl.BlockSpec(memory_space=pltpu.HBM),) * 4,
        scratch_shapes=[pltpu.VMEM(block.shape, block.dtype) for block in solved]
        + [pltpu.VMEM(shape, blocks[0].dtype) for shape in final]
        + [pltpu.SemaphoreType.DMA((4,))] * 2,
        compiler_params=pltpu.CompilerParams(vmem_limit_bytes=2**20),
    )(*solved)
    return tuple(block if turn else block.T for block, turn in zip(solved, turned))


def solution(mesh):
    in_specs = (
        P("col", "row"),
        P("col", "row"),
        P("col", "row"),
        P("col", "row"),
        P("row", "col"),
        P("row", "col"),
        P("row", "col"),
        P("row", "col"),
        P("row", "col"),
        P("row", "col"),
        P("row", "col"),
        P(),
        P(),
        P(),
    )
    out_specs = (P("row", "col"), P("row", "col"), P("row", "col"), P("row", "col"))
    return jax.shard_map(
        fused_device, mesh=mesh, in_specs=in_specs, out_specs=out_specs, check_vma=False
    )
```

```python
import functools

import jax
import jax.numpy as jnp
from jax import lax
from jax.experimental import pallas as pl
from jax.experimental.pallas import tpu as pltpu
from jax.sharding import PartitionSpec as P


def swapped(value, axis, stride):
    mask = 2**stride
    pairs = [(source, source ^ mask) for source in range(lax.axis_size(axis))]
    return lax.ppermute(value, axis, pairs)


def route_tables(mapping, child_index, parent_sep, parent_upd, strips, row_index):
    positions = lax.dynamic_index_in_dim(mapping, child_index, 0, keepdims=False)
    sep_rows = parent_sep // strips
    in_separator = positions < parent_sep
    if parent_upd > 0:
        upd_rows = parent_upd // strips
        target = jnp.where(
            in_separator, positions // sep_rows, (positions - parent_sep) // upd_rows
        )
        offset = jnp.where(
            in_separator, positions % sep_rows, sep_rows + (positions - parent_sep) % upd_rows
        )
    else:
        target = positions // sep_rows
        offset = positions % sep_rows
    block_rows = positions.shape[0] // strips
    blocks = target.reshape(strips, block_rows)
    matches = (blocks[:, :, None] == jnp.arange(strips, dtype=jnp.int32)[None, None, :]).astype(
        jnp.int32
    )
    slot_of = jnp.sum((jnp.cumsum(matches, axis=1) - 1) * matches, axis=2).reshape(-1)
    block_len = sep_rows + parent_upd // strips
    capacity = 2 * positions.shape[0] // (strips * strips)
    source = jnp.arange(positions.shape[0], dtype=jnp.int32) // block_rows
    mine_here = target == row_index
    column_at = jnp.where(mine_here, slot_of, capacity)
    lookup = jnp.full((strips, capacity + 1), block_len, jnp.int32)
    lookup = lookup.at[source, column_at].set(jnp.where(mine_here, offset, block_len))[:, :capacity]
    local_target = lax.dynamic_slice_in_dim(target, row_index * block_rows, block_rows)
    local_slots = lax.dynamic_slice_in_dim(slot_of, row_index * block_rows, block_rows)
    return (local_target, local_slots, lookup, capacity, block_len)


def pack_rows(values, local_target, local_slots, strips, capacity):
    buffer = jnp.zeros((strips, capacity, values.shape[1]), values.dtype)
    return buffer.at[local_target, local_slots].set(values)


def unpack_rows(received, lookup, block_len):
    summed = jnp.zeros((block_len + 1, received.shape[2]), jnp.float32)
    return summed.at[lookup].add(received.astype(jnp.float32))[:block_len]


def spread(portion, depth_bits, pass_on, column):
    for bit_index in range(depth_bits):
        partner = pass_on(portion, bit_index)
        is_upper = column >> bit_index & 1 == 1
        portion = jnp.where(
            is_upper,
            jnp.concatenate([partner, portion], axis=-1),
            jnp.concatenate([portion, partner], axis=-1),
        )
    return portion


def shrink(entire, depth_bits, pass_on, column):
    for bit_index in reversed(range(depth_bits)):
        half_width = entire.shape[-1] // 2
        low_part = entire[..., :half_width]
        high_part = entire[..., half_width:]
        is_upper = column >> bit_index & 1 == 1
        kept_part = jnp.where(is_upper, high_part, low_part)
        sent_part = jnp.where(is_upper, low_part, high_part)
        entire = kept_part + pass_on(sent_part, bit_index)
    return entire


def per_device(
    inverse_top,
    inverse_one,
    inverse_two,
    inverse_leaf,
    coupling_one,
    coupling_two,
    coupling_leaf,
    rhs_top,
    rhs_one,
    rhs_two,
    rhs_leaf,
    parent_map_one,
    parent_map_two,
    parent_map_leaf,
):
    strips = lax.axis_size("row")
    col_count = lax.axis_size("col")
    row_here = lax.axis_index("row")
    column = lax.axis_index("col")
    inverses = [inverse_top, inverse_one, inverse_two, inverse_leaf]
    couplings = [None, coupling_one, coupling_two, coupling_leaf]
    right_sides = [rhs_top, rhs_one, rhs_two, rhs_leaf]
    parent_maps = [None, parent_map_one, parent_map_two, parent_map_leaf]
    orders = [inverse.shape[1] * strips for inverse in inverses]
    groups = [col_count >> tree_level for tree_level in range(4)]
    group_bits = [group_size.bit_length() - 1 for group_size in groups]
    pass_rhs = lambda values, bit_index: swapped(values, "col", bit_index)
    pass_update_sum = lambda values, bit_index: swapped(
        values.astype(jnp.bfloat16), "col", bit_index
    ).astype(values.dtype)
    pass_update_spread = lambda values, bit_index: swapped(values, "col", bit_index)
    pass_solution_sum = lambda values, bit_index: swapped(
        values.astype(jnp.bfloat16), "col", bit_index
    ).astype(values.dtype)
    pass_solution_spread = lambda values, bit_index: swapped(values, "col", bit_index)
    full_rhs = [
        spread(right_sides[tree_level], group_bits[tree_level], pass_rhs, column)
        for tree_level in range(4)
    ]
    own_routes = [None]
    for tree_level in range(1, 4):
        parent_order = orders[tree_level - 1]
        parent_update = parent_order if tree_level > 1 else 0
        front_here = column // groups[tree_level]
        own_routes.append(
            route_tables(
                parent_maps[tree_level], front_here, parent_order, parent_update, strips, row_here
            )
        )
    pivots = [None] * 4
    incoming = None
    for tree_level in (3, 2, 1, 0):
        sep_rows = inverses[tree_level].shape[1]
        if incoming is None:
            separator = full_rhs[tree_level]
            own_update = None
        else:
            separator = (full_rhs[tree_level].astype(jnp.float32) + incoming[:sep_rows]).astype(
                jnp.bfloat16
            )
            own_update = lax.optimization_barrier(incoming[sep_rows:].astype(jnp.bfloat16))
        partial_value = jnp.dot(inverses[tree_level], separator, preferred_element_type=jnp.float32)
        solved = lax.psum(partial_value.astype(jnp.bfloat16), "row")
        pivots[tree_level] = solved
        if tree_level > 0:
            coupled = jnp.dot(couplings[tree_level], solved, preferred_element_type=jnp.float32)
            reduced = shrink(coupled, group_bits[tree_level], pass_update_sum, column)
            if own_update is None:
                portion = (-reduced).astype(jnp.bfloat16)
            else:
                start_at = column % groups[tree_level] * reduced.shape[1]
                kept_rows = lax.dynamic_slice_in_dim(own_update, start_at, reduced.shape[1], 1)
                portion = (kept_rows.astype(jnp.float32) - reduced).astype(jnp.bfloat16)
            updated = spread(portion, group_bits[tree_level], pass_update_spread, column)
            own_target, own_slots, own_lookup, capacity, block_len = own_routes[tree_level]
            got_own = lax.all_to_all(
                pack_rows(updated, own_target, own_slots, strips, capacity),
                "row",
                split_axis=0,
                concat_axis=0,
                tiled=True,
            )
            own_part = unpack_rows(got_own, own_lookup, block_len)
            partner = swapped(own_part.astype(jnp.bfloat16), "col", group_bits[tree_level])
            incoming = own_part + partner.astype(jnp.float32)
    solutions = [None] * 4
    parent_solution = None
    parent_gathered = None
    for tree_level in range(4):
        solved = pivots[tree_level]
        gathered = None
        if tree_level == 0:
            residual = solved
        else:
            own_target, own_slots, own_lookup, capacity, block_len = own_routes[tree_level]
            pieces = [parent_solution]
            if parent_gathered is not None:
                pieces.append(parent_gathered)
            pieces.append(jnp.zeros((1, parent_solution.shape[1]), jnp.bfloat16))
            parent_rows = jnp.concatenate(pieces, axis=0)
            returned = lax.all_to_all(
                parent_rows[own_lookup], "row", split_axis=0, concat_axis=0, tiled=True
            )
            gathered = returned[own_target, own_slots]
            coupling_term = jnp.dot(
                couplings[tree_level].T, gathered, preferred_element_type=jnp.float32
            )
            residual = (
                solved.astype(jnp.float32)
                - lax.psum(coupling_term.astype(jnp.bfloat16), "row").astype(jnp.float32)
            ).astype(jnp.bfloat16)
        contribution = jnp.dot(inverses[tree_level].T, residual, preferred_element_type=jnp.float32)
        if tree_level == 0:
            summed = lax.psum(contribution.astype(jnp.bfloat16), "col")
            solution = summed
            rhs_width = solution.shape[1] // groups[0]
            solutions[0] = lax.dynamic_slice_in_dim(
                solution, column % groups[0] * rhs_width, rhs_width, 1
            )
        else:
            portion = shrink(
                contribution, group_bits[tree_level], pass_solution_sum, column
            ).astype(jnp.bfloat16)
            solutions[tree_level] = portion
            if tree_level < 3:
                solution = spread(portion, group_bits[tree_level], pass_solution_spread, column)
        parent_solution = solution
        parent_gathered = gathered
    return (solutions[0], solutions[1], solutions[2], solutions[3])


MESH = pl.DeviceIdType.MESH
VMEM_LIMIT = 32 * 2**20


def dot_nn(left, right):
    return lax.dot_general(left, right, (((1,), (0,)), ((), ())), preferred_element_type=jnp.float32)


def dot_nt(left, right):
    return lax.dot_general(left, right, (((1,), (1,)), ((), ())), preferred_element_type=jnp.float32)


def eye(size):
    rows = lax.broadcasted_iota(jnp.int32, (size, size), 0)
    columns = lax.broadcasted_iota(jnp.int32, (size, size), 1)
    return jnp.where(rows == columns, 1.0, 0.0).astype(jnp.bfloat16)


def flipped(value, mask):
    result = value
    bit = 1
    while bit <= mask:
        if mask & bit:
            result = result + bit * (1 - 2 * ((value // bit) % 2))
        bit *= 2
    return result


class Plan:
    def __init__(self, rows, cols, inverse_shapes, rhs_top_shape, map_shape):
        self.rows, self.cols = rows, cols
        self.strip = [shape[1] for shape in inverse_shapes]
        self.order = [shape[1] * rows for shape in inverse_shapes]
        self.local = [shape[0] for shape in inverse_shapes]
        self.group = [cols >> level for level in range(4)]
        self.columns = rhs_top_shape[1] * cols
        self.width = [self.columns // group if group else 0 for group in self.group]
        self.mine = self.columns // rows
        self.map_shape = map_shape

    def total(self, level):
        return self.order[level] * (2 if level else 1)

    def result_shapes(self):
        shapes = list(zip(self.width, self.strip))
        return shapes[:3] + [(self.width[3] // 2, 2 * self.strip[3])]

    def span_rows(self):
        n, order, width = self.mine, self.order, self.width
        shared = 3 * (n // 4) * order[1] + 3 * (n // 2) * order[0] + n // 2 * order[1]
        inner = 2 * n * order[3] + 4 * n * order[2] + 8 * (n // 4) * order[1]
        joined = sum(2 * order[level] * self.local[level] for level in (2, 3))
        joined += sum(order[level] * self.local[level] for level in (0, 1))
        return max(shared, inner, joined, 9 * n * order[1], 3 * width[0] * order[0], 3 * n * order[2]) // 128

    def fits(self):
        table = sum(
            2 * self.total(level) * self.order[level + 1] * 2 for level in range(3)
        )
        if self.rows != 4 or self.group[3] != 1 or self.mine * self.rows != self.columns or table > 24 * 2**20:
            return False
        if self.group != [8, 4, 2, 1] or self.mine % 64:
            return False
        for level in range(4):
            if self.strip[level] % 64 or self.order[level] % 128 or self.local[level] % 64:
                return False
        if not packed((self.mine, self.strip[1])):
            return False
        return narrow(self.strip[3]) and not any(narrow(strip) for strip in self.strip[:3])


def elements(shape):
    count = 1
    for extent in shape:
        count *= extent
    return count


def packed(shape):
    return shape[1] > 128 and shape[1] % 128 == 64


def packed_shape(shape):
    return (shape[0] * (shape[1] // 128) + shape[0] // 2, 128)


def narrow(size):
    return size < 128


def phase(number):
    return jax.named_scope(str(number))


def build_kernel(plan):
    R, CC, N = plan.rows, plan.cols, plan.mine
    S, K, L, G, W = plan.order, plan.strip, plan.local, plan.group, plan.width
    N2, NH, NQ, chips = 2 * N, N // 2, N // G[1], G[0] // 2
    bf = jnp.bfloat16
    scratch = []

    def ref(shape, dtype=bf):
        scratch.append(pltpu.VMEM(shape, dtype))
        return len(scratch) - 1

    def sems(*shape):
        scratch.append(pltpu.SemaphoreType.DMA(shape) if shape else pltpu.SemaphoreType.DMA)
        return len(scratch) - 1

    levels, lower = range(4), (1, 2, 3)
    z_shape = [(S[3], L[3]) if l == 3 else (L[l], S[l]) for l in levels]
    c_shape = [None] + [(S[l], L[l]) for l in lower]
    Z = [ref(z_shape[l]) for l in levels]
    C = [None] + [ref(c_shape[l]) for l in lower]
    Zm = [ref(z_shape[l]) for l in levels]
    Cm = [None] + [ref(c_shape[l]) for l in lower]
    Zp = [ref((R,) + packed_shape((L[l], K[l]))) if l < 3 and packed((L[l], K[l])) else None for l in levels]
    Cp = [None] + [ref((R,) + packed_shape((K[l], L[l]))) if packed((K[l], L[l])) else None for l in lower]
    Zraw = [ref((L[l], K[l])) if Zp[l] is not None else None for l in levels]
    Craw = [None] + [ref((K[l], L[l])) if Cp[l] is not None else None for l in lower]
    Zr, Zs = [sems() for _ in levels], [sems() for _ in levels]
    Cr, Cs = [None] + [sems() for _ in lower], [None] + [sems() for _ in lower]
    Zmr, Cmr, mates, mates1 = [sems() for _ in levels], [None] + [sems() for _ in lower], sems(), sems()
    table = [ref((2, plan.total(l), S[l + 1])) for l in range(3)]
    held_map = [None] + [ref(plan.map_shape[l - 1], jnp.int32) for l in lower]
    local = sems(6)
    B = [ref((NH, S[0])), ref((2, R) + packed_shape((N, K[1]))), ref((S[2], N2)), ref((S[3], N2))]
    B1, rhs_raw, rhs_packed = ref((N2, S[1])), ref((N, K[1])), ref(packed_shape((N, K[1])))
    Bs, Br = [sems() for _ in levels], [sems() for _ in levels]
    Ds, Dr = [sems(), sems(), sems()], [sems(), sems(2), sems()]
    y = [None] + [ref((4, NH, L[l])) for l in lower]
    yb = [None] + [ref((2, NH, L[l])) for l in lower]
    ys, yr = [None] + [sems() for _ in lower], [None] + [sems() for _ in lower]
    u = [None, ref((2, G[1], NQ, S[1])), ref((2, 2, G[1], NQ, S[2])), ref((2, N2, S[3]))]
    ur, ur1 = [None, None, sems(), sems()], sems(2)
    f0 = ref((NH, S[0]), jnp.float32)
    up1, ut1, ut1r = ref((2, G[1], NQ, S[1])), ref((G[1], NQ, S[1])), sems()
    h1 = ref((2, NQ, S[1]))
    folded, early1 = ref((2, L[1], S[2])), ref((N2, L[1]), jnp.float32)
    up2, ut2, ut2r = ref((2, N, S[2])), ref((N, S[2])), sems()
    xp0, xr0, xr0r = ref((NH, S[0])), ref((chips, NH, S[0])), sems()
    x0 = ref((NH, S[0]))
    xp1, xr1, xr1r = ref((NH, S[1])), ref((NH, S[1])), sems()
    v = [None] + [ref((NH, S[l])) for l in (1, 2)]
    x1, x2 = ref((NH, S[1])), ref((NH, S[2]))
    f1, f3 = ref((R, NH, K[1])), ref((2 * R, NH // 2, 2 * K[3]))
    folded3, folded1 = ref((2, 2 * S[2], L[3])), ref((2, S[0], L[1]))
    Os, Or = [sems() for _ in levels], [sems() for _ in levels]
    plane, inner, beside = sems(), sems(), sems()
    scratch.append(pltpu.SemaphoreType.REGULAR)
    ready = len(scratch) - 1
    scratch.append(pltpu.SemaphoreType.REGULAR)
    ready_group = len(scratch) - 1
    span = ref((plan.span_rows(), 128))

    def kernel(*refs):
        inverse = refs[0:4]
        coupling = (None,) + tuple(refs[4:7])
        rhs = refs[7:11]
        maps = (None,) + tuple(refs[11:14])
        outs = refs[14:18]
        held = refs[18:]
        at = lambda index: held[index]
        z = lax.axis_index("row")
        c = lax.axis_index("col")
        core, chip = c % 2, c // 2
        middle = jnp.logical_and(z > 0, z < R - 1)
        border = jnp.logical_not(middle)
        half = z % 2
        pair = z + 1 - 2 * half
        across = R - 1 - z
        beyond = R - 1 - pair
        sent = {}

        def remote(src, dst, ssem, rsem, z_to, c_to):
            return pltpu.make_async_remote_copy(
                src_ref=src, dst_ref=dst, send_sem=ssem, recv_sem=rsem,
                device_id=(z_to, c_to), device_id_type=MESH,
            )

        def push(src, dst, ssem, rsem, z_to, c_to):
            remote(src, dst, ssem, rsem, z_to, c_to).start()

        def counted(src, dst, index, rsem, z_to, c_to):
            push(src, dst, at(index), rsem, z_to, c_to)
            sent[index] = sent.get(index, 0) + elements(src.shape)

        def arrived(dst, rsem):
            pltpu.make_async_copy(dst, dst, rsem).wait()

        def take(sem, count):
            view = at(span).at[pl.ds(0, count // 128)]
            pltpu.make_async_copy(view, view, sem).wait()

        barrier = pltpu.get_barrier_semaphore()
        group_here = [(z, flipped(c, m)) for m in range(1, G[1])]
        opposite = (z, flipped(c, G[1]))

        def greet(semaphore, *friends):
            for friend in friends:
                pl.semaphore_signal(semaphore, inc=1, device_id=friend, device_id_type=MESH)

        greet(barrier, (pair, c))

        @pl.when(middle)
        def _():
            greet(barrier, (across, c), (beyond, c), *group_here)

        @pl.when(border)
        def _():
            greet(barrier, opposite)

        raws = [(rhs[1], at(rhs_raw))]
        for l in levels:
            if Zp[l] is not None:
                raws.append((inverse[l], at(Zraw[l])))
            if l and Cp[l] is not None:
                raws.append((coupling[l], at(Craw[l])))
        loads = raws + [(maps[l], at(held_map[l])) for l in lower]
        for i, (src, dst) in enumerate(loads):
            pltpu.make_async_copy(src, dst, at(local).at[i]).start()

        def slot(kind, l, r):
            if kind == 0:
                if Zp[l] is not None:
                    return at(Zp[l]).at[r], at(Zr[l])
                if l == 3:
                    low = pl.multiple_of(r * K[l], 16)
                    return at(Z[l]).at[pl.ds(low, K[l])], at(Zr[l])
                low = pl.multiple_of(r * K[l], 128)
                return at(Z[l]).at[:, pl.ds(low, K[l])], at(Zr[l])
            if Cp[l] is not None:
                return at(Cp[l]).at[r], at(Cr[l])
            low = pl.multiple_of(r * K[l], 16)
            return at(C[l]).at[pl.ds(low, K[l])], at(Cr[l])

        def is_packed(kind, l):
            return (Zp, Cp)[kind][l] is not None

        def source(kind, l):
            if is_packed(kind, l):
                return slot(kind, l, z)[0]
            return (inverse, coupling)[kind][l]

        def send_sem(kind, l):
            return at((Zs, Cs)[kind][l])

        def own_load(kind, l):
            if not is_packed(kind, l):
                dst, sem = slot(kind, l, z)
                pltpu.make_async_copy(source(kind, l), dst, sem).start()

        def own_send(kind, l):
            dst, sem = slot(kind, l, z)
            push(source(kind, l), dst, send_sem(kind, l), sem, jnp.where(middle, across, pair), c)

            @pl.when(border)
            def _():
                push(source(kind, l), dst, send_sem(kind, l), sem, beyond, c)

        def own_out(kind, l):
            dst, sem = slot(kind, l, z)
            push(source(kind, l), dst, send_sem(kind, l), sem, pair, c)

        def pass_on(kind, l, origins=(across, beyond)):
            for r in origins:
                dst, sem = slot(kind, l, r)
                push(dst, dst, send_sem(kind, l), sem, pair, c)

        def settle_all(kind, l):
            rsem = slot(kind, l, z)[1]
            if is_packed(kind, l):
                arrived(at((Zp, Cp)[kind][l]).at[pl.ds(0, R - 1)], rsem)
                unpack(kind, l)
            else:
                arrived(at((Z, C)[kind][l]), rsem)

        def unpacked(block, rows, lanes):
            whole = lanes // 128 * rows
            rest = block[whole:]
            rest = jnp.concatenate([rest[:, :lanes % 128], rest[:, lanes % 128:]], axis=0)
            return jnp.concatenate([block[i:i + rows] for i in range(0, whole, rows)] + [rest], axis=1)

        def unpack(kind, l):
            rows, lanes = (L[l], K[l]) if kind == 0 else (K[l], L[l])
            for r in range(R):
                value = unpacked(at((Zp, Cp)[kind][l])[r], rows, lanes)
                if kind == 0:
                    at(Z[l])[:, r * lanes:(r + 1) * lanes] = value
                else:
                    at(C[l])[r * rows:(r + 1) * rows, :] = value

        def pack(raw):
            value = raw[...]
            rows, lanes = value.shape
            whole = lanes - lanes % 128
            pieces = [value[:, i:i + 128] for i in range(0, whole, 128)]
            rest = value[:, whole:]
            rest = jnp.concatenate([rest[:rows // 2], rest[rows // 2:]], axis=1)
            return jnp.concatenate(pieces + [rest], axis=0)

        def drain(kind, l):
            if is_packed(kind, l):
                whole = at((Zp, Cp)[kind][l])
                part = whole.at[pl.ds(0, R // 2)]
            else:
                whole = at((Z, C)[kind][l])
                if kind == 0 and l < 3:
                    part = whole.at[:, pl.ds(0, S[l] // 2)]
                else:
                    part = whole.at[pl.ds(0, S[l] // 2)]

            @pl.when(middle)
            def _():
                arrived(whole, send_sem(kind, l))

            @pl.when(border)
            def _():
                arrived(part, send_sem(kind, l))

        def rhs_pieces(l):
            q = c % G[l]
            if l == 3:
                return [
                    (rhs[3].at[:, pl.ds(i * N2, N2)], at(B[3]).at[pl.ds(pl.multiple_of(z * K[3], 16), K[3])], 1 + i)
                    for i in range(2)
                ]
            if l == 2:
                return [(rhs[2], at(B[2]).at[pl.ds(pl.multiple_of(z * K[2], 16), K[2])], 1 + q)]
            if l == 1:
                return [(at(rhs_packed), at(B[1]).at[q % 2, z], 1 + q // 2)]
            lanes = pl.ds(pl.multiple_of(z * K[0], 128), K[0])
            return [(rhs[0], at(B[0]).at[:, lanes], q // 2)]

        def start_rhs(l):
            for src, dst, z_to in rhs_pieces(l):
                @pl.when(z_to == z)
                def _():
                    pltpu.make_async_copy(src, dst, at(Br[l])).start()

                @pl.when(z_to != z)
                def _():
                    push(src, dst, at(Bs[l]), at(Br[l]), z_to, c)

        def drain_rhs(l):
            pieces = rhs_pieces(l)
            if l == 3:
                @pl.when(middle)
                def _():
                    arrived(at(B[3]).at[pl.ds(0, K[3])], at(Bs[3]))

                @pl.when(border)
                def _():
                    arrived(at(B[3]).at[pl.ds(0, 2 * K[3])], at(Bs[3]))
                return
            src, dst, z_to = pieces[0]

            @pl.when(z_to != z)
            def _():
                arrived(dst, at(Bs[l]))

        def rhs_spread(l):
            q = c % G[l]
            if l == 2:
                return z == 1 + q, at(B[2]), at(Dr[2])
            if l == 1:
                return z == 1 + q // 2, at(B[1]).at[q % 2], at(Dr[1]).at[q % 2]
            return z == q // 2, at(B[0]), at(Dr[0])

        def spread_rhs(l):
            holds, here, rsem = rhs_spread(l)

            @pl.when(holds)
            def _():
                arrived(here, at(Br[l]))
                for m in range(2, CC, 2) if l == 0 else range(1, G[l]):
                    push(here, here, at(Ds[l]), rsem, z, flipped(c, m))

        def drain_spread(l):
            holds, here, _ = rhs_spread(l)

            @pl.when(holds)
            def _():
                take(at(Ds[l]), (chips - 1, G[1] - 1, 1)[l] * elements(here.shape))

        def wait_rhs(l):
            holds, here, rsem = rhs_spread(l)
            if l != 1:
                @pl.when(jnp.logical_not(holds))
                def _():
                    arrived(here, rsem)
                return
            for part in range(2):
                @pl.when(jnp.logical_not(jnp.logical_and(holds, c % 2 == part)))
                def _():
                    arrived(at(B[1]).at[part], at(Dr[1]).at[part])

        def make_table(l):
            front = c // G[l]
            step = K[l]
            for child in range(2):
                row = at(held_map[l + 1])[pl.ds(2 * front + child, 1), :]

                def body(i, carry):
                    start = pl.multiple_of(i * step, 16)
                    at_row = lax.broadcasted_iota(jnp.int32, (step, S[l + 1]), 0) + start
                    at(table[l])[child, pl.ds(start, step), :] = jnp.where(
                        at_row == row, 1.0, 0.0
                    ).astype(bf)
                    return carry

                lax.fori_loop(0, plan.total(l) // step, body, 0)

        def gathered(l, low, size, first, second):
            value = dot_nt(first, at(table[l])[0, low:low + size, :])
            return value + dot_nt(second, at(table[l])[1, low:low + size, :])

        def forward(kind, l):
            own, copy = at((Z, C)[kind][l]), at((Zm, Cm)[kind][l])
            ssem = at(mates1 if own.shape[1] % 128 else mates)
            push(own, copy, ssem, at((Zmr, Cmr)[kind][l]), z, flipped(c, 1))

        def hand_over(l):
            at(yb[l])[0] = at(y[l])[2 * half + core]
            src = at(y[l]).at[2 * half + 1 - core]
            push(src, at(yb[l]).at[1], at(ys[l]), at(yr[l]), z, flipped(c, 1))
            src = at(y[l]).at[2 * (1 - half) + core]
            push(src, at(yb[l]).at[0], at(ys[l]), at(yr[l]), pair, c)
            src = at(y[l]).at[2 * (1 - half) + 1 - core]
            push(src, at(yb[l]).at[1], at(ys[l]), at(yr[l]), pair, flipped(c, 1))

        with phase(2):
            @pl.when(middle)
            def _():
                pl.semaphore_wait(barrier, G[1] + 1)

            @pl.when(border)
            def _():
                pl.semaphore_wait(barrier, 3)

        with phase(3):
            own_send(0, 3)
            start_rhs(3)
            own_send(1, 3)
            pltpu.make_async_copy(*loads[0], at(local).at[0]).wait()
            at(rhs_packed)[...] = pack(at(rhs_raw))
            start_rhs(2)
            start_rhs(1)
            own_send(0, 2)
            own_send(1, 2)
            for i, (src, dst) in enumerate(loads[1:]):
                pltpu.make_async_copy(src, dst, at(local).at[i + 1]).wait()
            for l in levels:
                if Zp[l] is not None:
                    at(Zp[l])[z] = pack(at(Zraw[l]))
                if l and Cp[l] is not None:
                    at(Cp[l])[z] = pack(at(Craw[l]))
            own_send(0, 1)
            own_send(1, 1)
            for l in levels:
                own_load(0, l)
                if l:
                    own_load(1, l)

            @pl.when(middle)
            def _():
                own_out(0, 0)
                for l in (3, 2, 1):
                    own_out(0, l)
                    own_out(1, l)

            @pl.when(border)
            def _():
                greet(at(ready), opposite)
                pl.semaphore_wait(at(ready), 1)
                greet(at(ready), (pair, c))

        def last_send(turn):
            @pl.when(turn)
            def _():
                own_send(0, 0)

        make_table(2)

        @pl.when(middle)
        def _():
            with phase(31):
                arrived(at(B[3]), at(Br[3]))
                right = dot_nt(eye(N2), at(B[3])[...]).astype(bf)
                settle_all(0, 3)
                start_rhs(0)
                last_send(core == 0)
                pl.semaphore_wait(at(ready), 1)
                greet(at(ready_group), *group_here)
            with phase(32):
                solved = dot_nn(right, at(Z[3])[...]).astype(bf)
                at(y[3])[...] = solved.reshape(4, NH, L[3])
                settle_all(1, 3)
            with phase(33):
                at(u[3])[core] = (-dot_nt(solved, at(C[3])[...])).astype(bf)
                here = at(u[3]).at[core]
                counted(here, here, inner, at(ur[3]), z, flipped(c, 1))
                pl.semaphore_wait(at(ready_group), G[1] - 1)
                greet(at(ready), (pair, c))
                pass_on(0, 3)
                pass_on(1, 3)
        spread_rhs(2)
        spread_rhs(1)
        make_table(1)

        @pl.when(middle)
        def _():
            with phase(21):
                arrived(at(u[3]).at[0], at(ur[3]))
                wait_rhs(2)
            with phase(22):
                pair_of = at(u[3])[0], at(u[3])[1]
                right = dot_nt(eye(N2), at(B[2])[...]) + gathered(2, 0, S[2], *pair_of)
                right = right.astype(bf)
                lower_part = pl.ds(pl.multiple_of(core * N, N), N)
                pair_of = at(u[3])[0, lower_part, :], at(u[3])[1, lower_part, :]
                kept = gathered(2, S[2], S[2], *pair_of)
            with phase(23):
                settle_all(0, 2)
                pass_on(0, 2)
            with phase(24):
                solved = dot_nt(right, at(Z[2])[...]).astype(bf)
                at(y[2])[...] = solved.reshape(4, NH, L[2])
            with phase(25):
                settle_all(1, 2)
            with phase(26):
                at(up2)[...] = dot_nt(solved, at(C[2])[...]).astype(bf).reshape(2, N, S[2])
                counted(at(up2).at[1 - core], at(ut2), inner, at(ut2r), z, flipped(c, 1))
            with phase(27):
                own = at(up2)[core].astype(jnp.float32)
                arrived(at(ut2), at(ut2r))
                own = kept - (own + at(ut2)[...].astype(jnp.float32))
                child = (c // G[2]) % 2
                at(u[2])[child, core] = own.astype(bf).reshape(G[1], NQ, S[2])
                here = at(u[2]).at[child, core]
                for m in (3, 2, 1):
                    counted(here, here, inner, at(ur[2]), z, flipped(c, m))
        make_table(0)
        q, child = c % G[1], (c // G[1]) % 2

        @pl.when(middle)
        def _():
            with phase(11):
                wait_rhs(1)
                for part in range(2):
                    for r in range(R):
                        value = unpacked(at(B[1])[part, r], N, K[1])
                        at(B1)[part * N:(part + 1) * N, r * K[1]:(r + 1) * K[1]] = value
            with phase(14):
                settle_all(0, 1)
                pass_on(0, 1)
            with phase(10):
                at(early1)[...] = dot_nt(at(B1)[...], at(Z[1])[...])
                for i in range(2):
                    at(folded)[i] = dot_nn(at(Z[1])[...], at(table[1])[i, :S[1], :]).astype(bf)
            with phase(12):
                take(at(ur[2]), 3 * N * S[2])
            with phase(13):
                pair_of = [at(u[2])[i].reshape(N2, S[2]) for i in range(2)]
                solved = at(early1)[...]
                for i in range(2):
                    solved = solved + dot_nt(pair_of[i], at(folded)[i])
                solved = solved.astype(bf)
                at(y[1])[...] = solved.reshape(4, NH, L[1])
            with phase(16):
                settle_all(1, 1)
            with phase(17):
                def couple(part):
                    rows = at(y[1])[pl.ds(pl.multiple_of(2 * part, 2), 2)].reshape(N, L[1])
                    value = dot_nt(rows, at(C[1])[...]).astype(bf)
                    at(up1)[part] = value.reshape(G[1], NQ, S[1])

                couple(1 - half)
                for m in (3, 2, 1):
                    src = at(up1).at[1 - half, flipped(q, m)]
                    counted(src, at(ut1).at[m], inner, at(ut1r), pair, flipped(c, m))
                couple(half)
                for m in (3, 2, 1):
                    src = at(up1).at[half, flipped(q, m)]
                    counted(src, at(ut1).at[m], inner, at(ut1r), z, flipped(c, m))
                last_send(core == 1)
                pair_of = [at(u[2])[i, :, q].reshape(2 * NQ, S[2]) for i in range(2)]
                kept = gathered(1, S[1], S[1], *pair_of)
                at(h1)[...] = kept.astype(bf).reshape(2, NQ, S[1])
                at(up1)[1 - half, q] = (
                    at(up1)[1 - half, q].astype(jnp.float32) - at(h1)[1 - half].astype(jnp.float32)
                ).astype(bf)
                counted(at(up1).at[1 - half, q], at(ut1).at[0], inner, at(ut1r), pair, c)
                spread_rhs(0)
                settle_all(0, 0)
                pass_on(0, 0)
                pass_on(1, 1)
                hand_over(1)
                pass_on(1, 2)
                hand_over(2)
                hand_over(3)
                forward(0, 0)

        @pl.when(border)
        def _():
            with phase(18):
                pl.semaphore_wait(at(ready), 1)
                for kind, l in ((0, 3), (1, 3), (0, 2)):
                    settle_all(kind, l)
                    if (kind, l) == (0, 3):
                        start_rhs(0)
                    if (kind, l) != (1, 3):
                        last_send(core == (0 if l == 3 else 1))
                    forward(kind, l)
                spread_rhs(0)
                arrived(at(ut1), at(ut1r))
                value = at(ut1)[0].astype(jnp.float32)
                for m in range(1, G[1]):
                    value = value + at(ut1)[m].astype(jnp.float32)
                at(u[1])[child, q] = (-value).astype(bf)

        @pl.when(middle)
        def _():
            with phase(19):
                value = at(up1)[half, q].astype(jnp.float32)
                arrived(at(ut1).at[pl.ds(1, G[1] - 1)], at(ut1r))
                for m in range(1, G[1]):
                    value = value + at(ut1)[m].astype(jnp.float32)
                at(u[1])[child, q] = (at(h1)[half].astype(jnp.float32) - value).astype(bf)
        here = at(u[1]).at[child, q]
        kept_here = q // 2 == core
        for m in (6, 4, 2):
            rsem = at(ur1).at[0 if m == 2 else 1]
            counted(here, here, plane, rsem, z, flipped(2 * chip + q // 2, m))

        @pl.when(jnp.logical_not(kept_here))
        def _():
            push(here, here, at(beside), at(ur1).at[0], z, flipped(c, 1))

        @pl.when(border)
        def _():
            with phase(40):
                settle_all(0, 0)
                forward(0, 0)

        @pl.when(middle)
        def _():
            with phase(20):
                for l in lower:
                    for kind in range(2):
                        forward(kind, l)
        with phase(41):
            @pl.when(kept_here)
            def _():
                take(at(ur1).at[0], NQ * S[1])

            @pl.when(jnp.logical_not(kept_here))
            def _():
                take(at(ur1).at[0], 2 * NQ * S[1])
            wait_rhs(0)
        columns = pl.ds(pl.multiple_of(2 * core, 2), 2)
        with phase(42):
            part = dot_nt(at(u[1])[child, columns].reshape(NH, S[1]), at(table[0])[child])
            at(f0)[...] = at(B[0])[...].astype(jnp.float32) + part
            take(at(ur1).at[1], 2 * NQ * S[1])
        with phase(49):
            part = dot_nt(at(u[1])[1 - child, columns].reshape(NH, S[1]), at(table[0])[1 - child])
            right = (at(f0)[...] + part).astype(bf)
        with phase(43):
            arrived(at(Zm[0]), at(Zmr[0]))
        with phase(44):
            value = 0.0
            for blocks in (Z, Zm):
                solved = dot_nt(right, at(blocks[0])[...]).astype(bf)
                value = value + dot_nn(solved, at(blocks[0])[...])
            value = value.astype(bf)
            at(xp0)[...] = value
            for m in (3, 1, 2):
                counted(at(xp0), at(xr0).at[m], plane, at(xr0r), z, flipped(c, 2 * m))

        @pl.when(border)
        def _():
            with phase(45):
                settle_all(0, 1)
                forward(0, 1)
        def wait_mate(l):
            @pl.when(middle)
            def _():
                arrived(at(yb[l]).at[1], at(yr[l]))

            @pl.when(border)
            def _():
                arrived(at(yb[l]), at(yr[l]))
            if l < 3:
                arrived(at(Zm[l]), at(Zmr[l]))
            if l == 2:
                arrived(at(Cm[l]), at(Cmr[l]))

        with phase(50):
            arrived(at(Zm[3]), at(Zmr[3]))
            arrived(at(Cm[3]), at(Cmr[3]))
            for mate in range(2):
                leaf = core if mate == 0 else 1 - core
                block = at((C, Cm)[mate][3])[...]
                at(folded3)[mate] = dot_nn(at(table[2])[leaf], block).astype(bf)

        @pl.when(border)
        def _():
            with phase(48):
                settle_all(1, 1)
                forward(1, 1)
        with phase(57):
            at(folded1)[0] = dot_nn(at(table[0])[child], at(C[1])[...]).astype(bf)
        with phase(52):
            arrived(at(Cm[1]), at(Cmr[1]))
        with phase(58):
            at(folded1)[1] = dot_nn(at(table[0])[child], at(Cm[1])[...]).astype(bf)
        with phase(46):
            arrived(at(xr0).at[pl.ds(1, chips - 1)], at(xr0r))
        with phase(47):
            value = at(xp0)[...].astype(jnp.float32)
            for m in range(1, chips):
                value = value + at(xr0)[m].astype(jnp.float32)
            value = value.astype(bf)
            at(x0)[...] = value

        farthest = jnp.where(border, across, beyond)
        second = jnp.where(border, beyond, across)

        def leave(l, piece, dst, c_to, kept=None):
            for r in (farthest, second, pair):
                push(piece(r), dst, at(Os[l]), at(Or[l]), r, c_to)

            keep = lambda: pltpu.make_async_copy(piece(z), dst, at(Or[l])).start()
            give = lambda: push(piece(z), dst, at(Os[l]), at(Or[l]), z, c_to)
            if kept is None:
                pl.when(c_to == c)(keep)
                pl.when(c_to != c)(give)
            elif kept:
                keep()
            else:
                give()

        top_here, one_here = chip == z, q // 2 == z // 2
        one_to, two_to = 2 * chip + z % 2, 2 * chip + z // 2

        def top_piece(r):
            return at(x0).at[:, pl.ds(pl.multiple_of(r * K[0], 128), K[0])]

        @pl.when(top_here)
        def _():
            leave(0, top_piece, outs[0], c, True)

        def placed(l, low):
            return outs[l].at[pl.ds(pl.multiple_of(low, 16), NH)]

        def residual(l, index, coupled, low):
            return (at(yb[l])[index].astype(jnp.float32) - dot_nn(low, at(coupled[l])[...])).astype(bf)

        wait_mate(1)
        with phase(53):
            total = 0.0
            for mate in range(2):
                below = at(yb[1])[mate].astype(jnp.float32) - dot_nn(value, at(folded1)[mate])
                total = total + dot_nn(below.astype(bf), at((Z, Zm)[mate][1])[...])
            at(xp1)[...] = total.astype(bf)
            counted(at(xp1), at(xr1), plane, at(xr1r), z, flipped(c, 2))
            top = value
        side = chip % 2
        @pl.when(border)
        def _():
            with phase(56):
                settle_all(1, 2)
                forward(1, 2)
        with phase(51):
            at(v[1])[...] = dot_nn(top, at(table[0])[child]).astype(bf)
            low = at(v[1])[...]
        with phase(54):
            early = dot_nn(low, at(table[1])[side, S[1]:, :])
            arrived(at(xr1), at(xr1r))
        with phase(55):
            value = (at(xp1)[...].astype(jnp.float32) + at(xr1)[...].astype(jnp.float32)).astype(bf)
            at(v[2])[...] = (dot_nn(value, at(table[1])[side, :S[1], :]) + early).astype(bf)
            at(x1)[...] = value
            low = at(v[2])[...]
        wait_mate(2)
        with phase(57):
            value = dot_nn(residual(2, 0, C, low), at(Z[2])[...])
            value = value + dot_nn(residual(2, 1, Cm, low), at(Zm[2])[...])
            at(x2)[...] = value.astype(bf)
            high = at(x2)[...]
        with phase(58):
            @pl.when(one_here)
            def _():
                for r in range(R):
                    at(f1)[r] = at(x1)[:, r * K[1]:(r + 1) * K[1]]
                leave(1, lambda r: at(f1).at[r], placed(1, core * NH), one_to)

            def two_piece(r):
                return at(x2).at[:, pl.ds(pl.multiple_of(r * K[2], 128), K[2])]

            leave(2, two_piece, placed(2, half * N + core * NH), two_to)
        with phase(59):
            wait_mate(3)
        with phase(60):
            for mate in range(2):
                below = dot_nn(high, at(folded3)[mate, :S[2], :])
                below = below + dot_nn(low, at(folded3)[mate, S[2]:, :])
                below = (at(yb[3])[mate].astype(jnp.float32) - below).astype(bf)
                value = dot_nt(below, at((Z, Zm)[mate][3])[...]).astype(bf)
                for r in range(R):
                    piece = value[:, r * K[3]:(r + 1) * K[3]]
                    at(f3)[mate * R + r] = jnp.concatenate([piece[:NH // 2], piece[NH // 2:]], axis=1)
            low_row = pl.multiple_of((z * N + core * NH) // 2, 16)
            leaf_out = outs[3].at[pl.ds(low_row, NH // 2)]
            for mate in range(2):
                leave(3, lambda r: at(f3).at[mate * R + r], leaf_out, flipped(c, mate), mate == 0)
        with phase(61):
            for l in levels:
                drain(0, l)
                if l:
                    drain(1, l)
                drain_rhs(l)
                if l < 3:
                    drain_spread(l)

            @pl.when(middle)
            def _():
                for l in lower:
                    arrived(at(y[l]).at[pl.ds(0, 3)], at(ys[l]))
                take(at(inner), sent[inner])
            take(at(plane), sent[plane])
            joined = [shape for shape in z_shape + c_shape[1:] if shape[1] % 128 == 0]
            take(at(mates), sum(elements(shape) for shape in joined))
            for shape, copy in zip(c_shape[1:], Cm[1:]):
                if shape[1] % 128:
                    arrived(at(copy), at(mates1))

            @pl.when(jnp.logical_not(kept_here))
            def _():
                arrived(at(u[1]).at[child, q], at(beside))

            @pl.when(top_here)
            def _():
                arrived(at(x0).at[:, pl.ds(0, S[0] - K[0])], at(Os[0]))

            @pl.when(jnp.logical_and(one_here, one_to == c))
            def _():
                arrived(at(f1).at[pl.ds(0, R - 1)], at(Os[1]))

            @pl.when(jnp.logical_and(one_here, one_to != c))
            def _():
                arrived(at(f1), at(Os[1]))

            @pl.when(two_to == c)
            def _():
                arrived(at(x2).at[:, pl.ds(0, S[2] - K[2])], at(Os[2]))

            @pl.when(two_to != c)
            def _():
                arrived(at(x2), at(Os[2]))
            arrived(at(f3).at[pl.ds(0, 2 * R - 1)], at(Os[3]))
        with phase(62):
            for l in levels:
                arrived(outs[l], at(Or[l]))

    return kernel, scratch


def hand_on(turned, *refs):
    given, results, staged, made = refs[:4], refs[4:8], refs[8:12], refs[12:16]
    arriving, leaving = refs[16], refs[17]
    copies = []
    for i in (3, 2, 1, 0):
        if turned[i]:
            pltpu.make_async_copy(given[i], staged[i], arriving.at[i]).start()
        else:
            copies.append(pltpu.make_async_copy(given[i], results[i], leaving.at[i]))
            copies[-1].start()
    for i in (3, 2):
        pltpu.make_async_copy(given[i], staged[i], arriving.at[i]).wait()
        rows, lanes = staged[i].shape
        both = dot_nt(eye(lanes), staged[i][...]).astype(made[i].dtype)
        if made[i].shape != (lanes, rows):
            pieces = []
            for low in range(0, rows, 16):
                pieces += [both[:lanes // 2, low:low + 16], both[lanes // 2:, low:low + 16]]
            both = jnp.concatenate(pieces, axis=1)
        made[i][...] = both
        copies.append(pltpu.make_async_copy(made[i], results[i], leaving.at[i]))
        copies[-1].start()
    for copy in copies:
        copy.wait()


def fused_device(*blocks):
    plan = Plan(
        lax.axis_size("row"), lax.axis_size("col"),
        [block.shape for block in blocks[:4]], blocks[7].shape,
        [block.shape for block in blocks[11:14]],
    )
    if not plan.fits():
        return per_device(*blocks)
    kernel, scratch = build_kernel(plan)
    blocks = list(blocks)
    for at in (0, 1, 2, 3, 7, 8, 9, 10):
        if narrow(blocks[at].shape[1]):
            blocks[at] = blocks[at].T
    blocks = [pltpu.with_memory_space_constraint(block, pltpu.HBM) for block in blocks]
    anywhere = pl.BlockSpec(memory_space=pltpu.HBM)
    solved = pl.pallas_call(
        kernel,
        out_shape=tuple(
            jax.ShapeDtypeStruct(shape, blocks[0].dtype) for shape in plan.result_shapes()
        ),
        in_specs=[anywhere] * 14,
        out_specs=(pl.BlockSpec(memory_space=pl.ANY),) * 4,
        scratch_shapes=scratch,
        compiler_params=pltpu.CompilerParams(
            collective_id=0, has_side_effects=True, vmem_limit_bytes=VMEM_LIMIT
        ),
    )(*blocks)
    turned = [not narrow(width) for width in plan.width]
    final = [
        (strip, width) if turn else (width, strip)
        for width, strip, turn in zip(plan.width, plan.strip, turned)
    ]
    solved = pl.pallas_call(
        functools.partial(hand_on, turned),
        out_shape=tuple(jax.ShapeDtypeStruct(shape, blocks[0].dtype) for shape in final),
        in_specs=[pl.BlockSpec(memory_space=pl.ANY)] * 4,
        out_specs=(pl.BlockSpec(memory_space=pltpu.HBM),) * 4,
        scratch_shapes=[pltpu.VMEM(block.shape, block.dtype) for block in solved]
        + [pltpu.VMEM(shape, blocks[0].dtype) for shape in final]
        + [pltpu.SemaphoreType.DMA((4,))] * 2,
        compiler_params=pltpu.CompilerParams(vmem_limit_bytes=2**20),
    )(*solved)
    return tuple(block if turn else block.T for block, turn in zip(solved, turned))


def solution(mesh):
    in_specs = (
        P("col", "row"),
        P("col", "row"),
        P("col", "row"),
        P("col", "row"),
        P("row", "col"),
        P("row", "col"),
        P("row", "col"),
        P("row", "col"),
        P("row", "col"),
        P("row", "col"),
        P("row", "col"),
        P(),
        P(),
        P(),
    )
    out_specs = (P("row", "col"), P("row", "col"), P("row", "col"), P("row", "col"))
    return jax.shard_map(
        fused_device, mesh=mesh, in_specs=in_specs, out_specs=out_specs, check_vma=False
    )
```

```python
import functools

import jax
import jax.numpy as jnp
from jax import lax
from jax.experimental import pallas as pl
from jax.experimental.pallas import tpu as pltpu
from jax.sharding import PartitionSpec as P


def swapped(value, axis, stride):
    mask = 2**stride
    pairs = [(source, source ^ mask) for source in range(lax.axis_size(axis))]
    return lax.ppermute(value, axis, pairs)


def route_tables(mapping, child_index, parent_sep, parent_upd, strips, row_index):
    positions = lax.dynamic_index_in_dim(mapping, child_index, 0, keepdims=False)
    sep_rows = parent_sep // strips
    in_separator = positions < parent_sep
    if parent_upd > 0:
        upd_rows = parent_upd // strips
        target = jnp.where(
            in_separator, positions // sep_rows, (positions - parent_sep) // upd_rows
        )
        offset = jnp.where(
            in_separator, positions % sep_rows, sep_rows + (positions - parent_sep) % upd_rows
        )
    else:
        target = positions // sep_rows
        offset = positions % sep_rows
    block_rows = positions.shape[0] // strips
    blocks = target.reshape(strips, block_rows)
    matches = (blocks[:, :, None] == jnp.arange(strips, dtype=jnp.int32)[None, None, :]).astype(
        jnp.int32
    )
    slot_of = jnp.sum((jnp.cumsum(matches, axis=1) - 1) * matches, axis=2).reshape(-1)
    block_len = sep_rows + parent_upd // strips
    capacity = 2 * positions.shape[0] // (strips * strips)
    source = jnp.arange(positions.shape[0], dtype=jnp.int32) // block_rows
    mine_here = target == row_index
    column_at = jnp.where(mine_here, slot_of, capacity)
    lookup = jnp.full((strips, capacity + 1), block_len, jnp.int32)
    lookup = lookup.at[source, column_at].set(jnp.where(mine_here, offset, block_len))[:, :capacity]
    local_target = lax.dynamic_slice_in_dim(target, row_index * block_rows, block_rows)
    local_slots = lax.dynamic_slice_in_dim(slot_of, row_index * block_rows, block_rows)
    return (local_target, local_slots, lookup, capacity, block_len)


def pack_rows(values, local_target, local_slots, strips, capacity):
    buffer = jnp.zeros((strips, capacity, values.shape[1]), values.dtype)
    return buffer.at[local_target, local_slots].set(values)


def unpack_rows(received, lookup, block_len):
    summed = jnp.zeros((block_len + 1, received.shape[2]), jnp.float32)
    return summed.at[lookup].add(received.astype(jnp.float32))[:block_len]


def spread(portion, depth_bits, pass_on, column):
    for bit_index in range(depth_bits):
        partner = pass_on(portion, bit_index)
        is_upper = column >> bit_index & 1 == 1
        portion = jnp.where(
            is_upper,
            jnp.concatenate([partner, portion], axis=-1),
            jnp.concatenate([portion, partner], axis=-1),
        )
    return portion


def shrink(entire, depth_bits, pass_on, column):
    for bit_index in reversed(range(depth_bits)):
        half_width = entire.shape[-1] // 2
        low_part = entire[..., :half_width]
        high_part = entire[..., half_width:]
        is_upper = column >> bit_index & 1 == 1
        kept_part = jnp.where(is_upper, high_part, low_part)
        sent_part = jnp.where(is_upper, low_part, high_part)
        entire = kept_part + pass_on(sent_part, bit_index)
    return entire


def per_device(
    inverse_top,
    inverse_one,
    inverse_two,
    inverse_leaf,
    coupling_one,
    coupling_two,
    coupling_leaf,
    rhs_top,
    rhs_one,
    rhs_two,
    rhs_leaf,
    parent_map_one,
    parent_map_two,
    parent_map_leaf,
):
    strips = lax.axis_size("row")
    col_count = lax.axis_size("col")
    row_here = lax.axis_index("row")
    column = lax.axis_index("col")
    inverses = [inverse_top, inverse_one, inverse_two, inverse_leaf]
    couplings = [None, coupling_one, coupling_two, coupling_leaf]
    right_sides = [rhs_top, rhs_one, rhs_two, rhs_leaf]
    parent_maps = [None, parent_map_one, parent_map_two, parent_map_leaf]
    orders = [inverse.shape[1] * strips for inverse in inverses]
    groups = [col_count >> tree_level for tree_level in range(4)]
    group_bits = [group_size.bit_length() - 1 for group_size in groups]
    pass_rhs = lambda values, bit_index: swapped(values, "col", bit_index)
    pass_update_sum = lambda values, bit_index: swapped(
        values.astype(jnp.bfloat16), "col", bit_index
    ).astype(values.dtype)
    pass_update_spread = lambda values, bit_index: swapped(values, "col", bit_index)
    pass_solution_sum = lambda values, bit_index: swapped(
        values.astype(jnp.bfloat16), "col", bit_index
    ).astype(values.dtype)
    pass_solution_spread = lambda values, bit_index: swapped(values, "col", bit_index)
    full_rhs = [
        spread(right_sides[tree_level], group_bits[tree_level], pass_rhs, column)
        for tree_level in range(4)
    ]
    own_routes = [None]
    for tree_level in range(1, 4):
        parent_order = orders[tree_level - 1]
        parent_update = parent_order if tree_level > 1 else 0
        front_here = column // groups[tree_level]
        own_routes.append(
            route_tables(
                parent_maps[tree_level], front_here, parent_order, parent_update, strips, row_here
            )
        )
    pivots = [None] * 4
    incoming = None
    for tree_level in (3, 2, 1, 0):
        sep_rows = inverses[tree_level].shape[1]
        if incoming is None:
            separator = full_rhs[tree_level]
            own_update = None
        else:
            separator = (full_rhs[tree_level].astype(jnp.float32) + incoming[:sep_rows]).astype(
                jnp.bfloat16
            )
            own_update = lax.optimization_barrier(incoming[sep_rows:].astype(jnp.bfloat16))
        partial_value = jnp.dot(inverses[tree_level], separator, preferred_element_type=jnp.float32)
        solved = lax.psum(partial_value.astype(jnp.bfloat16), "row")
        pivots[tree_level] = solved
        if tree_level > 0:
            coupled = jnp.dot(couplings[tree_level], solved, preferred_element_type=jnp.float32)
            reduced = shrink(coupled, group_bits[tree_level], pass_update_sum, column)
            if own_update is None:
                portion = (-reduced).astype(jnp.bfloat16)
            else:
                start_at = column % groups[tree_level] * reduced.shape[1]
                kept_rows = lax.dynamic_slice_in_dim(own_update, start_at, reduced.shape[1], 1)
                portion = (kept_rows.astype(jnp.float32) - reduced).astype(jnp.bfloat16)
            updated = spread(portion, group_bits[tree_level], pass_update_spread, column)
            own_target, own_slots, own_lookup, capacity, block_len = own_routes[tree_level]
            got_own = lax.all_to_all(
                pack_rows(updated, own_target, own_slots, strips, capacity),
                "row",
                split_axis=0,
                concat_axis=0,
                tiled=True,
            )
            own_part = unpack_rows(got_own, own_lookup, block_len)
            partner = swapped(own_part.astype(jnp.bfloat16), "col", group_bits[tree_level])
            incoming = own_part + partner.astype(jnp.float32)
    solutions = [None] * 4
    parent_solution = None
    parent_gathered = None
    for tree_level in range(4):
        solved = pivots[tree_level]
        gathered = None
        if tree_level == 0:
            residual = solved
        else:
            own_target, own_slots, own_lookup, capacity, block_len = own_routes[tree_level]
            pieces = [parent_solution]
            if parent_gathered is not None:
                pieces.append(parent_gathered)
            pieces.append(jnp.zeros((1, parent_solution.shape[1]), jnp.bfloat16))
            parent_rows = jnp.concatenate(pieces, axis=0)
            returned = lax.all_to_all(
                parent_rows[own_lookup], "row", split_axis=0, concat_axis=0, tiled=True
            )
            gathered = returned[own_target, own_slots]
            coupling_term = jnp.dot(
                couplings[tree_level].T, gathered, preferred_element_type=jnp.float32
            )
            residual = (
                solved.astype(jnp.float32)
                - lax.psum(coupling_term.astype(jnp.bfloat16), "row").astype(jnp.float32)
            ).astype(jnp.bfloat16)
        contribution = jnp.dot(inverses[tree_level].T, residual, preferred_element_type=jnp.float32)
        if tree_level == 0:
            summed = lax.psum(contribution.astype(jnp.bfloat16), "col")
            solution = summed
            rhs_width = solution.shape[1] // groups[0]
            solutions[0] = lax.dynamic_slice_in_dim(
                solution, column % groups[0] * rhs_width, rhs_width, 1
            )
        else:
            portion = shrink(
                contribution, group_bits[tree_level], pass_solution_sum, column
            ).astype(jnp.bfloat16)
            solutions[tree_level] = portion
            if tree_level < 3:
                solution = spread(portion, group_bits[tree_level], pass_solution_spread, column)
        parent_solution = solution
        parent_gathered = gathered
    return (solutions[0], solutions[1], solutions[2], solutions[3])


MESH = pl.DeviceIdType.MESH
VMEM_LIMIT = 32 * 2**20


def dot_nn(left, right):
    return lax.dot_general(left, right, (((1,), (0,)), ((), ())), preferred_element_type=jnp.float32)


def dot_nt(left, right):
    return lax.dot_general(left, right, (((1,), (1,)), ((), ())), preferred_element_type=jnp.float32)


def eye(size):
    rows = lax.broadcasted_iota(jnp.int32, (size, size), 0)
    columns = lax.broadcasted_iota(jnp.int32, (size, size), 1)
    return jnp.where(rows == columns, 1.0, 0.0).astype(jnp.bfloat16)


def flipped(value, mask):
    result = value
    bit = 1
    while bit <= mask:
        if mask & bit:
            result = result + bit * (1 - 2 * ((value // bit) % 2))
        bit *= 2
    return result


class Plan:
    def __init__(self, rows, cols, inverse_shapes, rhs_top_shape, map_shape):
        self.rows, self.cols = rows, cols
        self.strip = [shape[1] for shape in inverse_shapes]
        self.order = [shape[1] * rows for shape in inverse_shapes]
        self.local = [shape[0] for shape in inverse_shapes]
        self.group = [cols >> level for level in range(4)]
        self.columns = rhs_top_shape[1] * cols
        self.width = [self.columns // group if group else 0 for group in self.group]
        self.mine = self.columns // rows
        self.map_shape = map_shape

    def total(self, level):
        return self.order[level] * (2 if level else 1)

    def result_shapes(self):
        shapes = list(zip(self.width, self.strip))
        return shapes[:3] + [(self.width[3] // 2, 2 * self.strip[3])]

    def span_rows(self):
        n, order, width = self.mine, self.order, self.width
        shared = 3 * (n // 4) * order[1] + 3 * (n // 2) * order[0] + n // 2 * order[1]
        inner = 2 * n * order[3] + 4 * n * order[2] + 8 * (n // 4) * order[1]
        joined = sum(2 * order[level] * self.local[level] for level in (2, 3))
        joined += sum(order[level] * self.local[level] for level in (0, 1))
        return max(shared, inner, joined, 9 * n * order[1], 3 * width[0] * order[0], 3 * n * order[2]) // 128

    def fits(self):
        table = sum(
            2 * self.total(level) * self.order[level + 1] * 2 for level in range(3)
        )
        if self.rows != 4 or self.group[3] != 1 or self.mine * self.rows != self.columns or table > 24 * 2**20:
            return False
        if self.group != [8, 4, 2, 1] or self.mine % 64:
            return False
        for level in range(4):
            if self.strip[level] % 64 or self.order[level] % 128 or self.local[level] % 64:
                return False
        if not packed((self.mine, self.strip[1])):
            return False
        return narrow(self.strip[3]) and not any(narrow(strip) for strip in self.strip[:3])


def elements(shape):
    count = 1
    for extent in shape:
        count *= extent
    return count


def packed(shape):
    return shape[1] > 128 and shape[1] % 128 == 64


def packed_shape(shape):
    return (shape[0] * (shape[1] // 128) + shape[0] // 2, 128)


def narrow(size):
    return size < 128


def phase(number):
    return jax.named_scope(str(number))


def build_kernel(plan):
    R, CC, N = plan.rows, plan.cols, plan.mine
    S, K, L, G, W = plan.order, plan.strip, plan.local, plan.group, plan.width
    N2, NH, NQ, chips = 2 * N, N // 2, N // G[1], G[0] // 2
    bf = jnp.bfloat16
    scratch = []

    def ref(shape, dtype=bf):
        scratch.append(pltpu.VMEM(shape, dtype))
        return len(scratch) - 1

    def sems(*shape):
        scratch.append(pltpu.SemaphoreType.DMA(shape) if shape else pltpu.SemaphoreType.DMA)
        return len(scratch) - 1

    levels, lower = range(4), (1, 2, 3)
    z_shape = [(S[3], L[3]) if l == 3 else (L[l], S[l]) for l in levels]
    c_shape = [None] + [(S[l], L[l]) for l in lower]
    Z = [ref(z_shape[l]) for l in levels]
    C = [None] + [ref(c_shape[l]) for l in lower]
    Zm = [ref(z_shape[l]) for l in levels]
    Cm = [None] + [ref(c_shape[l]) for l in lower]
    Zp = [ref((R,) + packed_shape((L[l], K[l]))) if l < 3 and packed((L[l], K[l])) else None for l in levels]
    Cp = [None] + [ref((R,) + packed_shape((K[l], L[l]))) if packed((K[l], L[l])) else None for l in lower]
    Zraw = [ref((L[l], K[l])) if Zp[l] is not None else None for l in levels]
    Craw = [None] + [ref((K[l], L[l])) if Cp[l] is not None else None for l in lower]
    Zr, Zs = [sems() for _ in levels], [sems() for _ in levels]
    Cr, Cs = [None] + [sems() for _ in lower], [None] + [sems() for _ in lower]
    Zmr, Cmr, mates, mates1 = [sems() for _ in levels], [None] + [sems() for _ in lower], sems(), sems()
    table = [ref((2, plan.total(l), S[l + 1])) for l in range(3)]
    held_map = [None] + [ref(plan.map_shape[l - 1], jnp.int32) for l in lower]
    local = sems(6)
    B = [ref((NH, S[0])), ref((2, R) + packed_shape((N, K[1]))), ref((S[2], N2)), ref((S[3], N2))]
    B1, rhs_raw, rhs_packed = ref((N2, S[1])), ref((N, K[1])), ref(packed_shape((N, K[1])))
    Bs, Br = [sems() for _ in levels], [sems() for _ in levels]
    Ds, Dr = [sems(), sems(), sems()], [sems(), sems(2), sems()]
    y = [None] + [ref((4, NH, L[l])) for l in lower]
    yb = [None] + [ref((2, NH, L[l])) for l in lower]
    ys, yr = [None] + [sems() for _ in lower], [None] + [sems() for _ in lower]
    u = [None, ref((2, G[1], NQ, S[1])), ref((2, 2, G[1], NQ, S[2])), ref((2, N2, S[3]))]
    ur, ur1 = [None, None, sems(), sems()], sems(2)
    f0 = ref((NH, S[0]), jnp.float32)
    up1, ut1, ut1r = ref((2, G[1], NQ, S[1])), ref((G[1], NQ, S[1])), sems()
    h1 = ref((2, NQ, S[1]))
    folded, early1 = ref((2, L[1], S[2])), ref((N2, L[1]), jnp.float32)
    up2, ut2, ut2r = ref((2, N, S[2])), ref((N, S[2])), sems()
    xp0, xr0, xr0r = ref((NH, S[0])), ref((chips, NH, S[0])), sems()
    x0 = ref((NH, S[0]))
    xp1, xr1, xr1r = ref((NH, S[1])), ref((NH, S[1])), sems()
    v = [None] + [ref((NH, S[l])) for l in (1, 2)]
    x1, x2 = ref((NH, S[1])), ref((NH, S[2]))
    f1, f3 = ref((R, NH, K[1])), ref((2 * R, NH // 2, 2 * K[3]))
    folded3, folded1 = ref((2, 2 * S[2], L[3])), ref((2, S[0], L[1]))
    Os, Or = [sems() for _ in levels], [sems() for _ in levels]
    plane, inner, beside = sems(), sems(), sems()
    scratch.append(pltpu.SemaphoreType.REGULAR)
    ready = len(scratch) - 1
    scratch.append(pltpu.SemaphoreType.REGULAR)
    ready_group = len(scratch) - 1
    span = ref((plan.span_rows(), 128))

    def kernel(*refs):
        inverse = refs[0:4]
        coupling = (None,) + tuple(refs[4:7])
        rhs = refs[7:11]
        maps = (None,) + tuple(refs[11:14])
        outs = refs[14:18]
        held = refs[18:]
        at = lambda index: held[index]
        z = lax.axis_index("row")
        c = lax.axis_index("col")
        core, chip = c % 2, c // 2
        middle = jnp.logical_and(z > 0, z < R - 1)
        border = jnp.logical_not(middle)
        half = z % 2
        pair = z + 1 - 2 * half
        across = R - 1 - z
        beyond = R - 1 - pair
        sent = {}

        def remote(src, dst, ssem, rsem, z_to, c_to):
            return pltpu.make_async_remote_copy(
                src_ref=src, dst_ref=dst, send_sem=ssem, recv_sem=rsem,
                device_id=(z_to, c_to), device_id_type=MESH,
            )

        def push(src, dst, ssem, rsem, z_to, c_to):
            remote(src, dst, ssem, rsem, z_to, c_to).start()

        def counted(src, dst, index, rsem, z_to, c_to):
            push(src, dst, at(index), rsem, z_to, c_to)
            sent[index] = sent.get(index, 0) + elements(src.shape)

        def arrived(dst, rsem):
            pltpu.make_async_copy(dst, dst, rsem).wait()

        def take(sem, count):
            view = at(span).at[pl.ds(0, count // 128)]
            pltpu.make_async_copy(view, view, sem).wait()

        barrier = pltpu.get_barrier_semaphore()
        group_here = [(z, flipped(c, m)) for m in range(1, G[1])]
        opposite = (z, flipped(c, G[1]))

        def greet(semaphore, *friends):
            for friend in friends:
                pl.semaphore_signal(semaphore, inc=1, device_id=friend, device_id_type=MESH)

        greet(barrier, (pair, c))

        @pl.when(middle)
        def _():
            greet(barrier, (across, c), (beyond, c), *group_here)

        @pl.when(border)
        def _():
            greet(barrier, opposite)

        raws = [(rhs[1], at(rhs_raw))]
        for l in levels:
            if Zp[l] is not None:
                raws.append((inverse[l], at(Zraw[l])))
            if l and Cp[l] is not None:
                raws.append((coupling[l], at(Craw[l])))
        loads = raws + [(maps[l], at(held_map[l])) for l in lower]
        for i, (src, dst) in enumerate(loads):
            pltpu.make_async_copy(src, dst, at(local).at[i]).start()

        def slot(kind, l, r):
            if kind == 0:
                if Zp[l] is not None:
                    return at(Zp[l]).at[r], at(Zr[l])
                if l == 3:
                    low = pl.multiple_of(r * K[l], 16)
                    return at(Z[l]).at[pl.ds(low, K[l])], at(Zr[l])
                low = pl.multiple_of(r * K[l], 128)
                return at(Z[l]).at[:, pl.ds(low, K[l])], at(Zr[l])
            if Cp[l] is not None:
                return at(Cp[l]).at[r], at(Cr[l])
            low = pl.multiple_of(r * K[l], 16)
            return at(C[l]).at[pl.ds(low, K[l])], at(Cr[l])

        def is_packed(kind, l):
            return (Zp, Cp)[kind][l] is not None

        def source(kind, l):
            if is_packed(kind, l):
                return slot(kind, l, z)[0]
            return (inverse, coupling)[kind][l]

        def send_sem(kind, l):
            return at((Zs, Cs)[kind][l])

        def own_load(kind, l):
            if not is_packed(kind, l):
                dst, sem = slot(kind, l, z)
                pltpu.make_async_copy(source(kind, l), dst, sem).start()

        def own_send(kind, l):
            dst, sem = slot(kind, l, z)
            push(source(kind, l), dst, send_sem(kind, l), sem, jnp.where(middle, across, pair), c)

            @pl.when(border)
            def _():
                push(source(kind, l), dst, send_sem(kind, l), sem, beyond, c)

        def own_out(kind, l):
            dst, sem = slot(kind, l, z)
            push(source(kind, l), dst, send_sem(kind, l), sem, pair, c)

        def pass_on(kind, l, origins=(across, beyond)):
            for r in origins:
                dst, sem = slot(kind, l, r)
                push(dst, dst, send_sem(kind, l), sem, pair, c)

        def settle_all(kind, l):
            rsem = slot(kind, l, z)[1]
            if is_packed(kind, l):
                arrived(at((Zp, Cp)[kind][l]).at[pl.ds(0, R - 1)], rsem)
                unpack(kind, l)
            else:
                arrived(at((Z, C)[kind][l]), rsem)

        def unpacked(block, rows, lanes):
            whole = lanes // 128 * rows
            rest = block[whole:]
            rest = jnp.concatenate([rest[:, :lanes % 128], rest[:, lanes % 128:]], axis=0)
            return jnp.concatenate([block[i:i + rows] for i in range(0, whole, rows)] + [rest], axis=1)

        def unpack(kind, l):
            rows, lanes = (L[l], K[l]) if kind == 0 else (K[l], L[l])
            for r in range(R):
                value = unpacked(at((Zp, Cp)[kind][l])[r], rows, lanes)
                if kind == 0:
                    at(Z[l])[:, r * lanes:(r + 1) * lanes] = value
                else:
                    at(C[l])[r * rows:(r + 1) * rows, :] = value

        def pack(raw):
            value = raw[...]
            rows, lanes = value.shape
            whole = lanes - lanes % 128
            pieces = [value[:, i:i + 128] for i in range(0, whole, 128)]
            rest = value[:, whole:]
            rest = jnp.concatenate([rest[:rows // 2], rest[rows // 2:]], axis=1)
            return jnp.concatenate(pieces + [rest], axis=0)

        def drain(kind, l):
            if is_packed(kind, l):
                whole = at((Zp, Cp)[kind][l])
                part = whole.at[pl.ds(0, R // 2)]
            else:
                whole = at((Z, C)[kind][l])
                if kind == 0 and l < 3:
                    part = whole.at[:, pl.ds(0, S[l] // 2)]
                else:
                    part = whole.at[pl.ds(0, S[l] // 2)]

            @pl.when(middle)
            def _():
                arrived(whole, send_sem(kind, l))

            @pl.when(border)
            def _():
                arrived(part, send_sem(kind, l))

        def rhs_pieces(l):
            q = c % G[l]
            if l == 3:
                return [
                    (rhs[3].at[:, pl.ds(i * N2, N2)], at(B[3]).at[pl.ds(pl.multiple_of(z * K[3], 16), K[3])], 1 + i)
                    for i in range(2)
                ]
            if l == 2:
                return [(rhs[2], at(B[2]).at[pl.ds(pl.multiple_of(z * K[2], 16), K[2])], 1 + q)]
            if l == 1:
                return [(at(rhs_packed), at(B[1]).at[q % 2, z], 1 + q // 2)]
            lanes = pl.ds(pl.multiple_of(z * K[0], 128), K[0])
            return [(rhs[0], at(B[0]).at[:, lanes], q // 2)]

        def start_rhs(l):
            for src, dst, z_to in rhs_pieces(l):
                @pl.when(z_to == z)
                def _():
                    pltpu.make_async_copy(src, dst, at(Br[l])).start()

                @pl.when(z_to != z)
                def _():
                    push(src, dst, at(Bs[l]), at(Br[l]), z_to, c)

        def drain_rhs(l):
            pieces = rhs_pieces(l)
            if l == 3:
                @pl.when(middle)
                def _():
                    arrived(at(B[3]).at[pl.ds(0, K[3])], at(Bs[3]))

                @pl.when(border)
                def _():
                    arrived(at(B[3]).at[pl.ds(0, 2 * K[3])], at(Bs[3]))
                return
            src, dst, z_to = pieces[0]

            @pl.when(z_to != z)
            def _():
                arrived(dst, at(Bs[l]))

        def rhs_spread(l):
            q = c % G[l]
            if l == 2:
                return z == 1 + q, at(B[2]), at(Dr[2])
            if l == 1:
                return z == 1 + q // 2, at(B[1]).at[q % 2], at(Dr[1]).at[q % 2]
            return z == q // 2, at(B[0]), at(Dr[0])

        def spread_rhs(l):
            holds, here, rsem = rhs_spread(l)

            @pl.when(holds)
            def _():
                arrived(here, at(Br[l]))
                for m in range(2, CC, 2) if l == 0 else range(1, G[l]):
                    push(here, here, at(Ds[l]), rsem, z, flipped(c, m))

        def drain_spread(l):
            holds, here, _ = rhs_spread(l)

            @pl.when(holds)
            def _():
                take(at(Ds[l]), (chips - 1, G[1] - 1, 1)[l] * elements(here.shape))

        def wait_rhs(l):
            holds, here, rsem = rhs_spread(l)
            if l != 1:
                @pl.when(jnp.logical_not(holds))
                def _():
                    arrived(here, rsem)
                return
            for part in range(2):
                @pl.when(jnp.logical_not(jnp.logical_and(holds, c % 2 == part)))
                def _():
                    arrived(at(B[1]).at[part], at(Dr[1]).at[part])

        def make_table(l):
            front = c // G[l]
            step = K[l]
            for child in range(2):
                row = at(held_map[l + 1])[pl.ds(2 * front + child, 1), :]

                def body(i, carry):
                    start = pl.multiple_of(i * step, 16)
                    at_row = lax.broadcasted_iota(jnp.int32, (step, S[l + 1]), 0) + start
                    at(table[l])[child, pl.ds(start, step), :] = jnp.where(
                        at_row == row, 1.0, 0.0
                    ).astype(bf)
                    return carry

                lax.fori_loop(0, plan.total(l) // step, body, 0)

        def gathered(l, low, size, first, second):
            value = dot_nt(first, at(table[l])[0, low:low + size, :])
            return value + dot_nt(second, at(table[l])[1, low:low + size, :])

        def forward(kind, l):
            own, copy = at((Z, C)[kind][l]), at((Zm, Cm)[kind][l])
            ssem = at(mates1 if own.shape[1] % 128 else mates)
            push(own, copy, ssem, at((Zmr, Cmr)[kind][l]), z, flipped(c, 1))

        def hand_over(l):
            at(yb[l])[0] = at(y[l])[2 * half + core]
            src = at(y[l]).at[2 * half + 1 - core]
            push(src, at(yb[l]).at[1], at(ys[l]), at(yr[l]), z, flipped(c, 1))
            src = at(y[l]).at[2 * (1 - half) + core]
            push(src, at(yb[l]).at[0], at(ys[l]), at(yr[l]), pair, c)
            src = at(y[l]).at[2 * (1 - half) + 1 - core]
            push(src, at(yb[l]).at[1], at(ys[l]), at(yr[l]), pair, flipped(c, 1))

        with phase(2):
            @pl.when(middle)
            def _():
                pl.semaphore_wait(barrier, G[1] + 1)

            @pl.when(border)
            def _():
                pl.semaphore_wait(barrier, 3)

        with phase(3):
            own_send(0, 3)
            start_rhs(3)
            own_send(1, 3)
            pltpu.make_async_copy(*loads[0], at(local).at[0]).wait()
            at(rhs_packed)[...] = pack(at(rhs_raw))
            start_rhs(2)
            start_rhs(1)
            own_send(0, 2)
            own_send(1, 2)
            for i, (src, dst) in enumerate(loads[1:]):
                pltpu.make_async_copy(src, dst, at(local).at[i + 1]).wait()
            for l in levels:
                if Zp[l] is not None:
                    at(Zp[l])[z] = pack(at(Zraw[l]))
                if l and Cp[l] is not None:
                    at(Cp[l])[z] = pack(at(Craw[l]))
            own_send(0, 1)
            own_send(1, 1)
            for l in levels:
                own_load(0, l)
                if l:
                    own_load(1, l)

            @pl.when(middle)
            def _():
                own_out(0, 0)
                for l in (3, 2, 1):
                    own_out(0, l)
                    own_out(1, l)

            @pl.when(border)
            def _():
                greet(at(ready), opposite)
                pl.semaphore_wait(at(ready), 1)
                greet(at(ready), (pair, c))

        def last_send(turn):
            @pl.when(turn)
            def _():
                own_send(0, 0)

        make_table(2)

        @pl.when(middle)
        def _():
            with phase(31):
                arrived(at(B[3]), at(Br[3]))
                right = dot_nt(eye(N2), at(B[3])[...]).astype(bf)
                settle_all(0, 3)
                start_rhs(0)
                last_send(core == 0)
                pl.semaphore_wait(at(ready), 1)
                greet(at(ready_group), *group_here)
            with phase(32):
                solved = dot_nn(right, at(Z[3])[...]).astype(bf)
                at(y[3])[...] = solved.reshape(4, NH, L[3])
                settle_all(1, 3)
            with phase(33):
                at(u[3])[core] = (-dot_nt(solved, at(C[3])[...])).astype(bf)
                here = at(u[3]).at[core]
                counted(here, here, inner, at(ur[3]), z, flipped(c, 1))
                pl.semaphore_wait(at(ready_group), G[1] - 1)
                greet(at(ready), (pair, c))
                pass_on(0, 3)
                pass_on(1, 3)
        spread_rhs(2)
        spread_rhs(1)
        make_table(1)

        @pl.when(middle)
        def _():
            with phase(21):
                arrived(at(u[3]).at[0], at(ur[3]))
                wait_rhs(2)
            with phase(22):
                pair_of = at(u[3])[0], at(u[3])[1]
                right = dot_nt(eye(N2), at(B[2])[...]) + gathered(2, 0, S[2], *pair_of)
                right = right.astype(bf)
                lower_part = pl.ds(pl.multiple_of(core * N, N), N)
                pair_of = at(u[3])[0, lower_part, :], at(u[3])[1, lower_part, :]
                kept = gathered(2, S[2], S[2], *pair_of)
            with phase(23):
                settle_all(0, 2)
                pass_on(0, 2)
            with phase(24):
                solved = dot_nt(right, at(Z[2])[...]).astype(bf)
                at(y[2])[...] = solved.reshape(4, NH, L[2])
            with phase(25):
                settle_all(1, 2)
            with phase(26):
                at(up2)[...] = dot_nt(solved, at(C[2])[...]).astype(bf).reshape(2, N, S[2])
                counted(at(up2).at[1 - core], at(ut2), inner, at(ut2r), z, flipped(c, 1))
            with phase(27):
                own = at(up2)[core].astype(jnp.float32)
                arrived(at(ut2), at(ut2r))
                own = kept - (own + at(ut2)[...].astype(jnp.float32))
                child = (c // G[2]) % 2
                at(u[2])[child, core] = own.astype(bf).reshape(G[1], NQ, S[2])
                here = at(u[2]).at[child, core]
                for m in (3, 2, 1):
                    counted(here, here, inner, at(ur[2]), z, flipped(c, m))
        make_table(0)
        q, child = c % G[1], (c // G[1]) % 2

        @pl.when(middle)
        def _():
            with phase(11):
                wait_rhs(1)
                for part in range(2):
                    for r in range(R):
                        value = unpacked(at(B[1])[part, r], N, K[1])
                        at(B1)[part * N:(part + 1) * N, r * K[1]:(r + 1) * K[1]] = value
            with phase(14):
                settle_all(0, 1)
                pass_on(0, 1)
                last_send(core == 1)
            with phase(10):
                at(early1)[...] = dot_nt(at(B1)[...], at(Z[1])[...])
                for i in range(2):
                    at(folded)[i] = dot_nn(at(Z[1])[...], at(table[1])[i, :S[1], :]).astype(bf)
            with phase(12):
                take(at(ur[2]), 3 * N * S[2])
            with phase(13):
                pair_of = [at(u[2])[i].reshape(N2, S[2]) for i in range(2)]
                solved = at(early1)[...]
                for i in range(2):
                    solved = solved + dot_nt(pair_of[i], at(folded)[i])
                solved = solved.astype(bf)
                at(y[1])[...] = solved.reshape(4, NH, L[1])
            with phase(16):
                settle_all(1, 1)
            with phase(17):
                def couple(part):
                    rows = at(y[1])[pl.ds(pl.multiple_of(2 * part, 2), 2)].reshape(N, L[1])
                    value = dot_nt(rows, at(C[1])[...]).astype(bf)
                    at(up1)[part] = value.reshape(G[1], NQ, S[1])

                couple(1 - half)
                for m in (3, 2, 1):
                    src = at(up1).at[1 - half, flipped(q, m)]
                    counted(src, at(ut1).at[m], inner, at(ut1r), pair, flipped(c, m))
                couple(half)
                for m in (3, 2, 1):
                    src = at(up1).at[half, flipped(q, m)]
                    counted(src, at(ut1).at[m], inner, at(ut1r), z, flipped(c, m))
                pair_of = [at(u[2])[i, :, q].reshape(2 * NQ, S[2]) for i in range(2)]
                kept = gathered(1, S[1], S[1], *pair_of)
                at(h1)[...] = kept.astype(bf).reshape(2, NQ, S[1])
                at(up1)[1 - half, q] = (
                    at(up1)[1 - half, q].astype(jnp.float32) - at(h1)[1 - half].astype(jnp.float32)
                ).astype(bf)
                counted(at(up1).at[1 - half, q], at(ut1).at[0], inner, at(ut1r), pair, c)
                spread_rhs(0)
                settle_all(0, 0)
                pass_on(0, 0)
                pass_on(1, 1)
                hand_over(1)
                pass_on(1, 2)
                hand_over(2)
                hand_over(3)
                forward(0, 0)

        @pl.when(border)
        def _():
            with phase(18):
                pl.semaphore_wait(at(ready), 1)
                for kind, l in ((0, 3), (1, 3), (0, 2)):
                    settle_all(kind, l)
                    if (kind, l) == (0, 3):
                        start_rhs(0)
                    if (kind, l) != (1, 3):
                        last_send(core == (0 if l == 3 else 1))
                    forward(kind, l)
                spread_rhs(0)
                arrived(at(ut1), at(ut1r))
                value = at(ut1)[0].astype(jnp.float32)
                for m in range(1, G[1]):
                    value = value + at(ut1)[m].astype(jnp.float32)
                at(u[1])[child, q] = (-value).astype(bf)

        @pl.when(middle)
        def _():
            with phase(19):
                value = at(up1)[half, q].astype(jnp.float32)
                arrived(at(ut1).at[pl.ds(1, G[1] - 1)], at(ut1r))
                for m in range(1, G[1]):
                    value = value + at(ut1)[m].astype(jnp.float32)
                at(u[1])[child, q] = (at(h1)[half].astype(jnp.float32) - value).astype(bf)
        here = at(u[1]).at[child, q]
        kept_here = q // 2 == core
        for m in (6, 4, 2):
            rsem = at(ur1).at[0 if m == 2 else 1]
            counted(here, here, plane, rsem, z, flipped(2 * chip + q // 2, m))

        @pl.when(jnp.logical_not(kept_here))
        def _():
            push(here, here, at(beside), at(ur1).at[0], z, flipped(c, 1))

        @pl.when(border)
        def _():
            with phase(40):
                settle_all(0, 0)
                forward(0, 0)

        @pl.when(middle)
        def _():
            with phase(20):
                for l in lower:
                    for kind in range(2):
                        forward(kind, l)
        with phase(41):
            @pl.when(kept_here)
            def _():
                take(at(ur1).at[0], NQ * S[1])

            @pl.when(jnp.logical_not(kept_here))
            def _():
                take(at(ur1).at[0], 2 * NQ * S[1])
            wait_rhs(0)
        columns = pl.ds(pl.multiple_of(2 * core, 2), 2)
        with phase(42):
            part = dot_nt(at(u[1])[child, columns].reshape(NH, S[1]), at(table[0])[child])
            at(f0)[...] = at(B[0])[...].astype(jnp.float32) + part
            take(at(ur1).at[1], 2 * NQ * S[1])
        with phase(49):
            part = dot_nt(at(u[1])[1 - child, columns].reshape(NH, S[1]), at(table[0])[1 - child])
            right = (at(f0)[...] + part).astype(bf)
        with phase(43):
            arrived(at(Zm[0]), at(Zmr[0]))
        with phase(44):
            value = 0.0
            for blocks in (Z, Zm):
                solved = dot_nt(right, at(blocks[0])[...]).astype(bf)
                value = value + dot_nn(solved, at(blocks[0])[...])
            value = value.astype(bf)
            at(xp0)[...] = value
            for m in (3, 1, 2):
                counted(at(xp0), at(xr0).at[m], plane, at(xr0r), z, flipped(c, 2 * m))

        @pl.when(border)
        def _():
            with phase(45):
                settle_all(0, 1)
                forward(0, 1)
        def wait_mate(l):
            @pl.when(middle)
            def _():
                arrived(at(yb[l]).at[1], at(yr[l]))

            @pl.when(border)
            def _():
                arrived(at(yb[l]), at(yr[l]))
            if l < 3:
                arrived(at(Zm[l]), at(Zmr[l]))
            if l == 2:
                arrived(at(Cm[l]), at(Cmr[l]))

        with phase(50):
            arrived(at(Zm[3]), at(Zmr[3]))
            arrived(at(Cm[3]), at(Cmr[3]))
            for mate in range(2):
                leaf = core if mate == 0 else 1 - core
                block = at((C, Cm)[mate][3])[...]
                at(folded3)[mate] = dot_nn(at(table[2])[leaf], block).astype(bf)

        @pl.when(border)
        def _():
            with phase(48):
                settle_all(1, 1)
                forward(1, 1)
        with phase(57):
            at(folded1)[0] = dot_nn(at(table[0])[child], at(C[1])[...]).astype(bf)
        with phase(52):
            arrived(at(Cm[1]), at(Cmr[1]))
        with phase(58):
            at(folded1)[1] = dot_nn(at(table[0])[child], at(Cm[1])[...]).astype(bf)
        with phase(46):
            arrived(at(xr0).at[pl.ds(1, chips - 1)], at(xr0r))
        with phase(47):
            value = at(xp0)[...].astype(jnp.float32)
            for m in range(1, chips):
                value = value + at(xr0)[m].astype(jnp.float32)
            value = value.astype(bf)
            at(x0)[...] = value

        farthest = jnp.where(border, across, beyond)
        second = jnp.where(border, beyond, across)

        def leave(l, piece, dst, c_to, kept=None):
            for r in (farthest, second, pair):
                push(piece(r), dst, at(Os[l]), at(Or[l]), r, c_to)

            keep = lambda: pltpu.make_async_copy(piece(z), dst, at(Or[l])).start()
            give = lambda: push(piece(z), dst, at(Os[l]), at(Or[l]), z, c_to)
            if kept is None:
                pl.when(c_to == c)(keep)
                pl.when(c_to != c)(give)
            elif kept:
                keep()
            else:
                give()

        top_here, one_here = chip == z, q // 2 == z // 2
        one_to, two_to = 2 * chip + z % 2, 2 * chip + z // 2

        def top_piece(r):
            return at(x0).at[:, pl.ds(pl.multiple_of(r * K[0], 128), K[0])]

        def placed(l, low):
            return outs[l].at[pl.ds(pl.multiple_of(low, 16), NH)]

        def residual(l, index, coupled, low):
            return (at(yb[l])[index].astype(jnp.float32) - dot_nn(low, at(coupled[l])[...])).astype(bf)

        wait_mate(1)
        with phase(53):
            total = 0.0
            for mate in range(2):
                below = at(yb[1])[mate].astype(jnp.float32) - dot_nn(value, at(folded1)[mate])
                total = total + dot_nn(below.astype(bf), at((Z, Zm)[mate][1])[...])
            at(xp1)[...] = total.astype(bf)
            counted(at(xp1), at(xr1), plane, at(xr1r), z, flipped(c, 2))
            top = value

        @pl.when(top_here)
        def _():
            leave(0, top_piece, outs[0], c, True)

        side = chip % 2
        @pl.when(border)
        def _():
            with phase(56):
                settle_all(1, 2)
                forward(1, 2)
        with phase(51):
            at(v[1])[...] = dot_nn(top, at(table[0])[child]).astype(bf)
            low = at(v[1])[...]
        with phase(54):
            early = dot_nn(low, at(table[1])[side, S[1]:, :])
            arrived(at(xr1), at(xr1r))
        with phase(55):
            value = (at(xp1)[...].astype(jnp.float32) + at(xr1)[...].astype(jnp.float32)).astype(bf)
            at(v[2])[...] = (dot_nn(value, at(table[1])[side, :S[1], :]) + early).astype(bf)
            at(x1)[...] = value
            low = at(v[2])[...]
        wait_mate(2)
        with phase(57):
            value = dot_nn(residual(2, 0, C, low), at(Z[2])[...])
            value = value + dot_nn(residual(2, 1, Cm, low), at(Zm[2])[...])
            at(x2)[...] = value.astype(bf)
            high = at(x2)[...]
        with phase(58):
            @pl.when(one_here)
            def _():
                for r in range(R):
                    at(f1)[r] = at(x1)[:, r * K[1]:(r + 1) * K[1]]
                leave(1, lambda r: at(f1).at[r], placed(1, core * NH), one_to)

            def two_piece(r):
                return at(x2).at[:, pl.ds(pl.multiple_of(r * K[2], 128), K[2])]

            leave(2, two_piece, placed(2, half * N + core * NH), two_to)
        with phase(59):
            wait_mate(3)
        with phase(60):
            for mate in range(2):
                below = dot_nn(high, at(folded3)[mate, :S[2], :])
                below = below + dot_nn(low, at(folded3)[mate, S[2]:, :])
                below = (at(yb[3])[mate].astype(jnp.float32) - below).astype(bf)
                value = dot_nt(below, at((Z, Zm)[mate][3])[...]).astype(bf)
                for r in range(R):
                    piece = value[:, r * K[3]:(r + 1) * K[3]]
                    at(f3)[mate * R + r] = jnp.concatenate([piece[:NH // 2], piece[NH // 2:]], axis=1)
            low_row = pl.multiple_of((z * N + core * NH) // 2, 16)
            leaf_out = outs[3].at[pl.ds(low_row, NH // 2)]
            for mate in range(2):
                leave(3, lambda r: at(f3).at[mate * R + r], leaf_out, flipped(c, mate), mate == 0)
        with phase(61):
            for l in levels:
                drain(0, l)
                if l:
                    drain(1, l)
                drain_rhs(l)
                if l < 3:
                    drain_spread(l)

            @pl.when(middle)
            def _():
                for l in lower:
                    arrived(at(y[l]).at[pl.ds(0, 3)], at(ys[l]))
                take(at(inner), sent[inner])
            take(at(plane), sent[plane])
            joined = [shape for shape in z_shape + c_shape[1:] if shape[1] % 128 == 0]
            take(at(mates), sum(elements(shape) for shape in joined))
            for shape, copy in zip(c_shape[1:], Cm[1:]):
                if shape[1] % 128:
                    arrived(at(copy), at(mates1))

            @pl.when(jnp.logical_not(kept_here))
            def _():
                arrived(at(u[1]).at[child, q], at(beside))

            @pl.when(top_here)
            def _():
                arrived(at(x0).at[:, pl.ds(0, S[0] - K[0])], at(Os[0]))

            @pl.when(jnp.logical_and(one_here, one_to == c))
            def _():
                arrived(at(f1).at[pl.ds(0, R - 1)], at(Os[1]))

            @pl.when(jnp.logical_and(one_here, one_to != c))
            def _():
                arrived(at(f1), at(Os[1]))

            @pl.when(two_to == c)
            def _():
                arrived(at(x2).at[:, pl.ds(0, S[2] - K[2])], at(Os[2]))

            @pl.when(two_to != c)
            def _():
                arrived(at(x2), at(Os[2]))
            arrived(at(f3).at[pl.ds(0, 2 * R - 1)], at(Os[3]))
        with phase(62):
            for l in levels:
                arrived(outs[l], at(Or[l]))

    return kernel, scratch


def hand_on(turned, *refs):
    given, results, staged, made = refs[:4], refs[4:8], refs[8:12], refs[12:16]
    arriving, leaving = refs[16], refs[17]
    copies = []
    for i in (3, 2, 1, 0):
        if turned[i]:
            pltpu.make_async_copy(given[i], staged[i], arriving.at[i]).start()
        else:
            copies.append(pltpu.make_async_copy(given[i], results[i], leaving.at[i]))
            copies[-1].start()
    for i in (3, 2):
        pltpu.make_async_copy(given[i], staged[i], arriving.at[i]).wait()
        rows, lanes = staged[i].shape
        both = dot_nt(eye(lanes), staged[i][...]).astype(made[i].dtype)
        if made[i].shape != (lanes, rows):
            pieces = []
            for low in range(0, rows, 16):
                pieces += [both[:lanes // 2, low:low + 16], both[lanes // 2:, low:low + 16]]
            both = jnp.concatenate(pieces, axis=1)
        made[i][...] = both
        copies.append(pltpu.make_async_copy(made[i], results[i], leaving.at[i]))
        copies[-1].start()
    for copy in copies:
        copy.wait()


def fused_device(*blocks):
    plan = Plan(
        lax.axis_size("row"), lax.axis_size("col"),
        [block.shape for block in blocks[:4]], blocks[7].shape,
        [block.shape for block in blocks[11:14]],
    )
    if not plan.fits():
        return per_device(*blocks)
    kernel, scratch = build_kernel(plan)
    blocks = list(blocks)
    for at in (0, 1, 2, 3, 7, 8, 9, 10):
        if narrow(blocks[at].shape[1]):
            blocks[at] = blocks[at].T
    blocks = [pltpu.with_memory_space_constraint(block, pltpu.HBM) for block in blocks]
    anywhere = pl.BlockSpec(memory_space=pltpu.HBM)
    solved = pl.pallas_call(
        kernel,
        out_shape=tuple(
            jax.ShapeDtypeStruct(shape, blocks[0].dtype) for shape in plan.result_shapes()
        ),
        in_specs=[anywhere] * 14,
        out_specs=(pl.BlockSpec(memory_space=pl.ANY),) * 4,
        scratch_shapes=scratch,
        compiler_params=pltpu.CompilerParams(
            collective_id=0, has_side_effects=True, vmem_limit_bytes=VMEM_LIMIT
        ),
    )(*blocks)
    turned = [not narrow(width) for width in plan.width]
    final = [
        (strip, width) if turn else (width, strip)
        for width, strip, turn in zip(plan.width, plan.strip, turned)
    ]
    solved = pl.pallas_call(
        functools.partial(hand_on, turned),
        out_shape=tuple(jax.ShapeDtypeStruct(shape, blocks[0].dtype) for shape in final),
        in_specs=[pl.BlockSpec(memory_space=pl.ANY)] * 4,
        out_specs=(pl.BlockSpec(memory_space=pltpu.HBM),) * 4,
        scratch_shapes=[pltpu.VMEM(block.shape, block.dtype) for block in solved]
        + [pltpu.VMEM(shape, blocks[0].dtype) for shape in final]
        + [pltpu.SemaphoreType.DMA((4,))] * 2,
        compiler_params=pltpu.CompilerParams(vmem_limit_bytes=2**20),
    )(*solved)
    return tuple(block if turn else block.T for block, turn in zip(solved, turned))


def solution(mesh):
    in_specs = (
        P("col", "row"),
        P("col", "row"),
        P("col", "row"),
        P("col", "row"),
        P("row", "col"),
        P("row", "col"),
        P("row", "col"),
        P("row", "col"),
        P("row", "col"),
        P("row", "col"),
        P("row", "col"),
        P(),
        P(),
        P(),
    )
    out_specs = (P("row", "col"), P("row", "col"), P("row", "col"), P("row", "col"))
    return jax.shard_map(
        fused_device, mesh=mesh, in_specs=in_specs, out_specs=out_specs, check_vma=False
    )
```
